32 devices in a mesh: groups: 2 (over y), ctx: 4 (over z), fsdp: 4 (over x, core).
Axes of the slice: x: 2, y: 2, z: 4, core: 2. Of those that a mesh axis runs over, the one named last changes fastest.
Arguments:
- patches: bfloat16 [8192, 1024], P(('groups', 'ctx', 'fsdp')), parts along dimension 0, may hold values from -6 to 6
- labels: int32 [8192], P(('groups', 'ctx', 'fsdp')), parts along dimension 0, may hold values from 0 to 127
- op_ids: int32 [4, 3], P('groups'), parts along dimension 0, may hold values from 0 to 8
- mix_codes: int32 [4, 4], P('groups'), parts along dimension 0, may hold values from 1 to 8
- aug_gains: float32 [9, 1024], replicated, may hold values from 0.1 to 1.9
- in_weight: bfloat16 [1024, 1536], P('fsdp'), may hold values from -0.1875 to 0.1875
- dt_weight: bfloat16 [1024, 32], P('fsdp'), may hold values from -0.09375 to 0.09375
- dt_bias: float32 [2, 16], replicated, may hold values from -3.9 to -2.2
- decay_log: float32 [2, 16], replicated, may hold values from -12 to 0
- skip_gain: float32 [16], replicated, may hold values from 0.1 to 1.9
- norm_gain: float32 [1024], replicated, may hold values from 0.5 to 1.5
- out_weight: bfloat16 [1024, 1024], P('fsdp'), may hold values from -0.1875 to 0.1875
- head_weight: bfloat16 [1024, 128], replicated, may hold values from -8 to 8
Outputs:
- grad_out: float32 [2048, 1024], P(('groups', 'ctx', 'fsdp')), parts along dimension 0
- grad_head: float32 [2048, 128], P(('groups', 'ctx', 'fsdp')), parts along dimension 0
- patch_loss: float32 [8192], P(('groups', 'ctx', 'fsdp')), parts along dimension 0
The draws below stay inside these ranges and needn't reach their ends.
There are 2 independent parts, one for each index of `groups`. The reference program is written for one: setup_inputs(seed, part) draws one part's arguments, and reference() takes and returns one part's arrays. A program takes and returns all parts, laid end to end along the dimension named above; an argument that names none is the same for every part. Nothing has to cross between parts.
All inputs are finite; a program needn't handle non-finite values.
Results may differ from the reference program's by a relative error of at most 0.01505.
The reference program's roundings to bfloat16 on the way (of `views`, `projected`, `normed`, `hidden`, `grad_logits` and `grad_hidden`) count: a program that leaves them out, or rounds other values in their place, can miss the bound.
Values may be sent and summed in bfloat16 or wider, within the bound.
A program may use at most 128 MiB of HBM per device.

```python
import math
import jax
import jax.numpy as jnp
from jax import lax

D = 1024
HEADS = 16
HEAD_DIM = 64
STATE = 128
CLASSES = 128
VIEWS = 3
NOPS = 9
WIDTH_AUG = 3
BLOCK = 128
DIN = 1024
PROJ = 1536
PATCHES = 4096


def draw_decay_log(key, part):
    pick_key = jax.random.fold_in(key, 11)
    slow_key = jax.random.fold_in(key, 12)
    fast_key = jax.random.fold_in(key, 13)
    slow_share = 0.5
    slow_pick = jax.random.uniform(pick_key, (2, HEADS), jnp.float32) < slow_share
    slow_rate = jax.random.uniform(slow_key, (2, HEADS), jnp.float32, minval=math.log(4.0 / PATCHES), maxval=math.log(40.0 / PATCHES))
    fast_rate = jax.random.uniform(fast_key, (2, HEADS), jnp.float32, minval=math.log(0.4), maxval=0.0)
    return jnp.where(slow_pick, slow_rate, fast_rate).astype(jnp.float32)


def draw_head_weight(key, part):
    spread_factor = 3.0
    drawn = jax.random.normal(jax.random.fold_in(key, 21), (D, CLASSES), jnp.float32) * (spread_factor / math.sqrt(D))
    return jnp.clip(drawn, -8.0, 8.0).astype(jnp.bfloat16)


def plant(values, key, low, top_value):
    place = [jax.random.randint(jax.random.fold_in(key, axis), (), 0, length) for axis, length in enumerate(values.shape)]
    longest = values.shape.index(max(values.shape))
    beside = place[:longest] + [(place[longest] + 1) % values.shape[longest]] + place[longest + 1:]
    return values.at[tuple(place)].set(low).at[tuple(beside)].set(top_value)


def steps_of(stream_key, extent, cuts, low, top_value):
    loudness = 1.0
    for axis_at, shards_of in cuts:
        steps = jax.random.uniform(jax.random.fold_in(jax.random.fold_in(stream_key, 6), axis_at), (shards_of,), jnp.float32, low / len(cuts), top_value / len(cuts))
        loudness = loudness * jnp.repeat(jnp.exp(steps), extent[axis_at] // shards_of).reshape((-1,) + (1,) * (len(extent) - 1 - axis_at))
    return loudness


def normal_values(own_key, dims, width, bound, split=(), kind=jnp.bfloat16):
    level = steps_of(own_key, dims, split, -0.22, 0.18) if split else 1.0
    values = jax.random.normal(own_key, dims, jnp.float32) * width * level
    return jnp.minimum(jnp.maximum(values, -bound), bound).astype(kind)


def setup_inputs(seed: int = 0, part: int = 0) -> dict:
    seeds = jax.random.split(jax.random.key(seed), 14)
    part_keys = jax.random.split(jax.random.fold_in(seeds[13], part), 14)
    patches = normal_values(part_keys[0], (PATCHES, D), 1.0, 6.0, ((0, 16),))
    labels = plant(jax.random.randint(part_keys[1], (PATCHES,), 0, CLASSES), jax.random.fold_in(part_keys[1], 1), 0, CLASSES - 1).astype(jnp.int32)
    op_ids = plant(jax.random.randint(part_keys[2], (2, WIDTH_AUG), 0, NOPS), jax.random.fold_in(part_keys[2], 1), 0, NOPS - 1).astype(jnp.int32)
    mix_codes = plant(jax.random.randint(part_keys[3], (2, WIDTH_AUG + 1), 1, 9), jax.random.fold_in(part_keys[3], 1), 1, 8).astype(jnp.int32)
    aug_gains = jnp.clip(1.0 + 0.18 * jax.random.normal(seeds[4], (NOPS, D), jnp.float32), 0.1, 1.9)
    in_weight = normal_values(seeds[5], (D, PROJ), D ** -0.5, 0.1875, ((0, 4),))
    dt_weight = normal_values(seeds[6], (D, 2 * HEADS), (4 * D) ** -0.5, 0.09375, ((0, 4),))
    dt_bias = jnp.clip(jax.random.uniform(seeds[7], (2, HEADS), jnp.float32, -3.9, -2.2), -3.9, -2.2)
    decay_log = draw_decay_log(jax.random.fold_in(seeds[13], 71), part)
    skip_gain = jnp.clip(1.0 + 0.18 * jax.random.normal(seeds[9], (HEADS,), jnp.float32), 0.1, 1.9)
    norm_gain = jnp.clip(1.0 + 0.1 * jax.random.normal(seeds[10], (DIN,), jnp.float32), 0.5, 1.5)
    out_weight = normal_values(seeds[11], (DIN, D), DIN ** -0.5, 0.1875, ((0, 4),))
    head_weight = draw_head_weight(jax.random.fold_in(seeds[13], 71), part)
    return {"patches": patches, "labels": labels, "op_ids": op_ids, "mix_codes": mix_codes, "aug_gains": aug_gains, "in_weight": in_weight, "dt_weight": dt_weight, "dt_bias": dt_bias, "decay_log": decay_log, "skip_gain": skip_gain, "norm_gain": norm_gain, "out_weight": out_weight, "head_weight": head_weight}


loss_scale = 256.0
mix_lambda = 12.0
highest = lax.Precision.HIGHEST

def view_scales(op_ids, mix_codes, aug_gains):
    code_values = mix_codes.astype(jnp.float32)
    weights = code_values[:, :WIDTH_AUG] / lax.optimization_barrier(jnp.sum(code_values[:, :WIDTH_AUG], axis=1, keepdims=True))
    keep_share = code_values[:, WIDTH_AUG] / 9.0
    onehot = (op_ids[:, :, None] == jnp.arange(NOPS, dtype=jnp.int32)[None, None, :]).astype(jnp.float32)
    op_weights = lax.optimization_barrier(jnp.sum(onehot * weights[:, :, None], axis=1))
    mixed_gain = jnp.dot(op_weights, aug_gains, precision=highest)
    scaled = keep_share[:, None] + (1.0 - keep_share[:, None]) * mixed_gain
    return jnp.concatenate([jnp.ones((1, D), jnp.float32), scaled], axis=0)

def block_pass(values, write_vectors, read_vectors, step_sizes, decay_rates):
    length = values.shape[0]
    pieces = length // BLOCK
    shaped = (values.reshape(pieces, BLOCK, HEADS, HEAD_DIM), write_vectors.reshape(pieces, BLOCK, STATE), read_vectors.reshape(pieces, BLOCK, STATE), step_sizes.reshape(pieces, BLOCK, HEADS))
    lower_mask = jnp.arange(BLOCK)[:, None] >= jnp.arange(BLOCK)[None, :]

    def advance(carried_in, inputs):
        state_now, offset = carried_in
        piece_values, piece_write, piece_read, piece_steps = inputs
        value_float = piece_values.astype(jnp.float32)
        write_float = piece_write.astype(jnp.float32)
        read_float = piece_read.astype(jnp.float32)
        step_logs = piece_steps * decay_rates[None, :]
        running = jnp.cumsum(step_logs, axis=0)
        log_gaps = running[:, None, :] - running[None, :, :]
        mask_decay = jnp.exp(jnp.where(lower_mask[:, :, None], log_gaps, -1e+30))
        scores = jnp.dot(read_float, write_float.T, precision=highest)
        mixing = scores[:, :, None] * mask_decay * piece_steps[None, :, :]
        inside = jnp.einsum('tsh,shp->thp', mixing, value_float, precision=highest)
        carried = jnp.exp(running)[:, :, None] * jnp.einsum('tn,hpn->thp', read_float, state_now, precision=highest)
        last_log = running[-1]
        weighted = (jnp.exp(last_log[None, :] - running) * piece_steps)[:, :, None] * value_float
        new_state = jnp.exp(last_log)[:, None, None] * state_now + jnp.einsum('shp,sn->hpn', weighted, write_float, precision=highest)
        return ((new_state, offset + last_log), (inside + carried, offset[None, :] + running))
    initial = (jnp.zeros((HEADS, HEAD_DIM, STATE), jnp.float32), jnp.zeros((HEADS,), jnp.float32))
    (final_state, total_log), (outputs, positions_log) = lax.scan(advance, initial, shaped)
    return (outputs.reshape(length, HEADS, HEAD_DIM), positions_log.reshape(length, HEADS), final_state, total_log)

def loss_terms(logits, labels):
    log_probs = jax.nn.log_softmax(logits, axis=-1)
    probabilities = jnp.exp(log_probs)
    log_mean = jax.scipy.special.logsumexp(log_probs, axis=0) - jnp.log(jnp.float32(VIEWS))
    spread = lax.optimization_barrier(jnp.sum(probabilities * (log_probs - log_mean[None]), axis=(0, 2))) / VIEWS
    onehot = (labels[:, None] == jnp.arange(CLASSES, dtype=jnp.int32)[None, :]).astype(jnp.float32)
    cross_entropy = -lax.optimization_barrier(jnp.sum(onehot * log_probs[0], axis=-1))
    return cross_entropy + mix_lambda * spread

def reference(patches, labels, op_ids, mix_codes, aug_gains, in_weight, dt_weight, dt_bias, decay_log, skip_gain, norm_gain, out_weight, head_weight):
    scales = view_scales(op_ids, mix_codes, aug_gains)
    views = (scales[:, None, :] * patches.astype(jnp.float32)[None]).astype(jnp.bfloat16)
    flat_rows = views.reshape(VIEWS * PATCHES, D)
    projected = jnp.dot(flat_rows, in_weight, preferred_element_type=jnp.float32).astype(jnp.bfloat16)
    projected = projected.reshape(VIEWS, PATCHES, PROJ)
    raw_steps = jnp.dot(flat_rows, dt_weight, preferred_element_type=jnp.float32).reshape(VIEWS, PATCHES, 2, HEADS)
    step_sizes = jax.nn.softplus(raw_steps + dt_bias[None, None])
    decay_rates = -jnp.exp(decay_log)
    values = projected[:, :, :DIN].reshape(VIEWS, PATCHES, HEADS, HEAD_DIM)
    coefficients = projected[:, :, DIN:].reshape(VIEWS, PATCHES, 4, STATE)
    mapped = jax.vmap(block_pass, in_axes=(0, 0, 0, 0, None))
    forward_out = mapped(values, coefficients[:, :, 0], coefficients[:, :, 1], step_sizes[:, :, 0], decay_rates[0])[0]
    reverse_out = mapped(jnp.flip(values, 1), jnp.flip(coefficients[:, :, 2], 1), jnp.flip(coefficients[:, :, 3], 1), jnp.flip(step_sizes[:, :, 1], 1), decay_rates[1])[0]
    mixed = forward_out + jnp.flip(reverse_out, 1) + skip_gain[None, None, :, None] * values.astype(jnp.float32)
    mixed = mixed.reshape(VIEWS * PATCHES, DIN)
    normed = (mixed * lax.rsqrt(lax.optimization_barrier(jnp.mean(mixed * mixed, axis=-1, keepdims=True)) + 1e-05) * norm_gain[None, :]).astype(jnp.bfloat16)
    hidden = (flat_rows.astype(jnp.float32) + jnp.dot(normed, out_weight, preferred_element_type=jnp.float32)).astype(jnp.bfloat16)
    logits = jnp.dot(hidden, head_weight, preferred_element_type=jnp.float32).reshape(VIEWS, PATCHES, CLASSES)

    def per_patch(logit_values):
        return loss_terms(logit_values, labels)
    patch_loss, pullback = jax.vjp(per_patch, logits)
    grad_logits, = pullback(jnp.full((PATCHES,), loss_scale / PATCHES, jnp.float32))
    grad_logits_bf = grad_logits.reshape(VIEWS * PATCHES, CLASSES).astype(jnp.bfloat16)
    grad_hidden = lax.dot_general(grad_logits_bf, head_weight, (((1,), (1,)), ((), ())), preferred_element_type=jnp.float32).astype(jnp.bfloat16)
    grad_out = lax.dot_general(normed, grad_hidden, (((0,), (0,)), ((), ())), preferred_element_type=jnp.float32)
    grad_head = lax.dot_general(hidden, grad_logits_bf, (((0,), (0,)), ((), ())), preferred_element_type=jnp.float32)
    return (grad_out, grad_head, patch_loss)
```

```python
import functools
import jax
import jax.numpy as jnp
from jax import lax
from jax.experimental import pallas as pl
from jax.experimental.pallas import tpu as pltpu
from jax.sharding import PartitionSpec as P

D = 1024
HEADS = 16
HEAD_DIM = 64
STATE = 128
CLASSES = 128
VIEWS = 3
NOPS = 9
WIDTH_AUG = 3
BLOCK = 128
LANES = 128
LOG_ROWS = 8


loss_scale = 256.0
mix_lambda = 12.0
highest = lax.Precision.HIGHEST
f32 = jnp.float32
bf16 = jnp.bfloat16


def view_scales(op_ids, mix_codes, aug_gains):
    code_values = mix_codes.astype(jnp.float32)
    weights = code_values[:, :WIDTH_AUG] / jnp.sum(
        code_values[:, :WIDTH_AUG], axis=1, keepdims=True
    )
    keep_share = code_values[:, WIDTH_AUG] / 9.0
    onehot = (op_ids[:, :, None] == jnp.arange(NOPS, dtype=jnp.int32)[None, None, :]).astype(
        jnp.float32
    )
    op_weights = jnp.sum(onehot * weights[:, :, None], axis=1)
    mixed_gain = jnp.dot(op_weights, aug_gains, precision=highest)
    scaled = keep_share[:, None] + (1.0 - keep_share[:, None]) * mixed_gain
    return jnp.concatenate([jnp.ones((1, D), jnp.float32), scaled], axis=0)


def halves(value):
    high = value.astype(bf16)
    return high, (value - high.astype(f32)).astype(bf16)


def thirds(value):
    high = value.astype(bf16)
    rest = value - high.astype(f32)
    mid = rest.astype(bf16)
    return high, mid, (rest - mid.astype(f32)).astype(bf16)


def dot(a, b, dims=((1,), (0,))):
    return lax.dot_general(a, b, (dims, ((), ())), preferred_element_type=f32)


def spread(columns, first, heads):
    rows = columns.shape[0]
    lane = lax.broadcasted_iota(jnp.int32, (rows, LANES), 1)
    pieces = []
    for h in range(first, first + heads, 2):
        left = jnp.broadcast_to(columns[:, h : h + 1], (rows, LANES))
        right = jnp.broadcast_to(columns[:, h + 1 : h + 2], (rows, LANES))
        pieces.append(jnp.where(lane < HEAD_DIM, left, right))
    return jnp.concatenate(pieces, axis=1) if len(pieces) > 1 else pieces[0]


def project_kernel(place_ref, patches_ref, scale_ref, weight_ref, x_ref, coef_ref, raw_ref):
    width = x_ref.shape[2]
    patches = patches_ref[...].astype(f32)
    for v in range(VIEWS):
        view = (scale_ref[v : v + 1, :] * patches).astype(bf16)
        out = dot(view, weight_ref[...])
        x_ref[v] = out[:, :width].astype(bf16)
        coef_ref[v] = out[:, width : width + 4 * STATE].astype(bf16)
        raw_ref[v] = out[:, width + 4 * STATE :]


def states_kernel(heads, raw_ref, x_ref, coef_ref, bias_ref, rate_ref,
                  final_ref, prefix_ref, steps_ref, run_ref, pos_ref):
    rows, width = x_ref.shape[1:]
    pieces = rows // BLOCK
    row = lax.broadcasted_iota(jnp.int32, (BLOCK, BLOCK), 0)
    col = lax.broadcasted_iota(jnp.int32, (BLOCK, BLOCK), 1)
    lower = (row >= col).astype(f32).astype(bf16)
    upper = (row <= col).astype(f32).astype(bf16)
    is_forward = col < heads

    def first_pass(i, carried):
        state, total = carried
        at = pl.ds(pl.multiple_of(i * BLOCK, BLOCK), BLOCK)
        raw = raw_ref[0, at, :] + bias_ref[...]
        steps = jnp.maximum(raw, 0.0) + jnp.log1p(jnp.exp(-jnp.abs(raw)))
        parts = thirds(steps * rate_ref[...])
        down = sum(dot(lower, part) for part in parts)
        up = sum(dot(upper, part) for part in parts)
        run = jnp.where(is_forward, down, up)
        steps_ref[0, at, :] = steps
        run_ref[0, at, :] = run
        pos_ref[0, at, :] = run + total
        last = jnp.where(is_forward[:1], run[BLOCK - 1 :], run[:1])
        x = x_ref[0, at, :].astype(f32)
        weight = spread(jnp.exp(last - run) * steps, 0, heads)
        high, low = halves(weight * x)
        write = coef_ref[0, at, :STATE]
        fresh = dot(write, high, ((0,), (0,))) + dot(write, low, ((0,), (0,)))
        s_high, s_low = halves(state)
        prefix_ref[0, 0, i, :STATE, :] = s_high
        prefix_ref[0, 0, i, STATE:, :] = s_low
        return spread(jnp.exp(last), 0, heads) * state + fresh, total + last

    zero = jnp.zeros((STATE, width), f32)
    no_log = jnp.zeros((1, LANES), f32)
    state, total = lax.fori_loop(0, pieces, first_pass, (zero, no_log), unroll=4)
    final_ref[0, 0, :STATE, :] = state
    final_ref[0, 0, STATE:, :] = jnp.broadcast_to(spread(total, 0, heads), (LOG_ROWS, width))

    def second_pass(k, carried):
        state, total = carried
        i = pieces - 1 - k
        at = pl.ds(pl.multiple_of(i * BLOCK, BLOCK), BLOCK)
        run = run_ref[0, at, :]
        last = run[:1]
        pos_ref[0, at, :] = jnp.where(is_forward, pos_ref[0, at, :], run + total)
        x = x_ref[0, at, :].astype(f32)
        weight = spread(jnp.exp(last - run) * steps_ref[0, at, :], heads, heads)
        high, low = halves(weight * x)
        write = coef_ref[0, at, 2 * STATE : 3 * STATE]
        fresh = dot(write, high, ((0,), (0,))) + dot(write, low, ((0,), (0,)))
        s_high, s_low = halves(state)
        prefix_ref[0, 1, i, :STATE, :] = s_high
        prefix_ref[0, 1, i, STATE:, :] = s_low
        return spread(jnp.exp(last), heads, heads) * state + fresh, total + last

    state, total = lax.fori_loop(0, pieces, second_pass, (zero, no_log), unroll=4)
    final_ref[0, 1, :STATE, :] = state
    final_ref[0, 1, STATE:, :] = jnp.broadcast_to(spread(total, heads, heads), (LOG_ROWS, width))


def inside_kernel(heads, x_ref, coef_ref, prefix_ref, steps_ref, run_ref, skip_ref, *rest):
    out_ref = rest[-1]
    row = lax.broadcasted_iota(jnp.int32, (BLOCK, BLOCK), 0)
    col = lax.broadcasted_iota(jnp.int32, (BLOCK, BLOCK), 1)
    below, above = row > col, row < col
    x = x_ref[0]
    steps_t = steps_ref[0].T
    run = run_ref[0]
    run_t = run.T
    coef = coef_ref[0]
    write_f, read_f = coef[:, :STATE], coef[:, STATE : 2 * STATE]
    write_r, read_r = coef[:, 2 * STATE : 3 * STATE], coef[:, 3 * STATE :]
    score_f = dot(read_f, write_f, ((1,), (1,)))
    score_r = dot(read_r, write_r, ((1,), (1,)))
    lane = lax.broadcasted_iota(jnp.int32, (BLOCK, LANES), 1)
    zero = jnp.zeros((BLOCK, LANES), bf16)
    pieces = []
    for pair in range(heads // 2):
        highs, lows = [], []
        for h in (2 * pair, 2 * pair + 1):
            r = heads + h
            gap = jnp.where(
                below, run[:, h : h + 1] - run_t[h : h + 1], run[:, r : r + 1] - run_t[r : r + 1]
            )
            gap = jnp.where(row == col, 0.0, gap)
            from_f = score_f * steps_t[h : h + 1]
            from_r = score_r * steps_t[r : r + 1]
            weight = jnp.where(below, from_f, jnp.where(above, from_r, from_f + from_r))
            high, low = halves(weight * jnp.exp(gap))
            highs.append(high)
            lows.append(low)
        values = x[:, pair * LANES : (pair + 1) * LANES]
        stacked = jnp.concatenate(
            [jnp.where(lane < HEAD_DIM, values, zero), jnp.where(lane < HEAD_DIM, zero, values)],
            axis=0,
        )
        pieces.append(
            dot(jnp.concatenate(highs, axis=1), stacked)
            + dot(jnp.concatenate(lows, axis=1), stacked)
        )
    inside = jnp.concatenate(pieces, axis=1) if len(pieces) > 1 else pieces[0]
    grown = jnp.exp(run)
    carried_f = dot(jnp.concatenate([read_f, read_f], axis=1), prefix_ref[0, 0, 0])
    carried_r = dot(jnp.concatenate([read_r, read_r], axis=1), prefix_ref[0, 1, 0])
    out_ref[0] = (
        inside
        + spread(grown, 0, heads) * carried_f
        + spread(grown, heads, heads) * carried_r
        + skip_ref[...] * x.astype(f32)
    )


def incoming_kernel(heads, forward_ref, reverse_ref, coef_ref, pos_ref, local_ref,
                    mixed_ref, square_ref, held):
    width = local_ref.shape[2]

    @pl.when(pl.program_id(1) == 0)
    def _():
        for way, before in enumerate((forward_ref, reverse_ref)):
            high, low = halves(before[0])
            held[way, :STATE, :] = high
            held[way, STATE:, :] = low

    grown = jnp.exp(pos_ref[0])
    coef = coef_ref[0]
    read_f = coef[:, STATE : 2 * STATE]
    read_r = coef[:, 3 * STATE :]
    mixed = (
        local_ref[0]
        + spread(grown, 0, heads) * dot(jnp.concatenate([read_f, read_f], axis=1), held[0])
        + spread(grown, heads, heads) * dot(jnp.concatenate([read_r, read_r], axis=1), held[1])
    )
    mixed_ref[0] = mixed
    ones = jnp.ones((8, width), bf16)
    square_ref[0] = sum(dot(ones, part, ((1,), (1,))) for part in thirds(mixed * mixed))


def tail_kernel(shards, factor, normed_ref, out_w_ref, head_ref, patches_ref, scale_ref,
                label_ref, logit_ref, loss_ref, head_grad_ref, hidden_ref=None):
    rows = patches_ref.shape[0]
    head = head_ref[...]
    patches = patches_ref[...].astype(f32)
    hiddens, logs = [], []
    for v in range(VIEWS):
        total = dot(normed_ref[0, v], out_w_ref[0])
        for s in range(1, shards):
            total += dot(normed_ref[s, v], out_w_ref[s])
        view = (scale_ref[v : v + 1, :] * patches).astype(bf16)
        hidden = (view.astype(f32) + total).astype(bf16)
        hiddens.append(hidden)
        logits = dot(hidden, head)
        shifted = logits - jnp.max(logits, axis=1, keepdims=True)
        logs.append(shifted - jnp.log(jnp.sum(jnp.exp(shifted), axis=1, keepdims=True)))
    top = jnp.maximum(jnp.maximum(logs[0], logs[1]), logs[2])
    mean = top + jnp.log(sum(jnp.exp(log - top) for log in logs)) - jnp.log(f32(VIEWS))
    lane = lax.broadcasted_iota(jnp.int32, (rows, CLASSES), 1)
    onehot = (lane == label_ref[...]).astype(f32)
    spread_sum = jnp.zeros((rows, 1), f32)
    grads = []
    for v in range(VIEWS):
        prob = jnp.exp(logs[v])
        gap = logs[v] - mean
        inner = jnp.sum(prob * gap, axis=1, keepdims=True)
        spread_sum += inner
        grad = (mix_lambda / VIEWS) * prob * (gap - inner)
        if v == 0:
            grad += prob - onehot
        grads.append((factor * grad).astype(bf16))
        logit_ref[v] = grads[v]
    cross = -jnp.sum(onehot * logs[0], axis=1, keepdims=True)
    loss_ref[...] = cross + mix_lambda * (spread_sum / VIEWS)
    update = sum(dot(hiddens[v], grads[v], ((0,), (0,))) for v in range(VIEWS))

    @pl.when(pl.program_id(0) == 0)
    def _():
        head_grad_ref[...] = update

    @pl.when(pl.program_id(0) > 0)
    def _():
        head_grad_ref[...] += update


def grad_kernel(shards, normed_ref, logit_ref, head_ref, out_ref):
    grads = logit_ref[0, 0]
    hidden = dot(grads, head_ref[...], ((1,), (1,))).astype(bf16)
    update = dot(normed_ref[0], hidden, ((0,), (0,)))
    first = (pl.program_id(0) == 0) & (pl.program_id(1) == 0)

    @pl.when(first)
    def _():
        out_ref[...] = update

    @pl.when(jnp.logical_not(first))
    def _():
        out_ref[...] += update


def call(kernel, name, flops, moved, limit=48 << 20, **options):
    return pl.pallas_call(
        kernel,
        name=name,
        compiler_params=pltpu.CompilerParams(vmem_limit_bytes=limit),
        cost_estimate=pl.CostEstimate(flops=flops, bytes_accessed=moved, transcendentals=0),
        **options,
    )


def carried_in(state, decay, axis, reverse):
    count = lax.axis_size(axis)
    if reverse:
        hops = [(j, j - 1) for j in range(1, count)]
    else:
        hops = [(j, j + 1) for j in range(count - 1)]
    sent, got = state, jnp.zeros_like(state)
    for hop in range(count - 1):
        got = lax.ppermute(sent, axis, hops)
        sent = decay * got + state
    return got


def scatter_sum(terms, axes, count):
    blocks = terms.reshape(count, -1, terms.shape[1])
    return jnp.sum(lax.all_to_all(blocks, axes, split_axis=0, concat_axis=0), axis=0)


def on_device(
    patches,
    labels,
    op_ids,
    mix_codes,
    aug_gains,
    in_weight,
    dt_weight,
    dt_bias,
    decay_log,
    skip_gain,
    norm_gain,
    out_weight,
    head_weight,
):
    row_count = patches.shape[0]
    ctx_count = lax.axis_size("ctx")
    shards = lax.axis_size("fsdp")
    place = lax.axis_index("fsdp")
    total_patches = row_count * ctx_count * shards
    inner = out_weight.shape[0] * shards
    heads = HEADS // shards
    width = heads * HEAD_DIM
    rows = row_count * shards
    pieces = rows // BLOCK

    if shards == 4:
        across = lax.ppermute(patches, "fsdp", [(f, f ^ 2) for f in range(shards)])
        beside = lax.ppermute(patches, "fsdp", [(f, f ^ 1) for f in range(shards)])
        corner = lax.ppermute(across, "fsdp", [(f, f ^ 1) for f in range(shards)])
        patches_all = jnp.concatenate([patches, beside, across, corner], axis=0)
        flip = place
    else:
        patches_all = lax.all_gather(patches, "fsdp", axis=0, tiled=True)
        flip = jnp.zeros_like(place)
    columns_in = inner + 4 * STATE
    depth = in_weight.shape[0]
    sent_weight = jnp.concatenate(
        [
            in_weight[:, :inner]
            .reshape(depth, heads, shards, HEAD_DIM)
            .transpose(2, 0, 1, 3)
            .reshape(shards, depth, width),
            jnp.broadcast_to(in_weight[None, :, inner:], (shards, depth, 4 * STATE)),
            dt_weight.reshape(depth, 2 * heads, shards).transpose(2, 0, 1),
            jnp.zeros((shards, depth, LANES - 2 * heads), bf16),
        ],
        axis=2,
    )
    mine_weight = lax.all_to_all(sent_weight, "fsdp", split_axis=0, concat_axis=0)
    mine_weight = mine_weight.reshape(D, width + 5 * STATE)
    scales = view_scales(op_ids, mix_codes, aug_gains)
    tile = min(row_count, 128)
    per = row_count // tile
    placed = lambda s, i, flip_ref: ((s ^ flip_ref[0]) * per + i, 0)
    piece = lambda lanes: pl.BlockSpec((VIEWS, tile, lanes), lambda s, i, _: (0, s * per + i, 0))
    constant = lambda *dims: pl.BlockSpec(dims, lambda *_: (0,) * len(dims))
    x, coef, raw = call(
        project_kernel, "project",
        VIEWS * rows * D * (width + 5 * STATE) * 2, rows * D * 8,
        grid_spec=pltpu.PrefetchScalarGridSpec(
            num_scalar_prefetch=1,
            grid=(shards, per),
            in_specs=[pl.BlockSpec((tile, D), placed), constant(VIEWS, D),
                      constant(D, width + 5 * STATE)],
            out_specs=[piece(width), piece(4 * STATE), piece(LANES)],
        ),
        out_shape=[
            jax.ShapeDtypeStruct((VIEWS, rows, width), bf16),
            jax.ShapeDtypeStruct((VIEWS, rows, 4 * STATE), bf16),
            jax.ShapeDtypeStruct((VIEWS, rows, LANES), f32),
        ],
    )(flip.reshape(1).astype(jnp.int32), patches_all, scales, mine_weight)
    raw, out_later = lax.optimization_barrier((raw, out_weight))
    out_all = lax.all_gather(out_later, "fsdp", axis=0, tiled=True)

    def local_lanes(values):
        picked = lax.dynamic_index_in_dim(values.reshape(2 * heads, shards), place, 1, False)
        return jnp.pad(picked, (0, LANES - 2 * heads))[None, :]

    bias = local_lanes(dt_bias)
    rate = local_lanes(-jnp.exp(decay_log))
    skip = lax.dynamic_index_in_dim(skip_gain.reshape(heads, shards), place, 1, False)
    skip = jnp.repeat(skip, HEAD_DIM)[None, :]
    gain = norm_gain.reshape(heads, shards, HEAD_DIM)
    gain = lax.dynamic_index_in_dim(gain, place, 1, False).reshape(1, width)

    whole = lambda *dims: pl.BlockSpec((1, *dims), lambda v: (v,) + (0,) * len(dims))
    fixed = lambda *dims: pl.BlockSpec(dims, lambda *_: (0,) * len(dims))
    final, prefix, steps, run, pos = call(
        functools.partial(states_kernel, heads), "states",
        VIEWS * rows * STATE * width * 8, VIEWS * rows * 8192,
        grid=(VIEWS,),
        in_specs=[whole(rows, LANES), whole(rows, width), whole(rows, 4 * STATE),
                  fixed(1, LANES), fixed(1, LANES)],
        out_specs=[whole(2, STATE + LOG_ROWS, width), whole(2, pieces, 2 * STATE, width),
                   whole(rows, LANES), whole(rows, LANES), whole(rows, LANES)],
        out_shape=[
            jax.ShapeDtypeStruct((VIEWS, 2, STATE + LOG_ROWS, width), f32),
            jax.ShapeDtypeStruct((VIEWS, 2, pieces, 2 * STATE, width), bf16),
            jax.ShapeDtypeStruct((VIEWS, rows, LANES), f32),
            jax.ShapeDtypeStruct((VIEWS, rows, LANES), f32),
            jax.ShapeDtypeStruct((VIEWS, rows, LANES), f32),
        ],
    )(raw, x, coef, bias, rate)
    decay = jnp.exp(final[:, :, STATE : STATE + 1, :])
    forward_in = carried_in(final[:, 0, :STATE], decay[:, 0], "ctx", False)
    reverse_in = carried_in(final[:, 1, :STATE], decay[:, 1], "ctx", True)

    local = ()
    for v in range(VIEWS):
        at = lambda *dims, v=v: pl.BlockSpec(
            (1, *dims), lambda i: (v, i) + (0,) * (len(dims) - 1)
        )
        local = (call(
            functools.partial(inside_kernel, heads), "inside",
            rows * D * 8192, rows * 8192,
            grid=(pieces,),
            in_specs=[at(BLOCK, width), at(BLOCK, 4 * STATE),
                      pl.BlockSpec((1, 2, 1, 2 * STATE, width), lambda i, v=v: (v, 0, i, 0, 0)),
                      at(BLOCK, LANES), at(BLOCK, LANES), fixed(1, width)]
            + [pl.BlockSpec(memory_space=pl.ANY)] * len(local),
            out_specs=at(BLOCK, width),
            out_shape=jax.ShapeDtypeStruct((VIEWS, rows, width), f32),
            input_output_aliases={6: 0} if local else {},
        )(x, coef, prefix, steps, run, skip, *local),)
    (local,) = local
    block = lambda *dims: pl.BlockSpec((1, *dims), lambda v, i: (v, i) + (0,) * (len(dims) - 1))
    entering = pl.BlockSpec((1, STATE, width), lambda v, i: (v, 0, 0))

    span = min(rows, 512)
    mixed, squares = call(
        functools.partial(incoming_kernel, heads), "incoming",
        VIEWS * rows * STATE * width * 8, VIEWS * rows * 8192,
        grid=(VIEWS, rows // span),
        in_specs=[
            entering, entering,
            block(span, 4 * STATE), block(span, LANES), block(span, width)],
        out_specs=[block(span, width), pl.BlockSpec((1, 8, span), lambda v, i: (v, 0, i))],
        out_shape=[
            jax.ShapeDtypeStruct((VIEWS, rows, width), f32),
            jax.ShapeDtypeStruct((VIEWS, 8, rows), f32),
        ],
        scratch_shapes=[pltpu.VMEM((2, 2 * STATE, width), bf16)],
    )(forward_in, reverse_in, coef, pos, local)

    square_total = jnp.sum(lax.all_gather(squares[:, 0, :], "fsdp"), axis=0)
    scaling = lax.rsqrt(square_total / inner + 1e-05)
    normed = (mixed * scaling[:, :, None] * gain[None]).astype(bf16)
    outgoing = normed.reshape(VIEWS, shards, row_count, width).transpose(1, 0, 2, 3)
    arrived = lax.all_to_all(outgoing, "fsdp", split_axis=0, concat_axis=0)

    out_own = out_all.reshape(heads, shards, HEAD_DIM, D).transpose(1, 0, 2, 3)
    out_own = out_own.reshape(shards, width, D)
    tile = min(row_count, 128)
    grads, losses, head_term = call(
        functools.partial(tail_kernel, shards, loss_scale / total_patches), "tail",
        VIEWS * row_count * D * 3000, 6 << 20,
        grid=(row_count // tile,),
        in_specs=[
            pl.BlockSpec((shards, VIEWS, tile, width), lambda i: (0, 0, i, 0)),
            fixed(shards, width, D), fixed(D, CLASSES),
            pl.BlockSpec((tile, D), lambda i: (i, 0)),
            fixed(VIEWS, D),
            pl.BlockSpec((tile, 1), lambda i: (i, 0))],
        out_specs=[
            pl.BlockSpec((VIEWS, tile, CLASSES), lambda i: (0, i, 0)),
            pl.BlockSpec((tile, 1), lambda i: (i, 0)),
            fixed(D, CLASSES)],
        out_shape=[
            jax.ShapeDtypeStruct((VIEWS, row_count, CLASSES), bf16),
            jax.ShapeDtypeStruct((row_count, 1), f32),
            jax.ShapeDtypeStruct((D, CLASSES), f32),
        ],
    )(arrived, out_own, head_weight, patches, scales, labels[:, None])

    if ctx_count * shards == HEADS:
        grads_all = lax.all_gather(grads, "fsdp")
        grad_rows = call(
            functools.partial(grad_kernel, shards), "grads",
            VIEWS * rows * D * (width + CLASSES) * 2, 8 << 20,
            grid=(VIEWS, shards),
            in_specs=[
                pl.BlockSpec((1, row_count, width), lambda v, s: (v, s, 0)),
                pl.BlockSpec((1, 1, row_count, CLASSES), lambda v, s: (s, v, 0, 0)),
                fixed(D, CLASSES)],
            out_specs=fixed(width, D),
            out_shape=jax.ShapeDtypeStruct((width, D), f32),
        )(normed, grads_all, head_weight)
        grad_out = scatter_sum(grad_rows, "ctx", ctx_count)
    else:
        grad_hidden = lax.dot_general(
            grads, head_weight, (((2,), (1,)), ((), ())), preferred_element_type=f32
        ).astype(bf16)
        grad_rows = lax.dot_general(
            arrived, grad_hidden, (((1, 2), (0, 1)), ((), ())), preferred_element_type=f32
        )
        grad_rows = grad_rows.reshape(shards, heads, HEAD_DIM, D).transpose(1, 0, 2, 3)
        grad_out = lax.psum_scatter(
            grad_rows.reshape(inner, D), ("ctx", "fsdp"), scatter_dimension=0, tiled=True
        )
    grad_head = scatter_sum(head_term, ("ctx", "fsdp"), ctx_count * shards)
    return (grad_out, grad_head, losses[:, 0])


LOG2E = 1.4426950408889634
PEERS = 3


def stack3(value):
    high = value.astype(bf16).astype(f32)
    rest = value - high
    mid = rest.astype(bf16).astype(f32)
    low = rest - mid
    return jnp.concatenate([high, mid, low, jnp.zeros_like(value)], axis=0).astype(bf16)


def side3(value):
    return jnp.concatenate(thirds(value), axis=1)


TT = ((0,), (0,))
NT = ((1,), (1,))


def fused_kernel(factor, ops_ref, codes_ref, bias_ref, decay_ref, skip_ref,
                 gains_ref, norm_ref, label_ref, dtw_ref,
                 patches_ref, inw_ref, outw_ref, head_hbm,
                 grad_ref, head_grad_ref, loss_ref,
                 inw, perm, wc, w, z, pall, scales,
                 x_s, coef_s, rawt, steps_s, run_s, pre_s, drow, fresh_s, prefix, fin, dtot, inc,
                 local, sq, sq_in, normed, arrived, ow, head, hid, logit, part, sum_a, got_a, got_b,
                 got_c, spread_s, wide_s, cum_s, gain_s, loc_sem, send_sem, recv_sem):
    MESH = pl.DeviceIdType.MESH
    g, c, f = lax.axis_index("groups"), lax.axis_index("ctx"), lax.axis_index("fsdp")
    count = lax.axis_size("ctx")
    xx, k = f // 2, f % 2
    f1 = f + 1 - 2 * k
    f2 = f + 2 - 4 * xx
    f3 = f2 + 1 - 2 * k
    core, across, corner, other = (g, c, f1), (g, c, f2), (g, c, f3), (1 - g, c, f)
    used = [0]

    def remote(src, dst, to):
        n = used[0]
        used[0] += 1
        return pltpu.make_async_remote_copy(
            src_ref=src, dst_ref=dst, send_sem=send_sem.at[n], recv_sem=recv_sem.at[n],
            device_id=to, device_id_type=MESH)

    load_in = pltpu.make_async_copy(inw_ref, inw, loc_sem.at[0])
    load_own = pltpu.make_async_copy(patches_ref, pall.at[f], loc_sem.at[1])
    load_head = pltpu.make_async_copy(head_hbm, head, loc_sem.at[2])
    load_out = pltpu.make_async_copy(outw_ref, ow.at[:, f], loc_sem.at[3])
    load_in.start()
    load_own.start()
    load_head.start()
    load_out.start()

    barrier = pltpu.get_barrier_semaphore()
    for to in (core, across, corner, other):
        pl.semaphore_signal(barrier, inc=1, device_id=to, device_id_type=MESH)
    for j in range(1, count):
        pl.semaphore_signal(barrier, inc=1, device_id=(g, (c + j) % count, f), device_id_type=MESH)

    load_in.wait()
    lane = lax.broadcasted_iota(jnp.int32, (inw.shape[0], LANES), 1)
    for xr in range(2):
        for half in range(2):
            a = inw[:, (4 * half + xr) * LANES : (4 * half + xr + 1) * LANES].astype(f32)
            b = inw[:, (4 * half + 2 + xr) * LANES : (4 * half + 3 + xr) * LANES].astype(f32)
            at = slice(half * LANES, (half + 1) * LANES)
            perm[2 * xr, :, at] = jnp.where(lane < 64, a, pltpu.roll(b, 64, 1)).astype(bf16)
            perm[2 * xr + 1, :, at] = jnp.where(lane < 64, pltpu.roll(a, 64, 1), b).astype(bf16)
    wc[:, : 4 * STATE] = inw[:, D:]
    wc[:, 4 * STATE :] = jnp.concatenate(
        [dtw_ref[...].astype(f32), jnp.zeros((inw.shape[0], LANES - 2 * HEADS), f32)], axis=1
    ).astype(bf16)
    pl.semaphore_wait(barrier, 3 + count)

    def span(half, q):
        return pl.ds(pl.multiple_of(half * 128 + q * 64, 64), 64)

    first = []
    for q in range(2):
        rows = span(g, q)
        first.append((
            remote(perm.at[f2, rows], w.at[f, rows, pl.ds(0, 256)], across),
            remote(wc.at[rows], w.at[f, rows, pl.ds(256, 640)], across),
            remote(perm.at[f3, rows], z.at[rows], across),
        ))
        for copy in first[q]:
            copy.start()
    beside = (
        remote(perm.at[f1], w.at[f, :, pl.ds(0, 256)], core),
        remote(wc, w.at[f, :, pl.ds(256, 640)], core),
    )
    patch_core = remote(patches_ref, pall.at[f], core)
    for copy in beside:
        copy.start()
    patch_core.start()
    patch_across = []
    for b in range(2):
        rows = pl.ds(b * 128, 128)
        copy = remote(patches_ref.at[rows], pall.at[f, rows], across)
        copy.start()
        patch_across.append(copy)

    w[f, :, :256] = perm[f]
    w[f, :, 256:] = wc[...]
    row32 = lax.broadcasted_iota(jnp.int32, (32, 512), 0)
    col32 = lax.broadcasted_iota(jnp.int32, (32, 512), 1)
    spread_s[...] = ((row32 % 8 == col32 // 64) & (row32 < 24)).astype(f32).astype(bf16)
    row32 = lax.broadcasted_iota(jnp.int32, (32, 1024), 0)
    col32 = lax.broadcasted_iota(jnp.int32, (32, 1024), 1)
    wide_s[...] = ((row32 % 8 == col32 // 128) & (row32 < 24)).astype(f32).astype(bf16)
    row = lax.broadcasted_iota(jnp.int32, (BLOCK, BLOCK), 0)
    col = lax.broadcasted_iota(jnp.int32, (BLOCK, BLOCK), 1)
    cum_s[:, :BLOCK] = (row <= col).astype(f32).astype(bf16)
    cum_s[:, BLOCK:] = (row >= col).astype(f32).astype(bf16)
    scales[0:1, :] = jnp.ones((1, D), f32)
    for j in range(2):
        codes = [jnp.full((1, D), codes_ref[j, i].astype(f32), f32) for i in range(WIDTH_AUG + 1)]
        whole = codes[0] + codes[1] + codes[2]
        shares = [codes[i] / whole for i in range(WIDTH_AUG)]
        keep = codes[WIDTH_AUG] / 9.0
        mixed_gain = jnp.zeros((1, D), f32)
        for n in range(NOPS):
            picked = jnp.zeros((1, D), f32)
            for i in range(WIDTH_AUG):
                picked += shares[i] * jnp.where(ops_ref[j, i] == n, 1.0, 0.0)
            mixed_gain += picked * gains_ref[n : n + 1, :]
        scales[j + 1 : j + 2, :] = keep + (1.0 - keep) * mixed_gain
    line = lax.broadcasted_iota(jnp.int32, (8, LANES), 0)
    bias = jnp.zeros((8, LANES), f32)
    rate = jnp.zeros((8, LANES), f32)
    for d in range(2):
        for j in range(4):
            bias = jnp.where(line == 4 * d + j, bias_ref[d, 4 * j + f], bias)
            rate = jnp.where(line == 4 * d + j, decay_ref[d, 4 * j + f], rate)
    rate = -jnp.exp(rate) * LOG2E
    lane_w = lax.broadcasted_iota(jnp.int32, (8, 256), 1)
    skip = jnp.zeros((8, 256), f32)
    for j in range(4):
        skip = jnp.where(lane_w // HEAD_DIM == j, skip_ref[0, 4 * j + f], skip)
    lane_n = lax.broadcasted_iota(jnp.int32, (8, LANES), 1)
    gain_parts = []
    for half in range(2):
        a = jnp.broadcast_to(norm_ref[pl.ds(4 * half + xx, 1), :], (8, LANES))
        b = jnp.broadcast_to(norm_ref[pl.ds(4 * half + 2 + xx, 1), :], (8, LANES))
        even = jnp.where(lane_n < 64, a, pltpu.roll(b, 64, 1))
        odd = jnp.where(lane_n < 64, pltpu.roll(a, 64, 1), b)
        gain_parts.append(jnp.where(k == 0, even, odd))
    gain_s[...] = jnp.concatenate(gain_parts, axis=1)

    relays, onward = [], []
    for q in range(2):
        for copy in first[q]:
            copy.wait_recv()
        rows = span(g, q)
        pair = (
            remote(w.at[f2, rows], w.at[f2, rows], other),
            remote(z.at[rows], z.at[rows], other),
        )
        for copy in pair:
            copy.start()
        onward.append(pair)
        pair = (
            remote(z.at[rows], w.at[f2, rows, pl.ds(0, 256)], core),
            remote(w.at[f2, rows, pl.ds(256, 640)], w.at[f2, rows, pl.ds(256, 640)], core),
        )
        for copy in pair:
            copy.start()
        relays.append(pair)
    for q in range(2):
        for copy in onward[q]:
            copy.wait_recv()
        rows = span(1 - g, q)
        pair = (
            remote(z.at[rows], w.at[f2, rows, pl.ds(0, 256)], core),
            remote(w.at[f2, rows, pl.ds(256, 640)], w.at[f2, rows, pl.ds(256, 640)], core),
        )
        for copy in pair:
            copy.start()
        relays.append(pair)
    for copy in beside:
        copy.wait_recv()
    for pair in relays:
        for copy in pair:
            copy.wait_recv()
    load_own.wait()

    patch_relay = [
        remote(pall.at[f2, pl.ds(b * 128, 128)], pall.at[f2, pl.ds(b * 128, 128)], core)
        for b in range(2)
    ]
    out_across = remote(outw_ref, ow.at[:, f], across)
    out_core = remote(outw_ref, ow.at[:, f], core)
    out_relay = remote(ow.at[:, f2], ow.at[:, f2], core)

    def project(s, _):
        a = s // 4
        pair = (1 - a) * (s // 2) + a * (2 + s % 2)
        b = (1 - a) * (s % 2) + a * ((s - 4 * a) // 2)
        kb, xb = pair % 2, pair // 2
        src = 2 * (xx + xb - 2 * xx * xb) + (k + kb - 2 * k * kb)

        @pl.when(s == 2)
        def _():
            patch_core.wait_recv()

        for b_static in range(2):
            @pl.when(s == 4 + 2 * b_static)
            def _():
                patch_across[b_static].wait_recv()
                patch_relay[b_static].start()

            @pl.when(s == 5 + 2 * b_static)
            def _():
                patch_relay[b_static].wait_recv()

        rows = pall[src, pl.ds(pl.multiple_of(b * 128, 128), 128), :].astype(f32)
        view = jnp.concatenate(
            [(scales[v : v + 1, :] * rows).astype(bf16) for v in range(VIEWS)], axis=0)
        i = 2 * src + b
        out = dot(view, w[...].reshape(D, 896))
        for v in range(VIEWS):
            at = slice(v * 128, (v + 1) * 128)
            x_s[v, i] = out[at, :256].astype(bf16)
            coef_s[v, i] = out[at, 256:768].astype(bf16)
            rawt[v, i] = out[at, 768:].T[:32]
        return 0

    lax.fori_loop(0, 8, project, 0)
    out_across.start()
    out_core.start()

    def row_of(values):
        return dot(stack3(values)[:, :8], spread_s[...], TT)

    def states(v):
        fin[v, 0] = jnp.zeros((STATE, 256), f32)
        fin[v, 1] = jnp.zeros((STATE, 256), f32)

        def forward(i, total):
            raw = jnp.concatenate(
                [rawt[v, i, pl.ds(f + 16 * d, 4, stride=4), :] for d in range(2)], axis=0) + bias
            steps = jnp.maximum(raw, 0.0) + jnp.log1p(jnp.exp(-jnp.abs(raw)))
            cum = dot(stack3(steps * rate), cum_s[...])
            cum = cum[0:8] + cum[8:16] + cum[16:24]
            run = jnp.where(line < 4, cum[:, :BLOCK], cum[:, BLOCK:])
            last = jnp.where(line[:, :1] < 4, cum[:, BLOCK - 1 : BLOCK], cum[:, BLOCK : BLOCK + 1])
            last = jnp.broadcast_to(last, (8, LANES))
            steps_s[v, i] = steps
            run_s[v, i] = run
            pre_s[v, i] = jnp.where(line < 4, total, last)
            decay = row_of(jnp.exp2(last))
            drow[i] = decay
            xf = x_s[v, i].astype(f32)
            weight = dot(stack3(jnp.exp2(last - run) * steps), spread_s[...], TT)
            for d in range(2):
                high, low = halves(weight[:, 256 * d : 256 * (d + 1)] * xf)
                write = coef_s[v, i, :, 2 * STATE * d : 2 * STATE * d + STATE]
                fresh = dot(jnp.concatenate([write, write], axis=0),
                            jnp.concatenate([high, low], axis=0), TT)
                if d == 0:
                    state = fin[v, 0]
                    prefix[v, 0, i] = state
                    fin[v, 0] = decay[0:1, :256] * state + fresh
                else:
                    fresh_s[i] = fresh
            return total + last

        total = lax.fori_loop(0, 8, forward, jnp.zeros((8, LANES), f32), unroll=2)

        def backward(n, behind):
            i = 7 - n
            last = pre_s[v, i]
            pre_s[v, i] = jnp.where(line < 4, last, behind)
            state = fin[v, 1]
            prefix[v, 1, i] = state
            fin[v, 1] = drow[i, 0:1, 256:] * state + fresh_s[i]
            return behind + last

        lax.fori_loop(0, 8, backward, jnp.zeros((8, LANES), f32), unroll=2)
        dtot[v] = row_of(jnp.exp2(total))

    ahead = (g, (c + 1) % count, f)
    behind = (g, (c + count - 1) % count, f)
    chain = [[remote(fin.at[v, 0], inc.at[v, 0], ahead), remote(fin.at[v, 1], inc.at[v, 1], behind)]
             for v in range(VIEWS)]

    def hop(v, n):
        for d in range(2):
            place = c if d == 0 else count - 1 - c

            @pl.when(place == n)
            def _():
                if n == 0:
                    inc[v, d] = jnp.zeros((STATE, 256), f32)
                else:
                    chain[v][d].wait_recv()
                    fin[v, d] = fin[v, d] + dtot[v, 0:1, 256 * d : 256 * (d + 1)] * inc[v, d]
                if n < count - 1:
                    chain[v][d].start()

    def inside(v):
        def body(i, _):
            x = x_s[v, i]
            run, steps = run_s[v, i], steps_s[v, i]
            coef = coef_s[v, i]
            score_f = dot(coef[:, STATE : 2 * STATE], coef[:, :STATE], NT)
            score_r = dot(coef[:, 3 * STATE :], coef[:, 2 * STATE : 3 * STATE], NT)
            diagonal = jnp.sum(jnp.where(row == col, score_r, 0.0), axis=0, keepdims=True)
            extra = dot(stack3(steps * diagonal), spread_s[:, 256:], TT)
            wide = dot(stack3(run), wide_s[...], TT)
            keep = row >= col
            lane_b = lax.broadcasted_iota(jnp.int32, (BLOCK, LANES), 1)
            none = jnp.zeros((BLOCK, LANES), bf16)
            pieces = []
            for pair in range(2):
                highs, lows = [], []
                for h in (2 * pair, 2 * pair + 1):
                    r = 4 + h
                    gap = jnp.where(keep, wide[:, h * 128 : (h + 1) * 128] - run[h : h + 1],
                                    wide[:, r * 128 : (r + 1) * 128] - run[r : r + 1])
                    weight = jnp.where(keep, score_f * steps[h : h + 1], score_r * steps[r : r + 1])
                    high, low = halves(weight * jnp.exp2(gap))
                    highs.append(high)
                    lows.append(low)
                values = x[:, pair * LANES : (pair + 1) * LANES]
                left, right = jnp.where(lane_b < 64, values, none), jnp.where(lane_b < 64, none, values)
                pieces.append(dot(jnp.concatenate(highs + lows, axis=1),
                                  jnp.concatenate([left, right, left, right], axis=0)))
            local[v, i] = jnp.concatenate(pieces, axis=1) + (skip[0:1] + extra) * x.astype(f32)
            return 0

        lax.fori_loop(0, 8, body, 0)

    def carried(v):
        def body(i, _):
            grown = dot(stack3(jnp.exp2(run_s[v, i])), spread_s[...], TT)
            decay = row_of(jnp.exp2(pre_s[v, i]))
            mixed = local[v, i]
            for d in range(2):
                at = slice(256 * d, 256 * (d + 1))
                high, low = halves(prefix[v, d, i] + decay[0:1, at] * inc[v, d])
                read = coef_s[v, i, :, STATE * (1 + 2 * d) : STATE * (2 + 2 * d)]
                mixed += grown[:, at] * dot(jnp.concatenate([read, read], axis=1),
                                            jnp.concatenate([high, low], axis=0))
            local[v, i] = mixed
            square = mixed * mixed
            square = square[:, :LANES] + square[:, LANES:]
            sums = dot(jnp.ones((8, 3 * LANES), bf16), side3(square), NT)
            sq[v, pl.ds(i, 1), :] = sums[0:1]
            return 0

        lax.fori_loop(0, 8, body, 0, unroll=2)

    square_out = [[remote(sq.at[v], sq_in.at[p, v], to)
                   for p, to in enumerate((core, across, corner))] for v in range(VIEWS)]
    normed_out = [[remote(normed.at[v, fp], arrived.at[f, v], to)
                   for fp, to in ((f3, corner), (f2, across), (f1, core))] for v in range(VIEWS)]
    normed_own = [pltpu.make_async_copy(normed.at[v, f], arrived.at[f, v], loc_sem.at[4 + v])
                  for v in range(VIEWS)]

    def finish(v):
        for copy in square_out[v]:
            copy.wait_recv()
        total = (sq[v] + sq_in[0, v]) + (sq_in[1, v] + sq_in[2, v])
        parts = stack3(lax.rsqrt(total / D + 1e-05))
        row_i = lax.broadcasted_iota(jnp.int32, (32, 256), 0)

        def body(i, _):
            pick = ((row_i % 8 == i) & (row_i < 24)).astype(f32).astype(bf16)
            scaling = dot(parts, pick, TT)
            normed[v, i // 2, i % 2] = (local[v, i] * scaling * gain_s[0:1]).astype(bf16)
            return 0

        lax.fori_loop(0, 8, body, 0, unroll=2)
        for copy in normed_out[v]:
            copy.start()
        normed_own[v].start()

    states(0)
    hop(0, 0)
    states(1)
    hop(0, 1)
    hop(1, 0)
    states(2)
    hop(0, 2)
    hop(1, 1)
    hop(2, 0)
    inside(0)
    hop(1, 2)
    hop(2, 1)
    hop(0, 3)
    inside(1)
    hop(2, 2)
    out_across.wait_recv()
    out_relay.start()
    carried(0)
    for copy in square_out[0]:
        copy.start()
    inside(2)
    finish(0)
    hop(1, 3)
    carried(1)
    for copy in square_out[1]:
        copy.start()
    hop(2, 3)
    carried(2)
    for copy in square_out[2]:
        copy.start()
    finish(1)
    finish(2)

    load_head.wait()
    load_out.wait()
    out_core.wait_recv()
    out_relay.wait_recv()

    def hidden(v):
        for copy in normed_out[v]:
            copy.wait_recv()
        normed_own[v].wait()
        for b in range(2):
            full = jnp.concatenate([arrived[s, v, b] for s in range(4)], axis=1)
            total = dot(full, ow[...].reshape(D, D))
            view = (scales[v : v + 1, :] * pall[f, b * 128 : (b + 1) * 128, :].astype(f32)).astype(bf16)
            hid[v, b] = (view.astype(f32) + total).astype(bf16)

    for v in range(VIEWS):
        hidden(v)

    for b in range(2):
        logs = []
        for v in range(VIEWS):
            logits = dot(hid[v, b], head[...])
            shifted = logits - jnp.max(logits, axis=1, keepdims=True)
            logs.append(shifted - jnp.log(jnp.sum(jnp.exp(shifted), axis=1, keepdims=True)))
        top = jnp.maximum(jnp.maximum(logs[0], logs[1]), logs[2])
        mean = top + jnp.log(sum(jnp.exp(log - top) for log in logs)) - jnp.log(f32(VIEWS))
        onehot = (row == label_ref[b : b + 1, :]).astype(f32).T
        spread_sum = jnp.zeros((BLOCK, 1), f32)
        for v in range(VIEWS):
            prob = jnp.exp(logs[v])
            gap = logs[v] - mean
            inner = jnp.sum(prob * gap, axis=1, keepdims=True)
            spread_sum += inner
            grad = (mix_lambda / VIEWS) * prob * (gap - inner)
            if v == 0:
                grad += prob - onehot
            logit[v, b] = (factor * grad).astype(bf16)
        cross = -jnp.sum(onehot * logs[0], axis=1, keepdims=True)
        losses = cross + mix_lambda * (spread_sum / VIEWS)
        loss_ref[b : b + 1, :] = jnp.sum(jnp.where(row == col, losses, 0.0), axis=0, keepdims=True)

    grads = logit[...].reshape(VIEWS * 2 * BLOCK, CLASSES)
    for s in range(4):
        for half in range(2):
            lanes = slice(half * LANES, (half + 1) * LANES)
            term = dot(arrived[s, :, :, :, lanes].reshape(VIEWS * 2 * BLOCK, LANES), grads, TT)
            for e in range(2):
                part[s, 2 * half + e, :, :CLASSES] = term[64 * e : 64 * (e + 1)]
    for m in range(8):
        lanes = slice(m * LANES, (m + 1) * LANES)
        term = dot(hid[:, :, :, lanes].reshape(VIEWS * 2 * BLOCK, LANES), grads, TT)
        for e in range(2):
            part[2 * (m % 2) + e, m // 2, :, CLASSES:] = term[64 * e : 64 * (e + 1)]

    sum_core = [remote(part.at[2 * xs + 1 - k], got_a.at[n], core)
                for n, xs in enumerate((1 - xx, xx))]
    for copy in sum_core:
        copy.start()
    sum_core[0].wait_recv()
    sum_a[0] = part[2 * (1 - xx) + k] + got_a[0]
    sum_across = remote(sum_a.at[0], got_b, across)
    sum_across.start()
    sum_core[1].wait_recv()
    sum_a[1] = part[2 * xx + k] + got_a[1]
    sum_across.wait_recv()
    sum_a[1] = sum_a[1] + got_b[...]
    sum_ctx = [remote(sum_a.at[1, (c + j) % count], got_c.at[j - 1], (g, (c + j) % count, f))
               for j in range(1, count)]
    for copy in sum_ctx:
        copy.start()
    for copy in sum_ctx:
        copy.wait_recv()
    done = sum_a[1, c]
    for j in range(count - 1):
        done = done + got_c[j]
    head_grad_ref[...] = done[:, CLASSES:]
    pieces = jnp.concatenate([part_.astype(bf16) for part_ in thirds(done[:, :CLASSES])], axis=0)
    out = dot(pieces, head[...], NT)
    grad_ref[...] = out[0:64] + out[64:128] + out[128:192]

    sends = [copy for q in range(2) for copy in first[q] + onward[q]]
    sends += [copy for pair in relays for copy in pair]
    sends += list(beside) + [patch_core] + patch_across + patch_relay
    sends += [out_across, out_core, out_relay]
    sends += [copy for v in range(VIEWS) for copy in square_out[v] + normed_out[v]]
    sends += sum_core + [sum_across] + sum_ctx
    for copy in sends:
        copy.wait_send()
    for v in range(VIEWS):
        @pl.when(c < count - 1)
        def _():
            chain[v][0].wait_send()

        @pl.when(c > 0)
        def _():
            chain[v][1].wait_send()


def fused(patches, labels, op_ids, mix_codes, aug_gains, in_weight, dt_weight, dt_bias,
          decay_log, skip_gain, norm_gain, out_weight, head_weight):
    rows = patches.shape[0]
    ctx_count, shards = lax.axis_size("ctx"), lax.axis_size("fsdp")
    factor = loss_scale / (rows * ctx_count * shards)
    smem = pl.BlockSpec(memory_space=pltpu.SMEM)
    vmem = pl.BlockSpec(memory_space=pltpu.VMEM)
    far = pl.BlockSpec(memory_space=pl.ANY)
    V = pltpu.VMEM
    grad_out, grad_head, losses = pl.pallas_call(
        functools.partial(fused_kernel, factor),
        name="fused",
        out_shape=[
            jax.ShapeDtypeStruct((64, D), f32),
            jax.ShapeDtypeStruct((64, CLASSES), f32),
            jax.ShapeDtypeStruct((2, LANES), f32),
        ],
        in_specs=[smem] * 5 + [vmem] * 4 + [far] * 4,
        out_specs=[vmem] * 3,
        scratch_shapes=[
            V((256, 1536), bf16), V((4, 256, 256), bf16), V((256, 640), bf16), V((4, 256, 896), bf16),
            V((256, 256), bf16), V((4, 256, D), bf16), V((VIEWS, D), f32),
            V((VIEWS, 8, 128, 256), bf16), V((VIEWS, 8, 128, 512), bf16), V((VIEWS, 8, 32, 128), f32),
            V((VIEWS, 8, 8, 128), f32), V((VIEWS, 8, 8, 128), f32), V((VIEWS, 8, 8, 128), f32),
            V((8, 8, 512), f32), V((8, 128, 256), f32), V((VIEWS, 2, 8, 128, 256), f32),
            V((VIEWS, 2, 128, 256), f32), V((VIEWS, 8, 512), f32), V((VIEWS, 2, 128, 256), f32),
            V((VIEWS, 8, 128, 256), f32), V((VIEWS, 8, 128), f32), V((PEERS, VIEWS, 8, 128), f32),
            V((VIEWS, 4, 2, 128, 256), bf16), V((4, VIEWS, 2, 128, 256), bf16),
            V((4, 4, 64, D), bf16), V((D, CLASSES), bf16), V((VIEWS, 2, 128, D), bf16),
            V((VIEWS, 2, 128, CLASSES), bf16), V((4, 4, 64, 256), f32), V((2, 4, 64, 256), f32),
            V((2, 4, 64, 256), f32), V((4, 64, 256), f32), V((3, 64, 256), f32),
            V((32, 512), bf16), V((32, 1024), bf16), V((128, 256), bf16), V((8, 256), f32),
            pltpu.SemaphoreType.DMA((8,)),
            pltpu.SemaphoreType.DMA((72,)), pltpu.SemaphoreType.DMA((72,)),
        ],
        compiler_params=pltpu.CompilerParams(
            collective_id=0, has_side_effects=True, vmem_limit_bytes=56 << 20),
        cost_estimate=pl.CostEstimate(flops=20 << 30, bytes_accessed=8 << 20, transcendentals=0),
    )(op_ids, mix_codes, dt_bias, decay_log, skip_gain[None, :],
      aug_gains, norm_gain.reshape(8, LANES), labels.reshape(2, LANES), dt_weight,
      patches, in_weight, out_weight.reshape(4, 64, D), head_weight)
    return grad_out, grad_head, losses.reshape(rows)


def solution(mesh):
    sizes = dict(mesh.shape)
    small = sizes["groups"] == 2 and sizes["ctx"] == 4 and sizes["fsdp"] == 4
    return jax.shard_map(
        fused if small else on_device,
        mesh=mesh,
        in_specs=(
            P(("groups", "ctx", "fsdp"), None),
            P(("groups", "ctx", "fsdp")),
            P("groups", None),
            P("groups", None),
            P(),
            P("fsdp", None),
            P("fsdp", None),
            P(),
            P(),
            P(),
            P(),
            P("fsdp", None),
            P(),
        ),
        out_specs=(
            P(("groups", "ctx", "fsdp"), None),
            P(("groups", "ctx", "fsdp"), None),
            P(("groups", "ctx", "fsdp")),
        ),
        check_vma=False,
    )
```

```python
import functools
import jax
import jax.numpy as jnp
from jax import lax
from jax.experimental import pallas as pl
from jax.experimental.pallas import tpu as pltpu
from jax.sharding import PartitionSpec as P

D = 1024
HEADS = 16
HEAD_DIM = 64
STATE = 128
CLASSES = 128
VIEWS = 3
NOPS = 9
WIDTH_AUG = 3
BLOCK = 128
LANES = 128
LOG_ROWS = 8


loss_scale = 256.0
mix_lambda = 12.0
highest = lax.Precision.HIGHEST
f32 = jnp.float32
bf16 = jnp.bfloat16


def view_scales(op_ids, mix_codes, aug_gains):
    code_values = mix_codes.astype(jnp.float32)
    weights = code_values[:, :WIDTH_AUG] / jnp.sum(
        code_values[:, :WIDTH_AUG], axis=1, keepdims=True
    )
    keep_share = code_values[:, WIDTH_AUG] / 9.0
    onehot = (op_ids[:, :, None] == jnp.arange(NOPS, dtype=jnp.int32)[None, None, :]).astype(
        jnp.float32
    )
    op_weights = jnp.sum(onehot * weights[:, :, None], axis=1)
    mixed_gain = jnp.dot(op_weights, aug_gains, precision=highest)
    scaled = keep_share[:, None] + (1.0 - keep_share[:, None]) * mixed_gain
    return jnp.concatenate([jnp.ones((1, D), jnp.float32), scaled], axis=0)


def halves(value):
    high = value.astype(bf16)
    return high, (value - high.astype(f32)).astype(bf16)


def thirds(value):
    high = value.astype(bf16)
    rest = value - high.astype(f32)
    mid = rest.astype(bf16)
    return high, mid, (rest - mid.astype(f32)).astype(bf16)


def dot(a, b, dims=((1,), (0,))):
    return lax.dot_general(a, b, (dims, ((), ())), preferred_element_type=f32)


def spread(columns, first, heads):
    rows = columns.shape[0]
    lane = lax.broadcasted_iota(jnp.int32, (rows, LANES), 1)
    pieces = []
    for h in range(first, first + heads, 2):
        left = jnp.broadcast_to(columns[:, h : h + 1], (rows, LANES))
        right = jnp.broadcast_to(columns[:, h + 1 : h + 2], (rows, LANES))
        pieces.append(jnp.where(lane < HEAD_DIM, left, right))
    return jnp.concatenate(pieces, axis=1) if len(pieces) > 1 else pieces[0]


def project_kernel(place_ref, patches_ref, scale_ref, weight_ref, x_ref, coef_ref, raw_ref):
    width = x_ref.shape[2]
    patches = patches_ref[...].astype(f32)
    for v in range(VIEWS):
        view = (scale_ref[v : v + 1, :] * patches).astype(bf16)
        out = dot(view, weight_ref[...])
        x_ref[v] = out[:, :width].astype(bf16)
        coef_ref[v] = out[:, width : width + 4 * STATE].astype(bf16)
        raw_ref[v] = out[:, width + 4 * STATE :]


def states_kernel(heads, raw_ref, x_ref, coef_ref, bias_ref, rate_ref,
                  final_ref, prefix_ref, steps_ref, run_ref, pos_ref):
    rows, width = x_ref.shape[1:]
    pieces = rows // BLOCK
    row = lax.broadcasted_iota(jnp.int32, (BLOCK, BLOCK), 0)
    col = lax.broadcasted_iota(jnp.int32, (BLOCK, BLOCK), 1)
    lower = (row >= col).astype(f32).astype(bf16)
    upper = (row <= col).astype(f32).astype(bf16)
    is_forward = col < heads

    def first_pass(i, carried):
        state, total = carried
        at = pl.ds(pl.multiple_of(i * BLOCK, BLOCK), BLOCK)
        raw = raw_ref[0, at, :] + bias_ref[...]
        steps = jnp.maximum(raw, 0.0) + jnp.log1p(jnp.exp(-jnp.abs(raw)))
        parts = thirds(steps * rate_ref[...])
        down = sum(dot(lower, part) for part in parts)
        up = sum(dot(upper, part) for part in parts)
        run = jnp.where(is_forward, down, up)
        steps_ref[0, at, :] = steps
        run_ref[0, at, :] = run
        pos_ref[0, at, :] = run + total
        last = jnp.where(is_forward[:1], run[BLOCK - 1 :], run[:1])
        x = x_ref[0, at, :].astype(f32)
        weight = spread(jnp.exp(last - run) * steps, 0, heads)
        high, low = halves(weight * x)
        write = coef_ref[0, at, :STATE]
        fresh = dot(write, high, ((0,), (0,))) + dot(write, low, ((0,), (0,)))
        s_high, s_low = halves(state)
        prefix_ref[0, 0, i, :STATE, :] = s_high
        prefix_ref[0, 0, i, STATE:, :] = s_low
        return spread(jnp.exp(last), 0, heads) * state + fresh, total + last

    zero = jnp.zeros((STATE, width), f32)
    no_log = jnp.zeros((1, LANES), f32)
    state, total = lax.fori_loop(0, pieces, first_pass, (zero, no_log), unroll=4)
    final_ref[0, 0, :STATE, :] = state
    final_ref[0, 0, STATE:, :] = jnp.broadcast_to(spread(total, 0, heads), (LOG_ROWS, width))

    def second_pass(k, carried):
        state, total = carried
        i = pieces - 1 - k
        at = pl.ds(pl.multiple_of(i * BLOCK, BLOCK), BLOCK)
        run = run_ref[0, at, :]
        last = run[:1]
        pos_ref[0, at, :] = jnp.where(is_forward, pos_ref[0, at, :], run + total)
        x = x_ref[0, at, :].astype(f32)
        weight = spread(jnp.exp(last - run) * steps_ref[0, at, :], heads, heads)
        high, low = halves(weight * x)
        write = coef_ref[0, at, 2 * STATE : 3 * STATE]
        fresh = dot(write, high, ((0,), (0,))) + dot(write, low, ((0,), (0,)))
        s_high, s_low = halves(state)
        prefix_ref[0, 1, i, :STATE, :] = s_high
        prefix_ref[0, 1, i, STATE:, :] = s_low
        return spread(jnp.exp(last), heads, heads) * state + fresh, total + last

    state, total = lax.fori_loop(0, pieces, second_pass, (zero, no_log), unroll=4)
    final_ref[0, 1, :STATE, :] = state
    final_ref[0, 1, STATE:, :] = jnp.broadcast_to(spread(total, heads, heads), (LOG_ROWS, width))


def inside_kernel(heads, x_ref, coef_ref, prefix_ref, steps_ref, run_ref, skip_ref, *rest):
    out_ref = rest[-1]
    row = lax.broadcasted_iota(jnp.int32, (BLOCK, BLOCK), 0)
    col = lax.broadcasted_iota(jnp.int32, (BLOCK, BLOCK), 1)
    below, above = row > col, row < col
    x = x_ref[0]
    steps_t = steps_ref[0].T
    run = run_ref[0]
    run_t = run.T
    coef = coef_ref[0]
    write_f, read_f = coef[:, :STATE], coef[:, STATE : 2 * STATE]
    write_r, read_r = coef[:, 2 * STATE : 3 * STATE], coef[:, 3 * STATE :]
    score_f = dot(read_f, write_f, ((1,), (1,)))
    score_r = dot(read_r, write_r, ((1,), (1,)))
    lane = lax.broadcasted_iota(jnp.int32, (BLOCK, LANES), 1)
    zero = jnp.zeros((BLOCK, LANES), bf16)
    pieces = []
    for pair in range(heads // 2):
        highs, lows = [], []
        for h in (2 * pair, 2 * pair + 1):
            r = heads + h
            gap = jnp.where(
                below, run[:, h : h + 1] - run_t[h : h + 1], run[:, r : r + 1] - run_t[r : r + 1]
            )
            gap = jnp.where(row == col, 0.0, gap)
            from_f = score_f * steps_t[h : h + 1]
            from_r = score_r * steps_t[r : r + 1]
            weight = jnp.where(below, from_f, jnp.where(above, from_r, from_f + from_r))
            high, low = halves(weight * jnp.exp(gap))
            highs.append(high)
            lows.append(low)
        values = x[:, pair * LANES : (pair + 1) * LANES]
        stacked = jnp.concatenate(
            [jnp.where(lane < HEAD_DIM, values, zero), jnp.where(lane < HEAD_DIM, zero, values)],
            axis=0,
        )
        pieces.append(
            dot(jnp.concatenate(highs, axis=1), stacked)
            + dot(jnp.concatenate(lows, axis=1), stacked)
        )
    inside = jnp.concatenate(pieces, axis=1) if len(pieces) > 1 else pieces[0]
    grown = jnp.exp(run)
    carried_f = dot(jnp.concatenate([read_f, read_f], axis=1), prefix_ref[0, 0, 0])
    carried_r = dot(jnp.concatenate([read_r, read_r], axis=1), prefix_ref[0, 1, 0])
    out_ref[0] = (
        inside
        + spread(grown, 0, heads) * carried_f
        + spread(grown, heads, heads) * carried_r
        + skip_ref[...] * x.astype(f32)
    )


def incoming_kernel(heads, forward_ref, reverse_ref, coef_ref, pos_ref, local_ref,
                    mixed_ref, square_ref, held):
    width = local_ref.shape[2]

    @pl.when(pl.program_id(1) == 0)
    def _():
        for way, before in enumerate((forward_ref, reverse_ref)):
            high, low = halves(before[0])
            held[way, :STATE, :] = high
            held[way, STATE:, :] = low

    grown = jnp.exp(pos_ref[0])
    coef = coef_ref[0]
    read_f = coef[:, STATE : 2 * STATE]
    read_r = coef[:, 3 * STATE :]
    mixed = (
        local_ref[0]
        + spread(grown, 0, heads) * dot(jnp.concatenate([read_f, read_f], axis=1), held[0])
        + spread(grown, heads, heads) * dot(jnp.concatenate([read_r, read_r], axis=1), held[1])
    )
    mixed_ref[0] = mixed
    ones = jnp.ones((8, width), bf16)
    square_ref[0] = sum(dot(ones, part, ((1,), (1,))) for part in thirds(mixed * mixed))


def tail_kernel(shards, factor, normed_ref, out_w_ref, head_ref, patches_ref, scale_ref,
                label_ref, logit_ref, loss_ref, head_grad_ref, hidden_ref=None):
    rows = patches_ref.shape[0]
    head = head_ref[...]
    patches = patches_ref[...].astype(f32)
    hiddens, logs = [], []
    for v in range(VIEWS):
        total = dot(normed_ref[0, v], out_w_ref[0])
        for s in range(1, shards):
            total += dot(normed_ref[s, v], out_w_ref[s])
        view = (scale_ref[v : v + 1, :] * patches).astype(bf16)
        hidden = (view.astype(f32) + total).astype(bf16)
        hiddens.append(hidden)
        logits = dot(hidden, head)
        shifted = logits - jnp.max(logits, axis=1, keepdims=True)
        logs.append(shifted - jnp.log(jnp.sum(jnp.exp(shifted), axis=1, keepdims=True)))
    top = jnp.maximum(jnp.maximum(logs[0], logs[1]), logs[2])
    mean = top + jnp.log(sum(jnp.exp(log - top) for log in logs)) - jnp.log(f32(VIEWS))
    lane = lax.broadcasted_iota(jnp.int32, (rows, CLASSES), 1)
    onehot = (lane == label_ref[...]).astype(f32)
    spread_sum = jnp.zeros((rows, 1), f32)
    grads = []
    for v in range(VIEWS):
        prob = jnp.exp(logs[v])
        gap = logs[v] - mean
        inner = jnp.sum(prob * gap, axis=1, keepdims=True)
        spread_sum += inner
        grad = (mix_lambda / VIEWS) * prob * (gap - inner)
        if v == 0:
            grad += prob - onehot
        grads.append((factor * grad).astype(bf16))
        logit_ref[v] = grads[v]
    cross = -jnp.sum(onehot * logs[0], axis=1, keepdims=True)
    loss_ref[...] = cross + mix_lambda * (spread_sum / VIEWS)
    update = sum(dot(hiddens[v], grads[v], ((0,), (0,))) for v in range(VIEWS))

    @pl.when(pl.program_id(0) == 0)
    def _():
        head_grad_ref[...] = update

    @pl.when(pl.program_id(0) > 0)
    def _():
        head_grad_ref[...] += update


def grad_kernel(shards, normed_ref, logit_ref, head_ref, out_ref):
    grads = logit_ref[0, 0]
    hidden = dot(grads, head_ref[...], ((1,), (1,))).astype(bf16)
    update = dot(normed_ref[0], hidden, ((0,), (0,)))
    first = (pl.program_id(0) == 0) & (pl.program_id(1) == 0)

    @pl.when(first)
    def _():
        out_ref[...] = update

    @pl.when(jnp.logical_not(first))
    def _():
        out_ref[...] += update


def call(kernel, name, flops, moved, limit=48 << 20, **options):
    return pl.pallas_call(
        kernel,
        name=name,
        compiler_params=pltpu.CompilerParams(vmem_limit_bytes=limit),
        cost_estimate=pl.CostEstimate(flops=flops, bytes_accessed=moved, transcendentals=0),
        **options,
    )


def carried_in(state, decay, axis, reverse):
    count = lax.axis_size(axis)
    if reverse:
        hops = [(j, j - 1) for j in range(1, count)]
    else:
        hops = [(j, j + 1) for j in range(count - 1)]
    sent, got = state, jnp.zeros_like(state)
    for hop in range(count - 1):
        got = lax.ppermute(sent, axis, hops)
        sent = decay * got + state
    return got


def scatter_sum(terms, axes, count):
    blocks = terms.reshape(count, -1, terms.shape[1])
    return jnp.sum(lax.all_to_all(blocks, axes, split_axis=0, concat_axis=0), axis=0)


def on_device(
    patches,
    labels,
    op_ids,
    mix_codes,
    aug_gains,
    in_weight,
    dt_weight,
    dt_bias,
    decay_log,
    skip_gain,
    norm_gain,
    out_weight,
    head_weight,
):
    row_count = patches.shape[0]
    ctx_count = lax.axis_size("ctx")
    shards = lax.axis_size("fsdp")
    place = lax.axis_index("fsdp")
    total_patches = row_count * ctx_count * shards
    inner = out_weight.shape[0] * shards
    heads = HEADS // shards
    width = heads * HEAD_DIM
    rows = row_count * shards
    pieces = rows // BLOCK

    if shards == 4:
        across = lax.ppermute(patches, "fsdp", [(f, f ^ 2) for f in range(shards)])
        beside = lax.ppermute(patches, "fsdp", [(f, f ^ 1) for f in range(shards)])
        corner = lax.ppermute(across, "fsdp", [(f, f ^ 1) for f in range(shards)])
        patches_all = jnp.concatenate([patches, beside, across, corner], axis=0)
        flip = place
    else:
        patches_all = lax.all_gather(patches, "fsdp", axis=0, tiled=True)
        flip = jnp.zeros_like(place)
    columns_in = inner + 4 * STATE
    depth = in_weight.shape[0]
    sent_weight = jnp.concatenate(
        [
            in_weight[:, :inner]
            .reshape(depth, heads, shards, HEAD_DIM)
            .transpose(2, 0, 1, 3)
            .reshape(shards, depth, width),
            jnp.broadcast_to(in_weight[None, :, inner:], (shards, depth, 4 * STATE)),
            dt_weight.reshape(depth, 2 * heads, shards).transpose(2, 0, 1),
            jnp.zeros((shards, depth, LANES - 2 * heads), bf16),
        ],
        axis=2,
    )
    mine_weight = lax.all_to_all(sent_weight, "fsdp", split_axis=0, concat_axis=0)
    mine_weight = mine_weight.reshape(D, width + 5 * STATE)
    scales = view_scales(op_ids, mix_codes, aug_gains)
    tile = min(row_count, 128)
    per = row_count // tile
    placed = lambda s, i, flip_ref: ((s ^ flip_ref[0]) * per + i, 0)
    piece = lambda lanes: pl.BlockSpec((VIEWS, tile, lanes), lambda s, i, _: (0, s * per + i, 0))
    constant = lambda *dims: pl.BlockSpec(dims, lambda *_: (0,) * len(dims))
    x, coef, raw = call(
        project_kernel, "project",
        VIEWS * rows * D * (width + 5 * STATE) * 2, rows * D * 8,
        grid_spec=pltpu.PrefetchScalarGridSpec(
            num_scalar_prefetch=1,
            grid=(shards, per),
            in_specs=[pl.BlockSpec((tile, D), placed), constant(VIEWS, D),
                      constant(D, width + 5 * STATE)],
            out_specs=[piece(width), piece(4 * STATE), piece(LANES)],
        ),
        out_shape=[
            jax.ShapeDtypeStruct((VIEWS, rows, width), bf16),
            jax.ShapeDtypeStruct((VIEWS, rows, 4 * STATE), bf16),
            jax.ShapeDtypeStruct((VIEWS, rows, LANES), f32),
        ],
    )(flip.reshape(1).astype(jnp.int32), patches_all, scales, mine_weight)
    raw, out_later = lax.optimization_barrier((raw, out_weight))
    out_all = lax.all_gather(out_later, "fsdp", axis=0, tiled=True)

    def local_lanes(values):
        picked = lax.dynamic_index_in_dim(values.reshape(2 * heads, shards), place, 1, False)
        return jnp.pad(picked, (0, LANES - 2 * heads))[None, :]

    bias = local_lanes(dt_bias)
    rate = local_lanes(-jnp.exp(decay_log))
    skip = lax.dynamic_index_in_dim(skip_gain.reshape(heads, shards), place, 1, False)
    skip = jnp.repeat(skip, HEAD_DIM)[None, :]
    gain = norm_gain.reshape(heads, shards, HEAD_DIM)
    gain = lax.dynamic_index_in_dim(gain, place, 1, False).reshape(1, width)

    whole = lambda *dims: pl.BlockSpec((1, *dims), lambda v: (v,) + (0,) * len(dims))
    fixed = lambda *dims: pl.BlockSpec(dims, lambda *_: (0,) * len(dims))
    final, prefix, steps, run, pos = call(
        functools.partial(states_kernel, heads), "states",
        VIEWS * rows * STATE * width * 8, VIEWS * rows * 8192,
        grid=(VIEWS,),
        in_specs=[whole(rows, LANES), whole(rows, width), whole(rows, 4 * STATE),
                  fixed(1, LANES), fixed(1, LANES)],
        out_specs=[whole(2, STATE + LOG_ROWS, width), whole(2, pieces, 2 * STATE, width),
                   whole(rows, LANES), whole(rows, LANES), whole(rows, LANES)],
        out_shape=[
            jax.ShapeDtypeStruct((VIEWS, 2, STATE + LOG_ROWS, width), f32),
            jax.ShapeDtypeStruct((VIEWS, 2, pieces, 2 * STATE, width), bf16),
            jax.ShapeDtypeStruct((VIEWS, rows, LANES), f32),
            jax.ShapeDtypeStruct((VIEWS, rows, LANES), f32),
            jax.ShapeDtypeStruct((VIEWS, rows, LANES), f32),
        ],
    )(raw, x, coef, bias, rate)
    decay = jnp.exp(final[:, :, STATE : STATE + 1, :])
    forward_in = carried_in(final[:, 0, :STATE], decay[:, 0], "ctx", False)
    reverse_in = carried_in(final[:, 1, :STATE], decay[:, 1], "ctx", True)

    local = ()
    for v in range(VIEWS):
        at = lambda *dims, v=v: pl.BlockSpec(
            (1, *dims), lambda i: (v, i) + (0,) * (len(dims) - 1)
        )
        local = (call(
            functools.partial(inside_kernel, heads), "inside",
            rows * D * 8192, rows * 8192,
            grid=(pieces,),
            in_specs=[at(BLOCK, width), at(BLOCK, 4 * STATE),
                      pl.BlockSpec((1, 2, 1, 2 * STATE, width), lambda i, v=v: (v, 0, i, 0, 0)),
                      at(BLOCK, LANES), at(BLOCK, LANES), fixed(1, width)]
            + [pl.BlockSpec(memory_space=pl.ANY)] * len(local),
            out_specs=at(BLOCK, width),
            out_shape=jax.ShapeDtypeStruct((VIEWS, rows, width), f32),
            input_output_aliases={6: 0} if local else {},
        )(x, coef, prefix, steps, run, skip, *local),)
    (local,) = local
    block = lambda *dims: pl.BlockSpec((1, *dims), lambda v, i: (v, i) + (0,) * (len(dims) - 1))
    entering = pl.BlockSpec((1, STATE, width), lambda v, i: (v, 0, 0))

    span = min(rows, 512)
    mixed, squares = call(
        functools.partial(incoming_kernel, heads), "incoming",
        VIEWS * rows * STATE * width * 8, VIEWS * rows * 8192,
        grid=(VIEWS, rows // span),
        in_specs=[
            entering, entering,
            block(span, 4 * STATE), block(span, LANES), block(span, width)],
        out_specs=[block(span, width), pl.BlockSpec((1, 8, span), lambda v, i: (v, 0, i))],
        out_shape=[
            jax.ShapeDtypeStruct((VIEWS, rows, width), f32),
            jax.ShapeDtypeStruct((VIEWS, 8, rows), f32),
        ],
        scratch_shapes=[pltpu.VMEM((2, 2 * STATE, width), bf16)],
    )(forward_in, reverse_in, coef, pos, local)

    square_total = jnp.sum(lax.all_gather(squares[:, 0, :], "fsdp"), axis=0)
    scaling = lax.rsqrt(square_total / inner + 1e-05)
    normed = (mixed * scaling[:, :, None] * gain[None]).astype(bf16)
    outgoing = normed.reshape(VIEWS, shards, row_count, width).transpose(1, 0, 2, 3)
    arrived = lax.all_to_all(outgoing, "fsdp", split_axis=0, concat_axis=0)

    out_own = out_all.reshape(heads, shards, HEAD_DIM, D).transpose(1, 0, 2, 3)
    out_own = out_own.reshape(shards, width, D)
    tile = min(row_count, 128)
    grads, losses, head_term = call(
        functools.partial(tail_kernel, shards, loss_scale / total_patches), "tail",
        VIEWS * row_count * D * 3000, 6 << 20,
        grid=(row_count // tile,),
        in_specs=[
            pl.BlockSpec((shards, VIEWS, tile, width), lambda i: (0, 0, i, 0)),
            fixed(shards, width, D), fixed(D, CLASSES),
            pl.BlockSpec((tile, D), lambda i: (i, 0)),
            fixed(VIEWS, D),
            pl.BlockSpec((tile, 1), lambda i: (i, 0))],
        out_specs=[
            pl.BlockSpec((VIEWS, tile, CLASSES), lambda i: (0, i, 0)),
            pl.BlockSpec((tile, 1), lambda i: (i, 0)),
            fixed(D, CLASSES)],
        out_shape=[
            jax.ShapeDtypeStruct((VIEWS, row_count, CLASSES), bf16),
            jax.ShapeDtypeStruct((row_count, 1), f32),
            jax.ShapeDtypeStruct((D, CLASSES), f32),
        ],
    )(arrived, out_own, head_weight, patches, scales, labels[:, None])

    if ctx_count * shards == HEADS:
        grads_all = lax.all_gather(grads, "fsdp")
        grad_rows = call(
            functools.partial(grad_kernel, shards), "grads",
            VIEWS * rows * D * (width + CLASSES) * 2, 8 << 20,
            grid=(VIEWS, shards),
            in_specs=[
                pl.BlockSpec((1, row_count, width), lambda v, s: (v, s, 0)),
                pl.BlockSpec((1, 1, row_count, CLASSES), lambda v, s: (s, v, 0, 0)),
                fixed(D, CLASSES)],
            out_specs=fixed(width, D),
            out_shape=jax.ShapeDtypeStruct((width, D), f32),
        )(normed, grads_all, head_weight)
        grad_out = scatter_sum(grad_rows, "ctx", ctx_count)
    else:
        grad_hidden = lax.dot_general(
            grads, head_weight, (((2,), (1,)), ((), ())), preferred_element_type=f32
        ).astype(bf16)
        grad_rows = lax.dot_general(
            arrived, grad_hidden, (((1, 2), (0, 1)), ((), ())), preferred_element_type=f32
        )
        grad_rows = grad_rows.reshape(shards, heads, HEAD_DIM, D).transpose(1, 0, 2, 3)
        grad_out = lax.psum_scatter(
            grad_rows.reshape(inner, D), ("ctx", "fsdp"), scatter_dimension=0, tiled=True
        )
    grad_head = scatter_sum(head_term, ("ctx", "fsdp"), ctx_count * shards)
    return (grad_out, grad_head, losses[:, 0])


LOG2E = 1.4426950408889634
PEERS = 3
CHUNKS = 4
UNROLL_S = 4
UNROLL_I = 4
UNROLL_C = 4


def stack3(value):
    high = value.astype(bf16).astype(f32)
    rest = value - high
    mid = rest.astype(bf16).astype(f32)
    low = rest - mid
    return jnp.concatenate([high, mid, low, jnp.zeros_like(value)], axis=0).astype(bf16)


def side3(value):
    return jnp.concatenate(thirds(value), axis=1)


TT = ((0,), (0,))
NT = ((1,), (1,))


def fused_kernel(factor, ops_ref, codes_ref, bias_ref, decay_ref, skip_ref,
                 gains_ref, norm_ref, label_ref, dtw_ref,
                 patches_ref, inw_ref, outw_ref, head_hbm,
                 sum_ref, loss_ref,
                 w, wx, wdt, dts, pall, scales,
                 x_s, coef_s, rawt, steps_s, run_s, weight_p, grown_p, run_p, row_s, fresh_s,
                 prefix, fin, inc,
                 local, sq, sq_in, normed, arrived, ow, head, hid, logit, part, sum_a, got_a, got_b,
                 got_c, spread_s, lane_s, wide_s, cum_s, gain_s, loc_sem, send_sem, recv_sem):
    MESH = pl.DeviceIdType.MESH
    g, c, f = lax.axis_index("groups"), lax.axis_index("ctx"), lax.axis_index("fsdp")
    count = lax.axis_size("ctx")
    xx, k = f // 2, f % 2
    f1 = f + 1 - 2 * k
    f2 = f + 2 - 4 * xx
    f3 = f2 + 1 - 2 * k
    core, across, corner, other = (g, c, f1), (g, c, f2), (g, c, f3), (1 - g, c, f)
    used = [0]

    def tile(j, chip):
        return pl.ds(pl.multiple_of((2 * j + chip) * LANES, LANES), LANES)

    def remote(src, dst, to):
        n = used[0]
        used[0] += 1
        return pltpu.make_async_remote_copy(
            src_ref=src, dst_ref=dst, send_sem=send_sem.at[n], recv_sem=recv_sem.at[n],
            device_id=to, device_id_type=MESH)

    local_copies = [
        pltpu.make_async_copy(inw_ref.at[:, tile(j, xx)], w.at[f, :, pl.ds(j * LANES, LANES)],
                              loc_sem.at[8 + j]) for j in range(4)]
    local_copies += [
        pltpu.make_async_copy(inw_ref.at[:, pl.ds(D, 512)], w.at[f, :, pl.ds(512, 512)],
                              loc_sem.at[12]),
        pltpu.make_async_copy(dtw_ref, dts.at[f], loc_sem.at[13])]
    load_own = pltpu.make_async_copy(patches_ref, pall.at[f], loc_sem.at[1])
    load_head = pltpu.make_async_copy(head_hbm, head, loc_sem.at[2])
    load_out = pltpu.make_async_copy(outw_ref, ow.at[:, f], loc_sem.at[3])
    for copy in local_copies + [load_own, load_head, load_out]:
        copy.start()

    barrier = pltpu.get_barrier_semaphore()
    for to in (core, across, corner, other):
        pl.semaphore_signal(barrier, inc=1, device_id=to, device_id_type=MESH)
    for j in range(1, count):
        pl.semaphore_signal(barrier, inc=1, device_id=(g, (c + j) % count, f), device_id_type=MESH)

    pl.semaphore_wait(barrier, 3 + count)

    chunk = 128 // CHUNKS

    def span(half, q):
        return pl.ds(pl.multiple_of(half * 128 + q * chunk, chunk), chunk)

    first = []
    for q in range(CHUNKS):
        rows = span(g, q)
        group = [remote(inw_ref.at[rows, tile(j, 1 - xx)], w.at[f, rows, pl.ds(j * LANES, LANES)],
                        across) for j in range(4)]
        group.append(remote(inw_ref.at[rows, pl.ds(D, 512)], w.at[f, rows, pl.ds(512, 512)], across))
        for copy in group:
            copy.start()
        first.append(group)
    beside = [remote(inw_ref.at[:, tile(j, xx)], w.at[f, :, pl.ds(j * LANES, LANES)], core)
              for j in range(4)]
    beside.append(remote(inw_ref.at[:, pl.ds(D, 512)], w.at[f, :, pl.ds(512, 512)], core))
    small = [remote(dtw_ref, dts.at[f], to) for to in (across, corner, core)]
    patch_core = remote(patches_ref, pall.at[f], core)
    for copy in small + beside:
        copy.start()
    patch_core.start()
    patch_across = []
    for b in range(2):
        rows = pl.ds(b * 128, 128)
        patch_across.append(remote(patches_ref.at[rows], pall.at[f, rows], across))

    pick_row = lax.broadcasted_iota(jnp.int32, (2 * HEADS, LANES), 0)
    pick_col = lax.broadcasted_iota(jnp.int32, (2 * HEADS, LANES), 1)
    head_at = 16 * ((pick_col // 4) % 2) + 4 * (pick_col % 4) + pick_col // 8
    pick = ((pick_row == head_at) & (pick_col < 32)).astype(f32).astype(bf16)
    half_row = lax.broadcasted_iota(jnp.int32, (512, 256), 0)
    half_col = lax.broadcasted_iota(jnp.int32, (512, 256), 1)
    mine = (half_row == 128 * (half_col // 64) + 64 * k + half_col % 64).astype(f32).astype(bf16)
    row32 = lax.broadcasted_iota(jnp.int32, (32, 512), 0)
    col32 = lax.broadcasted_iota(jnp.int32, (32, 512), 1)
    spread_s[...] = ((row32 % 8 == col32 // 64) & (row32 < 24)).astype(f32).astype(bf16)
    row32 = lax.broadcasted_iota(jnp.int32, (32, 1024), 0)
    col32 = lax.broadcasted_iota(jnp.int32, (32, 1024), 1)
    row_l = lax.broadcasted_iota(jnp.int32, (LANES, 512), 0)
    col_l = lax.broadcasted_iota(jnp.int32, (LANES, 512), 1)
    lane_s[...] = (row_l == col_l // 64).astype(f32).astype(bf16)
    wide_s[...] = ((row32 % 8 == col32 // 128) & (row32 < 24)).astype(f32).astype(bf16)
    row = lax.broadcasted_iota(jnp.int32, (BLOCK, BLOCK), 0)
    col = lax.broadcasted_iota(jnp.int32, (BLOCK, BLOCK), 1)
    cum_s[:, :BLOCK] = (row <= col).astype(f32).astype(bf16)
    cum_s[:, BLOCK:] = (row >= col).astype(f32).astype(bf16)
    scales[0:1, :] = jnp.ones((1, D), f32)
    for j in range(2):
        codes = [jnp.full((1, D), codes_ref[j, i].astype(f32), f32) for i in range(WIDTH_AUG + 1)]
        whole = codes[0] + codes[1] + codes[2]
        shares = [codes[i] / whole for i in range(WIDTH_AUG)]
        keep = codes[WIDTH_AUG] / 9.0
        mixed_gain = jnp.zeros((1, D), f32)
        for n in range(NOPS):
            picked = jnp.zeros((1, D), f32)
            for i in range(WIDTH_AUG):
                picked += shares[i] * jnp.where(ops_ref[j, i] == n, 1.0, 0.0)
            mixed_gain += picked * gains_ref[n : n + 1, :]
        scales[j + 1 : j + 2, :] = keep + (1.0 - keep) * mixed_gain
    line = lax.broadcasted_iota(jnp.int32, (8, LANES), 0)
    bias = jnp.zeros((8, LANES), f32)
    rate = jnp.zeros((8, LANES), f32)
    for d in range(2):
        for j in range(4):
            bias = jnp.where(line == 4 * d + j, bias_ref[d, 4 * j + f], bias)
            rate = jnp.where(line == 4 * d + j, decay_ref[d, 4 * j + f], rate)
    rate = -jnp.exp(rate) * LOG2E
    lane_w = lax.broadcasted_iota(jnp.int32, (8, 256), 1)
    skip = jnp.zeros((8, 256), f32)
    for j in range(4):
        skip = jnp.where(lane_w // HEAD_DIM == j, skip_ref[0, 4 * j + f], skip)
    lane_n = lax.broadcasted_iota(jnp.int32, (8, LANES), 1)
    gain_parts = []
    for half in range(2):
        a = jnp.broadcast_to(norm_ref[pl.ds(4 * half + xx, 1), :], (8, LANES))
        b = jnp.broadcast_to(norm_ref[pl.ds(4 * half + 2 + xx, 1), :], (8, LANES))
        even = jnp.where(lane_n < 64, a, pltpu.roll(b, 64, 1))
        odd = jnp.where(lane_n < 64, pltpu.roll(a, 64, 1), b)
        gain_parts.append(jnp.where(k == 0, even, odd))
    gain_s[...] = jnp.concatenate(gain_parts, axis=1)

    relays, onward = [], []

    def to_core(rows):
        copy = remote(w.at[f2, rows], w.at[f2, rows], core)
        copy.start()
        relays.append(copy)

    def select(src):
        wx[src] = dot(w[src, :, :512], mine).astype(bf16)
        wdt[src] = dot(dts[src], pick, TT).astype(bf16)

    for q in range(CHUNKS):
        for copy in first[q]:
            copy.wait_recv()
        rows = span(g, q)
        copy = remote(w.at[f2, rows], w.at[f2, rows], other)
        copy.start()
        onward.append(copy)
        if q == CHUNKS - 2:
            for copy in patch_across:
                copy.start()
        to_core(rows)
    for copy in local_copies:
        copy.wait()
    for copy in small:
        copy.wait_recv()
    select(f)
    for copy in beside:
        copy.wait_recv()
    select(f1)
    for q in range(CHUNKS):
        onward[q].wait_recv()
        to_core(span(1 - g, q))
    select(f2)
    for copy in relays:
        copy.wait_recv()
    select(f3)
    load_own.wait()

    patch_relay = [
        remote(pall.at[f2, pl.ds(b * 128, 128)], pall.at[f2, pl.ds(b * 128, 128)], core)
        for b in range(2)
    ]
    out_across = remote(outw_ref, ow.at[:, f], across)
    out_core = remote(outw_ref, ow.at[:, f], core)
    out_relay = remote(ow.at[:, f2], ow.at[:, f2], core)

    def project(s, _):
        a = s // 4
        pair = (1 - a) * (s // 2) + a * (2 + s % 2)
        b = (1 - a) * (s % 2) + a * ((s - 4 * a) // 2)
        kb, xb = pair % 2, pair // 2
        src = 2 * (xx + xb - 2 * xx * xb) + (k + kb - 2 * k * kb)

        @pl.when(s == 2)
        def _():
            patch_core.wait_recv()

        for b_static in range(2):
            @pl.when(s == 4 + 2 * b_static)
            def _():
                patch_across[b_static].wait_recv()
                patch_relay[b_static].start()

            @pl.when(s == 5 + 2 * b_static)
            def _():
                patch_relay[b_static].wait_recv()

        rows = pall[src, pl.ds(pl.multiple_of(b * 128, 128), 128), :].astype(f32)
        view = jnp.concatenate(
            [(scales[v : v + 1, :] * rows).astype(bf16) for v in range(VIEWS)], axis=0)
        i = 2 * src + b
        out = dot(view, wx[...].reshape(D, 256)).astype(bf16)
        coef = dot(view, w[:, :, 512:].reshape(D, 512)).astype(bf16)
        raw = dot(view, wdt[...].reshape(D, LANES))
        for v in range(VIEWS):
            at = slice(v * 128, (v + 1) * 128)
            x_s[v, i] = out[at]
            coef_s[v, i] = coef[at]
            rawt[8 * v + i] = raw[at].T[:32]
        return 0

    lax.fori_loop(0, 8, project, 0)
    out_across.start()
    out_core.start()

    def triple(values):
        high = values.astype(bf16).astype(f32)
        rest = values - high
        mid = rest.astype(bf16).astype(f32)
        return high, mid, rest - mid

    def stacked(values):
        return jnp.concatenate([*triple(values), jnp.zeros_like(values)], axis=1).astype(bf16)

    blocks = VIEWS * 8
    raw = rawt[:, pl.ds(pl.multiple_of(8 * f, 8), 8), :] + bias[None]
    steps_all = jnp.maximum(raw, 0.0) + jnp.log1p(jnp.exp(-jnp.abs(raw)))
    logs = jnp.concatenate(triple(steps_all * rate[None]), axis=0).reshape(3 * blocks * 8, BLOCK)
    cum = dot(logs.astype(bf16), cum_s[...]).reshape(3, blocks, 8, 2 * BLOCK)
    cum = cum[0] + cum[1] + cum[2]
    way = lax.broadcasted_iota(jnp.int32, (blocks, 8, BLOCK), 1) < 4
    run_all = jnp.where(way, cum[:, :, :BLOCK], cum[:, :, BLOCK:])
    last_all = jnp.where(way, jnp.broadcast_to(cum[:, :, BLOCK - 1 : BLOCK], way.shape),
                         jnp.broadcast_to(cum[:, :, BLOCK : BLOCK + 1], way.shape))
    steps_s[...] = steps_all
    run_s[...] = run_all
    weight_p[...] = stacked(jnp.exp2(last_all - run_all) * steps_all)
    grown_p[...] = stacked(jnp.exp2(run_all))
    run_p[...] = stacked(run_all)
    totals, before = [], [None] * blocks
    for v in range(VIEWS):
        lasts = [last_all[8 * v + i] for i in range(8)]
        ahead_sum, behind_sum = [jnp.zeros((8, LANES), f32)], [jnp.zeros((8, LANES), f32)]
        for i in range(8):
            ahead_sum.append(ahead_sum[-1] + lasts[i])
            behind_sum.append(behind_sum[-1] + lasts[7 - i])
        for i in range(8):
            before[8 * v + i] = jnp.where(line < 4, ahead_sum[i], behind_sum[7 - i])[None]
        totals.append(jnp.where(line < 4, ahead_sum[8], behind_sum[8])[None])
    pad = [jnp.zeros((8 - VIEWS, 8, LANES), f32)]
    decays = jnp.exp2(jnp.concatenate([last_all] + before + totals + pad, axis=0))
    count_rows = 2 * blocks + 8
    on_lane = (lax.broadcasted_iota(jnp.int32, decays.shape, 1)
               == lax.broadcasted_iota(jnp.int32, decays.shape, 2))
    flat = jnp.sum(jnp.where(on_lane, decays, 0.0), axis=1)
    flat = dot(jnp.concatenate(triple(flat), axis=0).astype(bf16), lane_s[...])
    row_s[...] = flat[:count_rows] + flat[count_rows : 2 * count_rows] + flat[2 * count_rows :]

    def states(v):
        fin[v, 0] = jnp.zeros((STATE, 256), f32)
        fin[v, 1] = jnp.zeros((STATE, 256), f32)

        def forward(i, _):
            n = 8 * v + i
            xf = x_s[v, i].astype(f32)
            weight = dot(weight_p[n], spread_s[...], TT)
            for d in range(2):
                high, low = halves(weight[:, 256 * d : 256 * (d + 1)] * xf)
                write = coef_s[v, i, :, 2 * STATE * d : 2 * STATE * d + STATE].T
                fresh = dot(jnp.concatenate([write, write], axis=1),
                            jnp.concatenate([high, low], axis=0))
                if d == 0:
                    state = fin[v, 0]
                    prefix[v, 0, i] = state
                    fin[v, 0] = row_s[pl.ds(n, 1), :256] * state + fresh
                else:
                    fresh_s[i] = fresh
            return 0

        lax.fori_loop(0, 8, forward, 0, unroll=UNROLL_S)

        def backward(m, _):
            i = 7 - m
            state = fin[v, 1]
            prefix[v, 1, i] = state
            fin[v, 1] = row_s[pl.ds(8 * v + i, 1), 256:] * state + fresh_s[i]
            return 0

        lax.fori_loop(0, 8, backward, 0, unroll=8)

    ahead = (g, (c + 1) % count, f)
    behind = (g, (c + count - 1) % count, f)
    sides = (pl.ds(0, LANES), pl.ds(LANES, LANES))
    chain = [[[remote(fin.at[v, d, :, side], inc.at[v, d, :, side], (ahead, behind)[d])
               for side in sides] for d in range(2)] for v in range(VIEWS)]

    def hop(v, n):
        for d in range(2):
            place = c if d == 0 else count - 1 - c

            @pl.when(place == n)
            def _():
                if n == 0:
                    inc[v, d] = jnp.zeros((STATE, 256), f32)
                for half in range(2):
                    at = slice(half * LANES, (half + 1) * LANES)
                    if n > 0:
                        chain[v][d][half].wait_recv()
                        fin[v, d, :, at] = (
                            fin[v, d, :, at] + inc[v, d, :, at]
                            * row_s[2 * blocks + v : 2 * blocks + v + 1,
                                    256 * d + LANES * half : 256 * d + LANES * (half + 1)])
                    if n < count - 1:
                        chain[v][d][half].start()

    def inside(v, start):
        def body(i, _):
            x = x_s[v, i]
            n = 8 * v + i
            run, steps = run_s[n], steps_s[n]
            coef = coef_s[v, i]
            score_f = dot(coef[:, STATE : 2 * STATE], coef[:, :STATE], NT)
            score_r = dot(coef[:, 3 * STATE :], coef[:, 2 * STATE : 3 * STATE], NT)
            diagonal = jnp.sum(jnp.where(row == col, score_r, 0.0), axis=0, keepdims=True)
            extra = dot(stack3(steps * diagonal), spread_s[:, 256:], TT)
            wide = dot(run_p[n], wide_s[...], TT)
            keep = row >= col
            lane_b = lax.broadcasted_iota(jnp.int32, (BLOCK, LANES), 1)
            none = jnp.zeros((BLOCK, LANES), bf16)
            pieces = []
            for pair in range(2):
                highs, lows = [], []
                for h in (2 * pair, 2 * pair + 1):
                    r = 4 + h
                    gap = jnp.where(keep, wide[:, h * 128 : (h + 1) * 128] - run[h : h + 1],
                                    wide[:, r * 128 : (r + 1) * 128] - run[r : r + 1])
                    weight = jnp.where(keep, score_f * steps[h : h + 1], score_r * steps[r : r + 1])
                    high, low = halves(weight * jnp.exp2(gap))
                    highs.append(high)
                    lows.append(low)
                values = x[:, pair * LANES : (pair + 1) * LANES]
                left, right = jnp.where(lane_b < 64, values, none), jnp.where(lane_b < 64, none, values)
                pieces.append(dot(jnp.concatenate(highs + lows, axis=1),
                                  jnp.concatenate([left, right, left, right], axis=0)))
            local[v, i] = jnp.concatenate(pieces, axis=1) + (skip[0:1] + extra) * x.astype(f32)
            return 0

        lax.fori_loop(start, start + 4, body, 0, unroll=UNROLL_I)

    def carried(v):
        def body(i, _):
            n = 8 * v + i
            grown = dot(grown_p[n], spread_s[...], TT)
            decay = row_s[pl.ds(blocks + n, 1), :]
            mixed = local[v, i]
            for d in range(2):
                at = slice(256 * d, 256 * (d + 1))
                high, low = halves(prefix[v, d, i] + decay[:, at] * inc[v, d])
                read = coef_s[v, i, :, STATE * (1 + 2 * d) : STATE * (2 + 2 * d)]
                mixed += grown[:, at] * dot(jnp.concatenate([read, read], axis=1),
                                            jnp.concatenate([high, low], axis=0))
            local[v, i] = mixed
            square = mixed * mixed
            square = square[:, :LANES] + square[:, LANES:]
            sums = dot(jnp.ones((8, 3 * LANES), bf16), side3(square), NT)
            sq[v, pl.ds(i, 1), :] = sums[0:1]
            return 0

        lax.fori_loop(0, 8, body, 0, unroll=UNROLL_C)

    square_out = [[remote(sq.at[v], sq_in.at[p, v], to)
                   for p, to in enumerate((core, across, corner))] for v in range(VIEWS)]
    normed_out = [[remote(normed.at[v, fp], arrived.at[f, v], to)
                   for fp, to in ((f3, corner), (f2, across), (f1, core))] for v in range(VIEWS)]
    normed_own = [pltpu.make_async_copy(normed.at[v, f], arrived.at[f, v], loc_sem.at[4 + v])
                  for v in range(VIEWS)]

    def finish(v):
        for copy in square_out[v]:
            copy.wait_recv()
        total = (sq[v] + sq_in[0, v]) + (sq_in[1, v] + sq_in[2, v])
        parts = stack3(lax.rsqrt(total / D + 1e-05))
        row_i = lax.broadcasted_iota(jnp.int32, (32, 256), 0)

        def body(i, _):
            pick = ((row_i % 8 == i) & (row_i < 24)).astype(f32).astype(bf16)
            scaling = dot(parts, pick, TT)
            normed[v, i // 2, i % 2] = (local[v, i] * scaling * gain_s[0:1]).astype(bf16)
            return 0

        lax.fori_loop(0, 8, body, 0, unroll=2)
        normed_out[v][0].start()
        normed_out[v][2].start()
        normed_own[v].start()

    def read_out(v):
        carried(v)
        for copy in square_out[v]:
            copy.start()
        if v > 0:
            normed_out[v - 1][1].start()

    states(0)
    hop(0, 0)
    states(1)
    states(2)
    hop(1, 0)
    hop(0, 1)
    inside(0, 0)
    hop(2, 0)
    inside(0, 4)
    hop(0, 2)
    hop(1, 1)
    inside(1, 0)
    inside(1, 4)
    out_across.wait_recv()
    out_relay.start()
    hop(2, 1)
    hop(1, 2)
    hop(0, 3)
    read_out(0)
    inside(2, 0)
    finish(0)
    hop(2, 2)
    hop(1, 3)
    read_out(1)
    inside(2, 4)
    finish(1)
    hop(2, 3)
    read_out(2)
    finish(2)
    normed_out[2][1].start()

    load_head.wait()
    load_out.wait()
    out_core.wait_recv()
    out_relay.wait_recv()

    def hidden(v):
        for copy in normed_out[v]:
            copy.wait_recv()
        normed_own[v].wait()
        for b in range(2):
            full = jnp.concatenate([arrived[s, v, b] for s in range(4)], axis=1)
            total = dot(full, ow[...].reshape(D, D))
            view = (scales[v : v + 1, :] * pall[f, b * 128 : (b + 1) * 128, :].astype(f32)).astype(bf16)
            hid[v, b] = (view.astype(f32) + total).astype(bf16)

    for v in range(VIEWS):
        hidden(v)

    for b in range(2):
        logs = []
        for v in range(VIEWS):
            logits = dot(hid[v, b], head[...])
            shifted = logits - jnp.max(logits, axis=1, keepdims=True)
            logs.append(shifted - jnp.log(jnp.sum(jnp.exp(shifted), axis=1, keepdims=True)))
        top = jnp.maximum(jnp.maximum(logs[0], logs[1]), logs[2])
        mean = top + jnp.log(sum(jnp.exp(log - top) for log in logs)) - jnp.log(f32(VIEWS))
        onehot = (row == label_ref[b : b + 1, :]).astype(f32).T
        spread_sum = jnp.zeros((BLOCK, 1), f32)
        for v in range(VIEWS):
            prob = jnp.exp(logs[v])
            gap = logs[v] - mean
            inner = jnp.sum(prob * gap, axis=1, keepdims=True)
            spread_sum += inner
            grad = (mix_lambda / VIEWS) * prob * (gap - inner)
            if v == 0:
                grad += prob - onehot
            logit[v, b] = (factor * grad).astype(bf16)
        cross = -jnp.sum(onehot * logs[0], axis=1, keepdims=True)
        losses = cross + mix_lambda * (spread_sum / VIEWS)
        loss_ref[b : b + 1, :] = jnp.sum(jnp.where(row == col, losses, 0.0), axis=0, keepdims=True)

    grads = logit[...].reshape(VIEWS * 2 * BLOCK, CLASSES)
    def sum_terms(chip):
        for kk in range(2):
            s = 2 * chip + kk
            for half in range(2):
                lanes = slice(half * LANES, (half + 1) * LANES)
                term = dot(arrived[s, :, :, :, lanes].reshape(VIEWS * 2 * BLOCK, LANES), grads, TT)
                for e in range(2):
                    part[s, 2 * half + e, :, :CLASSES] = term[64 * e : 64 * (e + 1)]
        for m in range(4):
            lanes = pl.ds(pl.multiple_of((2 * m + chip) * LANES, LANES), LANES)
            term = dot(hid[:, :, :, lanes].reshape(VIEWS * 2 * BLOCK, LANES), grads, TT)
            for e in range(2):
                part[2 * chip + e, m, :, CLASSES:] = term[64 * e : 64 * (e + 1)]

    order = [(c + off) % count for off in (2, 3, 1, 0)]
    sum_core = [[remote(part.at[2 * xs + 1 - k, j], got_a.at[n, j], core) for j in order]
                for n, xs in enumerate((1 - xx, xx))]
    sum_terms(1 - xx)
    for copy in sum_core[0]:
        copy.start()
    sum_terms(xx)
    for copy in sum_core[1]:
        copy.start()
    sum_across = []
    for n, j in enumerate(order):
        sum_core[0][n].wait_recv()
        sum_a[0, j] = part[2 * (1 - xx) + k, j] + got_a[0, j]
        copy = remote(sum_a.at[0, j], got_b.at[j], across)
        copy.start()
        sum_across.append(copy)
    sum_ctx = []
    for n, j in enumerate(order):
        sum_core[1][n].wait_recv()
        own = part[2 * xx + k, j] + got_a[1, j]
        sum_across[n].wait_recv()
        sum_a[1, j] = own + got_b[j]
        if n < 3:
            copy = remote(sum_a.at[1, j], got_c.at[n], (g, j, f))
            copy.start()
            sum_ctx.append(copy)
    for copy in sum_ctx:
        copy.wait_recv()
    done = sum_a[1, c]
    for j in range(count - 1):
        done = done + got_c[j]
    sum_ref[...] = done

    sends = [copy for group in first for copy in group] + onward + relays + beside + small
    sends += [patch_core] + patch_across + patch_relay
    sends += [out_across, out_core, out_relay]
    sends += [copy for v in range(VIEWS) for copy in square_out[v] + normed_out[v]]
    sends += sum_core[0] + sum_core[1] + sum_across + sum_ctx
    for copy in sends:
        copy.wait_send()
    for v in range(VIEWS):
        @pl.when(c < count - 1)
        def _():
            for copy in chain[v][0]:
                copy.wait_send()

        @pl.when(c > 0)
        def _():
            for copy in chain[v][1]:
                copy.wait_send()


def close_kernel(sum_ref, head_ref, lost_ref, grad_ref, head_grad_ref, loss_ref):
    head_grad_ref[...] = sum_ref[:, CLASSES:]
    loss_ref[...] = lost_ref[...]
    out = dot(jnp.concatenate(thirds(sum_ref[:, :CLASSES]), axis=0), head_ref[...], NT)
    grad_ref[...] = out[0:64] + out[64:128] + out[128:192]


def fused(patches, labels, op_ids, mix_codes, aug_gains, in_weight, dt_weight, dt_bias,
          decay_log, skip_gain, norm_gain, out_weight, head_weight):
    rows = patches.shape[0]
    ctx_count, shards = lax.axis_size("ctx"), lax.axis_size("fsdp")
    factor = loss_scale / (rows * ctx_count * shards)
    smem = pl.BlockSpec(memory_space=pltpu.SMEM)
    vmem = pl.BlockSpec(memory_space=pltpu.VMEM)
    far = pl.BlockSpec(memory_space=pl.ANY)
    V = pltpu.VMEM
    sums, losses = pl.pallas_call(
        functools.partial(fused_kernel, factor),
        name="fused",
        out_shape=[
            jax.ShapeDtypeStruct((64, 256), f32),
            jax.ShapeDtypeStruct((2, LANES), f32),
        ],
        in_specs=[smem] * 5 + [vmem] * 4 + [far] * 4,
        out_specs=[vmem] * 2,
        scratch_shapes=[
            V((4, 256, 1024), bf16), V((4, 256, 256), bf16), V((4, 256, LANES), bf16),
            V((4, 2 * HEADS, 256), bf16), V((4, 256, D), bf16), V((VIEWS, D), f32),
            V((VIEWS, 8, 128, 256), bf16), V((VIEWS, 8, 128, 512), bf16), V((24, 32, 128), f32),
            V((24, 8, 128), f32), V((24, 8, 128), f32), V((24, 32, 128), bf16), V((24, 32, 128), bf16),
            V((24, 32, 128), bf16), V((56, 512), f32), V((8, 128, 256), f32),
            V((VIEWS, 2, 8, 128, 256), f32), V((VIEWS, 2, 128, 256), f32), V((VIEWS, 2, 128, 256), f32),
            V((VIEWS, 8, 128, 256), f32), V((VIEWS, 8, 128), f32), V((PEERS, VIEWS, 8, 128), f32),
            V((VIEWS, 4, 2, 128, 256), bf16), V((4, VIEWS, 2, 128, 256), bf16),
            V((4, 4, 64, D), bf16), V((D, CLASSES), bf16), V((VIEWS, 2, 128, D), bf16),
            V((VIEWS, 2, 128, CLASSES), bf16), V((4, 4, 64, 256), f32), V((2, 4, 64, 256), f32),
            V((2, 4, 64, 256), f32), V((4, 64, 256), f32), V((3, 64, 256), f32),
            V((32, 512), bf16), V((LANES, 512), bf16), V((32, 1024), bf16), V((128, 256), bf16),
            V((8, 256), f32),
            pltpu.SemaphoreType.DMA((16,)),
            pltpu.SemaphoreType.DMA((96,)), pltpu.SemaphoreType.DMA((96,)),
        ],
        compiler_params=pltpu.CompilerParams(
            collective_id=0, has_side_effects=True, vmem_limit_bytes=56 << 20),
        cost_estimate=pl.CostEstimate(flops=20 << 30, bytes_accessed=8 << 20, transcendentals=0),
    )(op_ids, mix_codes, dt_bias, decay_log, skip_gain[None, :],
      aug_gains, norm_gain.reshape(8, LANES), labels.reshape(2, LANES), dt_weight.T,
      patches, in_weight, out_weight.reshape(4, 64, D), head_weight)
    grad_out, grad_head, losses = pl.pallas_call(
        close_kernel,
        name="close",
        out_shape=[
            jax.ShapeDtypeStruct((64, D), f32),
            jax.ShapeDtypeStruct((64, CLASSES), f32),
            jax.ShapeDtypeStruct((2, LANES), f32),
        ],
    )(sums, head_weight, losses)
    return grad_out, grad_head, losses.reshape(rows)


def solution(mesh):
    sizes = dict(mesh.shape)
    small = sizes["groups"] == 2 and sizes["ctx"] == 4 and sizes["fsdp"] == 4
    return jax.shard_map(
        fused if small else on_device,
        mesh=mesh,
        in_specs=(
            P(("groups", "ctx", "fsdp"), None),
            P(("groups", "ctx", "fsdp")),
            P("groups", None),
            P("groups", None),
            P(),
            P("fsdp", None),
            P("fsdp", None),
            P(),
            P(),
            P(),
            P(),
            P("fsdp", None),
            P(),
        ),
        out_specs=(
            P(("groups", "ctx", "fsdp"), None),
            P(("groups", "ctx", "fsdp"), None),
            P(("groups", "ctx", "fsdp")),
        ),
        check_vma=False,
    )
```

```python
import functools
import jax
import jax.numpy as jnp
from jax import lax
from jax.experimental import pallas as pl
from jax.experimental.pallas import tpu as pltpu
from jax.sharding import PartitionSpec as P

D = 1024
HEADS = 16
HEAD_DIM = 64
STATE = 128
CLASSES = 128
VIEWS = 3
NOPS = 9
WIDTH_AUG = 3
BLOCK = 128
LANES = 128
LOG_ROWS = 8


loss_scale = 256.0
mix_lambda = 12.0
highest = lax.Precision.HIGHEST
f32 = jnp.float32
bf16 = jnp.bfloat16


def view_scales(op_ids, mix_codes, aug_gains):
    code_values = mix_codes.astype(jnp.float32)
    weights = code_values[:, :WIDTH_AUG] / jnp.sum(
        code_values[:, :WIDTH_AUG], axis=1, keepdims=True
    )
    keep_share = code_values[:, WIDTH_AUG] / 9.0
    onehot = (op_ids[:, :, None] == jnp.arange(NOPS, dtype=jnp.int32)[None, None, :]).astype(
        jnp.float32
    )
    op_weights = jnp.sum(onehot * weights[:, :, None], axis=1)
    mixed_gain = jnp.dot(op_weights, aug_gains, precision=highest)
    scaled = keep_share[:, None] + (1.0 - keep_share[:, None]) * mixed_gain
    return jnp.concatenate([jnp.ones((1, D), jnp.float32), scaled], axis=0)


def halves(value):
    high = value.astype(bf16)
    return high, (value - high.astype(f32)).astype(bf16)


def thirds(value):
    high = value.astype(bf16)
    rest = value - high.astype(f32)
    mid = rest.astype(bf16)
    return high, mid, (rest - mid.astype(f32)).astype(bf16)


def dot(a, b, dims=((1,), (0,))):
    return lax.dot_general(a, b, (dims, ((), ())), preferred_element_type=f32)


def spread(columns, first, heads):
    rows = columns.shape[0]
    lane = lax.broadcasted_iota(jnp.int32, (rows, LANES), 1)
    pieces = []
    for h in range(first, first + heads, 2):
        left = jnp.broadcast_to(columns[:, h : h + 1], (rows, LANES))
        right = jnp.broadcast_to(columns[:, h + 1 : h + 2], (rows, LANES))
        pieces.append(jnp.where(lane < HEAD_DIM, left, right))
    return jnp.concatenate(pieces, axis=1) if len(pieces) > 1 else pieces[0]


def project_kernel(place_ref, patches_ref, scale_ref, weight_ref, x_ref, coef_ref, raw_ref):
    width = x_ref.shape[2]
    patches = patches_ref[...].astype(f32)
    for v in range(VIEWS):
        view = (scale_ref[v : v + 1, :] * patches).astype(bf16)
        out = dot(view, weight_ref[...])
        x_ref[v] = out[:, :width].astype(bf16)
        coef_ref[v] = out[:, width : width + 4 * STATE].astype(bf16)
        raw_ref[v] = out[:, width + 4 * STATE :]


def states_kernel(heads, raw_ref, x_ref, coef_ref, bias_ref, rate_ref,
                  final_ref, prefix_ref, steps_ref, run_ref, pos_ref):
    rows, width = x_ref.shape[1:]
    pieces = rows // BLOCK
    row = lax.broadcasted_iota(jnp.int32, (BLOCK, BLOCK), 0)
    col = lax.broadcasted_iota(jnp.int32, (BLOCK, BLOCK), 1)
    lower = (row >= col).astype(f32).astype(bf16)
    upper = (row <= col).astype(f32).astype(bf16)
    is_forward = col < heads

    def first_pass(i, carried):
        state, total = carried
        at = pl.ds(pl.multiple_of(i * BLOCK, BLOCK), BLOCK)
        raw = raw_ref[0, at, :] + bias_ref[...]
        steps = jnp.maximum(raw, 0.0) + jnp.log1p(jnp.exp(-jnp.abs(raw)))
        parts = thirds(steps * rate_ref[...])
        down = sum(dot(lower, part) for part in parts)
        up = sum(dot(upper, part) for part in parts)
        run = jnp.where(is_forward, down, up)
        steps_ref[0, at, :] = steps
        run_ref[0, at, :] = run
        pos_ref[0, at, :] = run + total
        last = jnp.where(is_forward[:1], run[BLOCK - 1 :], run[:1])
        x = x_ref[0, at, :].astype(f32)
        weight = spread(jnp.exp(last - run) * steps, 0, heads)
        high, low = halves(weight * x)
        write = coef_ref[0, at, :STATE]
        fresh = dot(write, high, ((0,), (0,))) + dot(write, low, ((0,), (0,)))
        s_high, s_low = halves(state)
        prefix_ref[0, 0, i, :STATE, :] = s_high
        prefix_ref[0, 0, i, STATE:, :] = s_low
        return spread(jnp.exp(last), 0, heads) * state + fresh, total + last

    zero = jnp.zeros((STATE, width), f32)
    no_log = jnp.zeros((1, LANES), f32)
    state, total = lax.fori_loop(0, pieces, first_pass, (zero, no_log), unroll=4)
    final_ref[0, 0, :STATE, :] = state
    final_ref[0, 0, STATE:, :] = jnp.broadcast_to(spread(total, 0, heads), (LOG_ROWS, width))

    def second_pass(k, carried):
        state, total = carried
        i = pieces - 1 - k
        at = pl.ds(pl.multiple_of(i * BLOCK, BLOCK), BLOCK)
        run = run_ref[0, at, :]
        last = run[:1]
        pos_ref[0, at, :] = jnp.where(is_forward, pos_ref[0, at, :], run + total)
        x = x_ref[0, at, :].astype(f32)
        weight = spread(jnp.exp(last - run) * steps_ref[0, at, :], heads, heads)
        high, low = halves(weight * x)
        write = coef_ref[0, at, 2 * STATE : 3 * STATE]
        fresh = dot(write, high, ((0,), (0,))) + dot(write, low, ((0,), (0,)))
        s_high, s_low = halves(state)
        prefix_ref[0, 1, i, :STATE, :] = s_high
        prefix_ref[0, 1, i, STATE:, :] = s_low
        return spread(jnp.exp(last), heads, heads) * state + fresh, total + last

    state, total = lax.fori_loop(0, pieces, second_pass, (zero, no_log), unroll=4)
    final_ref[0, 1, :STATE, :] = state
    final_ref[0, 1, STATE:, :] = jnp.broadcast_to(spread(total, heads, heads), (LOG_ROWS, width))


def inside_kernel(heads, x_ref, coef_ref, prefix_ref, steps_ref, run_ref, skip_ref, *rest):
    out_ref = rest[-1]
    row = lax.broadcasted_iota(jnp.int32, (BLOCK, BLOCK), 0)
    col = lax.broadcasted_iota(jnp.int32, (BLOCK, BLOCK), 1)
    below, above = row > col, row < col
    x = x_ref[0]
    steps_t = steps_ref[0].T
    run = run_ref[0]
    run_t = run.T
    coef = coef_ref[0]
    write_f, read_f = coef[:, :STATE], coef[:, STATE : 2 * STATE]
    write_r, read_r = coef[:, 2 * STATE : 3 * STATE], coef[:, 3 * STATE :]
    score_f = dot(read_f, write_f, ((1,), (1,)))
    score_r = dot(read_r, write_r, ((1,), (1,)))
    lane = lax.broadcasted_iota(jnp.int32, (BLOCK, LANES), 1)
    zero = jnp.zeros((BLOCK, LANES), bf16)
    pieces = []
    for pair in range(heads // 2):
        highs, lows = [], []
        for h in (2 * pair, 2 * pair + 1):
            r = heads + h
            gap = jnp.where(
                below, run[:, h : h + 1] - run_t[h : h + 1], run[:, r : r + 1] - run_t[r : r + 1]
            )
            gap = jnp.where(row == col, 0.0, gap)
            from_f = score_f * steps_t[h : h + 1]
            from_r = score_r * steps_t[r : r + 1]
            weight = jnp.where(below, from_f, jnp.where(above, from_r, from_f + from_r))
            high, low = halves(weight * jnp.exp(gap))
            highs.append(high)
            lows.append(low)
        values = x[:, pair * LANES : (pair + 1) * LANES]
        stacked = jnp.concatenate(
            [jnp.where(lane < HEAD_DIM, values, zero), jnp.where(lane < HEAD_DIM, zero, values)],
            axis=0,
        )
        pieces.append(
            dot(jnp.concatenate(highs, axis=1), stacked)
            + dot(jnp.concatenate(lows, axis=1), stacked)
        )
    inside = jnp.concatenate(pieces, axis=1) if len(pieces) > 1 else pieces[0]
    grown = jnp.exp(run)
    carried_f = dot(jnp.concatenate([read_f, read_f], axis=1), prefix_ref[0, 0, 0])
    carried_r = dot(jnp.concatenate([read_r, read_r], axis=1), prefix_ref[0, 1, 0])
    out_ref[0] = (
        inside
        + spread(grown, 0, heads) * carried_f
        + spread(grown, heads, heads) * carried_r
        + skip_ref[...] * x.astype(f32)
    )


def incoming_kernel(heads, forward_ref, reverse_ref, coef_ref, pos_ref, local_ref,
                    mixed_ref, square_ref, held):
    width = local_ref.shape[2]

    @pl.when(pl.program_id(1) == 0)
    def _():
        for way, before in enumerate((forward_ref, reverse_ref)):
            high, low = halves(before[0])
            held[way, :STATE, :] = high
            held[way, STATE:, :] = low

    grown = jnp.exp(pos_ref[0])
    coef = coef_ref[0]
    read_f = coef[:, STATE : 2 * STATE]
    read_r = coef[:, 3 * STATE :]
    mixed = (
        local_ref[0]
        + spread(grown, 0, heads) * dot(jnp.concatenate([read_f, read_f], axis=1), held[0])
        + spread(grown, heads, heads) * dot(jnp.concatenate([read_r, read_r], axis=1), held[1])
    )
    mixed_ref[0] = mixed
    ones = jnp.ones((8, width), bf16)
    square_ref[0] = sum(dot(ones, part, ((1,), (1,))) for part in thirds(mixed * mixed))


def tail_kernel(shards, factor, normed_ref, out_w_ref, head_ref, patches_ref, scale_ref,
                label_ref, logit_ref, loss_ref, head_grad_ref, hidden_ref=None):
    rows = patches_ref.shape[0]
    head = head_ref[...]
    patches = patches_ref[...].astype(f32)
    hiddens, logs = [], []
    for v in range(VIEWS):
        total = dot(normed_ref[0, v], out_w_ref[0])
        for s in range(1, shards):
            total += dot(normed_ref[s, v], out_w_ref[s])
        view = (scale_ref[v : v + 1, :] * patches).astype(bf16)
        hidden = (view.astype(f32) + total).astype(bf16)
        hiddens.append(hidden)
        logits = dot(hidden, head)
        shifted = logits - jnp.max(logits, axis=1, keepdims=True)
        logs.append(shifted - jnp.log(jnp.sum(jnp.exp(shifted), axis=1, keepdims=True)))
    top = jnp.maximum(jnp.maximum(logs[0], logs[1]), logs[2])
    mean = top + jnp.log(sum(jnp.exp(log - top) for log in logs)) - jnp.log(f32(VIEWS))
    lane = lax.broadcasted_iota(jnp.int32, (rows, CLASSES), 1)
    onehot = (lane == label_ref[...]).astype(f32)
    spread_sum = jnp.zeros((rows, 1), f32)
    grads = []
    for v in range(VIEWS):
        prob = jnp.exp(logs[v])
        gap = logs[v] - mean
        inner = jnp.sum(prob * gap, axis=1, keepdims=True)
        spread_sum += inner
        grad = (mix_lambda / VIEWS) * prob * (gap - inner)
        if v == 0:
            grad += prob - onehot
        grads.append((factor * grad).astype(bf16))
        logit_ref[v] = grads[v]
    cross = -jnp.sum(onehot * logs[0], axis=1, keepdims=True)
    loss_ref[...] = cross + mix_lambda * (spread_sum / VIEWS)
    update = sum(dot(hiddens[v], grads[v], ((0,), (0,))) for v in range(VIEWS))

    @pl.when(pl.program_id(0) == 0)
    def _():
        head_grad_ref[...] = update

    @pl.when(pl.program_id(0) > 0)
    def _():
        head_grad_ref[...] += update


def grad_kernel(shards, normed_ref, logit_ref, head_ref, out_ref):
    grads = logit_ref[0, 0]
    hidden = dot(grads, head_ref[...], ((1,), (1,))).astype(bf16)
    update = dot(normed_ref[0], hidden, ((0,), (0,)))
    first = (pl.program_id(0) == 0) & (pl.program_id(1) == 0)

    @pl.when(first)
    def _():
        out_ref[...] = update

    @pl.when(jnp.logical_not(first))
    def _():
        out_ref[...] += update


def call(kernel, name, flops, moved, limit=48 << 20, **options):
    return pl.pallas_call(
        kernel,
        name=name,
        compiler_params=pltpu.CompilerParams(vmem_limit_bytes=limit),
        cost_estimate=pl.CostEstimate(flops=flops, bytes_accessed=moved, transcendentals=0),
        **options,
    )


def carried_in(state, decay, axis, reverse):
    count = lax.axis_size(axis)
    if reverse:
        hops = [(j, j - 1) for j in range(1, count)]
    else:
        hops = [(j, j + 1) for j in range(count - 1)]
    sent, got = state, jnp.zeros_like(state)
    for hop in range(count - 1):
        got = lax.ppermute(sent, axis, hops)
        sent = decay * got + state
    return got


def scatter_sum(terms, axes, count):
    blocks = terms.reshape(count, -1, terms.shape[1])
    return jnp.sum(lax.all_to_all(blocks, axes, split_axis=0, concat_axis=0), axis=0)


def on_device(
    patches,
    labels,
    op_ids,
    mix_codes,
    aug_gains,
    in_weight,
    dt_weight,
    dt_bias,
    decay_log,
    skip_gain,
    norm_gain,
    out_weight,
    head_weight,
):
    row_count = patches.shape[0]
    ctx_count = lax.axis_size("ctx")
    shards = lax.axis_size("fsdp")
    place = lax.axis_index("fsdp")
    total_patches = row_count * ctx_count * shards
    inner = out_weight.shape[0] * shards
    heads = HEADS // shards
    width = heads * HEAD_DIM
    rows = row_count * shards
    pieces = rows // BLOCK

    if shards == 4:
        across = lax.ppermute(patches, "fsdp", [(f, f ^ 2) for f in range(shards)])
        beside = lax.ppermute(patches, "fsdp", [(f, f ^ 1) for f in range(shards)])
        corner = lax.ppermute(across, "fsdp", [(f, f ^ 1) for f in range(shards)])
        patches_all = jnp.concatenate([patches, beside, across, corner], axis=0)
        flip = place
    else:
        patches_all = lax.all_gather(patches, "fsdp", axis=0, tiled=True)
        flip = jnp.zeros_like(place)
    columns_in = inner + 4 * STATE
    depth = in_weight.shape[0]
    sent_weight = jnp.concatenate(
        [
            in_weight[:, :inner]
            .reshape(depth, heads, shards, HEAD_DIM)
            .transpose(2, 0, 1, 3)
            .reshape(shards, depth, width),
            jnp.broadcast_to(in_weight[None, :, inner:], (shards, depth, 4 * STATE)),
            dt_weight.reshape(depth, 2 * heads, shards).transpose(2, 0, 1),
            jnp.zeros((shards, depth, LANES - 2 * heads), bf16),
        ],
        axis=2,
    )
    mine_weight = lax.all_to_all(sent_weight, "fsdp", split_axis=0, concat_axis=0)
    mine_weight = mine_weight.reshape(D, width + 5 * STATE)
    scales = view_scales(op_ids, mix_codes, aug_gains)
    tile = min(row_count, 128)
    per = row_count // tile
    placed = lambda s, i, flip_ref: ((s ^ flip_ref[0]) * per + i, 0)
    piece = lambda lanes: pl.BlockSpec((VIEWS, tile, lanes), lambda s, i, _: (0, s * per + i, 0))
    constant = lambda *dims: pl.BlockSpec(dims, lambda *_: (0,) * len(dims))
    x, coef, raw = call(
        project_kernel, "project",
        VIEWS * rows * D * (width + 5 * STATE) * 2, rows * D * 8,
        grid_spec=pltpu.PrefetchScalarGridSpec(
            num_scalar_prefetch=1,
            grid=(shards, per),
            in_specs=[pl.BlockSpec((tile, D), placed), constant(VIEWS, D),
                      constant(D, width + 5 * STATE)],
            out_specs=[piece(width), piece(4 * STATE), piece(LANES)],
        ),
        out_shape=[
            jax.ShapeDtypeStruct((VIEWS, rows, width), bf16),
            jax.ShapeDtypeStruct((VIEWS, rows, 4 * STATE), bf16),
            jax.ShapeDtypeStruct((VIEWS, rows, LANES), f32),
        ],
    )(flip.reshape(1).astype(jnp.int32), patches_all, scales, mine_weight)
    raw, out_later = lax.optimization_barrier((raw, out_weight))
    out_all = lax.all_gather(out_later, "fsdp", axis=0, tiled=True)

    def local_lanes(values):
        picked = lax.dynamic_index_in_dim(values.reshape(2 * heads, shards), place, 1, False)
        return jnp.pad(picked, (0, LANES - 2 * heads))[None, :]

    bias = local_lanes(dt_bias)
    rate = local_lanes(-jnp.exp(decay_log))
    skip = lax.dynamic_index_in_dim(skip_gain.reshape(heads, shards), place, 1, False)
    skip = jnp.repeat(skip, HEAD_DIM)[None, :]
    gain = norm_gain.reshape(heads, shards, HEAD_DIM)
    gain = lax.dynamic_index_in_dim(gain, place, 1, False).reshape(1, width)

    whole = lambda *dims: pl.BlockSpec((1, *dims), lambda v: (v,) + (0,) * len(dims))
    fixed = lambda *dims: pl.BlockSpec(dims, lambda *_: (0,) * len(dims))
    final, prefix, steps, run, pos = call(
        functools.partial(states_kernel, heads), "states",
        VIEWS * rows * STATE * width * 8, VIEWS * rows * 8192,
        grid=(VIEWS,),
        in_specs=[whole(rows, LANES), whole(rows, width), whole(rows, 4 * STATE),
                  fixed(1, LANES), fixed(1, LANES)],
        out_specs=[whole(2, STATE + LOG_ROWS, width), whole(2, pieces, 2 * STATE, width),
                   whole(rows, LANES), whole(rows, LANES), whole(rows, LANES)],
        out_shape=[
            jax.ShapeDtypeStruct((VIEWS, 2, STATE + LOG_ROWS, width), f32),
            jax.ShapeDtypeStruct((VIEWS, 2, pieces, 2 * STATE, width), bf16),
            jax.ShapeDtypeStruct((VIEWS, rows, LANES), f32),
            jax.ShapeDtypeStruct((VIEWS, rows, LANES), f32),
            jax.ShapeDtypeStruct((VIEWS, rows, LANES), f32),
        ],
    )(raw, x, coef, bias, rate)
    decay = jnp.exp(final[:, :, STATE : STATE + 1, :])
    forward_in = carried_in(final[:, 0, :STATE], decay[:, 0], "ctx", False)
    reverse_in = carried_in(final[:, 1, :STATE], decay[:, 1], "ctx", True)

    local = ()
    for v in range(VIEWS):
        at = lambda *dims, v=v: pl.BlockSpec(
            (1, *dims), lambda i: (v, i) + (0,) * (len(dims) - 1)
        )
        local = (call(
            functools.partial(inside_kernel, heads), "inside",
            rows * D * 8192, rows * 8192,
            grid=(pieces,),
            in_specs=[at(BLOCK, width), at(BLOCK, 4 * STATE),
                      pl.BlockSpec((1, 2, 1, 2 * STATE, width), lambda i, v=v: (v, 0, i, 0, 0)),
                      at(BLOCK, LANES), at(BLOCK, LANES), fixed(1, width)]
            + [pl.BlockSpec(memory_space=pl.ANY)] * len(local),
            out_specs=at(BLOCK, width),
            out_shape=jax.ShapeDtypeStruct((VIEWS, rows, width), f32),
            input_output_aliases={6: 0} if local else {},
        )(x, coef, prefix, steps, run, skip, *local),)
    (local,) = local
    block = lambda *dims: pl.BlockSpec((1, *dims), lambda v, i: (v, i) + (0,) * (len(dims) - 1))
    entering = pl.BlockSpec((1, STATE, width), lambda v, i: (v, 0, 0))

    span = min(rows, 512)
    mixed, squares = call(
        functools.partial(incoming_kernel, heads), "incoming",
        VIEWS * rows * STATE * width * 8, VIEWS * rows * 8192,
        grid=(VIEWS, rows // span),
        in_specs=[
            entering, entering,
            block(span, 4 * STATE), block(span, LANES), block(span, width)],
        out_specs=[block(span, width), pl.BlockSpec((1, 8, span), lambda v, i: (v, 0, i))],
        out_shape=[
            jax.ShapeDtypeStruct((VIEWS, rows, width), f32),
            jax.ShapeDtypeStruct((VIEWS, 8, rows), f32),
        ],
        scratch_shapes=[pltpu.VMEM((2, 2 * STATE, width), bf16)],
    )(forward_in, reverse_in, coef, pos, local)

    square_total = jnp.sum(lax.all_gather(squares[:, 0, :], "fsdp"), axis=0)
    scaling = lax.rsqrt(square_total / inner + 1e-05)
    normed = (mixed * scaling[:, :, None] * gain[None]).astype(bf16)
    outgoing = normed.reshape(VIEWS, shards, row_count, width).transpose(1, 0, 2, 3)
    arrived = lax.all_to_all(outgoing, "fsdp", split_axis=0, concat_axis=0)

    out_own = out_all.reshape(heads, shards, HEAD_DIM, D).transpose(1, 0, 2, 3)
    out_own = out_own.reshape(shards, width, D)
    tile = min(row_count, 128)
    grads, losses, head_term = call(
        functools.partial(tail_kernel, shards, loss_scale / total_patches), "tail",
        VIEWS * row_count * D * 3000, 6 << 20,
        grid=(row_count // tile,),
        in_specs=[
            pl.BlockSpec((shards, VIEWS, tile, width), lambda i: (0, 0, i, 0)),
            fixed(shards, width, D), fixed(D, CLASSES),
            pl.BlockSpec((tile, D), lambda i: (i, 0)),
            fixed(VIEWS, D),
            pl.BlockSpec((tile, 1), lambda i: (i, 0))],
        out_specs=[
            pl.BlockSpec((VIEWS, tile, CLASSES), lambda i: (0, i, 0)),
            pl.BlockSpec((tile, 1), lambda i: (i, 0)),
            fixed(D, CLASSES)],
        out_shape=[
            jax.ShapeDtypeStruct((VIEWS, row_count, CLASSES), bf16),
            jax.ShapeDtypeStruct((row_count, 1), f32),
            jax.ShapeDtypeStruct((D, CLASSES), f32),
        ],
    )(arrived, out_own, head_weight, patches, scales, labels[:, None])

    if ctx_count * shards == HEADS:
        grads_all = lax.all_gather(grads, "fsdp")
        grad_rows = call(
            functools.partial(grad_kernel, shards), "grads",
            VIEWS * rows * D * (width + CLASSES) * 2, 8 << 20,
            grid=(VIEWS, shards),
            in_specs=[
                pl.BlockSpec((1, row_count, width), lambda v, s: (v, s, 0)),
                pl.BlockSpec((1, 1, row_count, CLASSES), lambda v, s: (s, v, 0, 0)),
                fixed(D, CLASSES)],
            out_specs=fixed(width, D),
            out_shape=jax.ShapeDtypeStruct((width, D), f32),
        )(normed, grads_all, head_weight)
        grad_out = scatter_sum(grad_rows, "ctx", ctx_count)
    else:
        grad_hidden = lax.dot_general(
            grads, head_weight, (((2,), (1,)), ((), ())), preferred_element_type=f32
        ).astype(bf16)
        grad_rows = lax.dot_general(
            arrived, grad_hidden, (((1, 2), (0, 1)), ((), ())), preferred_element_type=f32
        )
        grad_rows = grad_rows.reshape(shards, heads, HEAD_DIM, D).transpose(1, 0, 2, 3)
        grad_out = lax.psum_scatter(
            grad_rows.reshape(inner, D), ("ctx", "fsdp"), scatter_dimension=0, tiled=True
        )
    grad_head = scatter_sum(head_term, ("ctx", "fsdp"), ctx_count * shards)
    return (grad_out, grad_head, losses[:, 0])


LOG2E = 1.4426950408889634
PEERS = 3
CHUNKS = 4
UNROLL_S = 8
PIECES = 4
UNROLL_I = 4
UNROLL_C = 4


def stack3(value):
    high = value.astype(bf16).astype(f32)
    rest = value - high
    mid = rest.astype(bf16).astype(f32)
    low = rest - mid
    return jnp.concatenate([high, mid, low, jnp.zeros_like(value)], axis=0).astype(bf16)


def side3(value):
    return jnp.concatenate(thirds(value), axis=1)


TT = ((0,), (0,))
NT = ((1,), (1,))


def fused_kernel(factor, ops_hbm, codes_hbm, bias_hbm, decay_hbm, skip_hbm,
                 gains_hbm, norm_hbm, label_hbm, dtw_ref,
                 patches_ref, inw_ref, outw_ref, head_hbm,
                 sum_ref, loss_ref,
                 w, wx, wdt, dts, pall, scales,
                 x_s, coef_s, rawt, steps_s, run_s, weight_p, grown_p, run_p, row_s, fresh_s,
                 prefix, fin, inc,
                 local, sq, sq_in, normed, arrived, ow, head, hid, logit, part, sum_a, got_a, got_b,
                 got_c, spread_s, lane_s, wide_s, cum_s, gain_s,
                 ops_ref, codes_ref, bias_ref, decay_ref, skip_ref, gains_ref, norm_ref, label_ref,
                 loc_sem, send_sem, recv_sem):
    MESH = pl.DeviceIdType.MESH
    g, c, f = lax.axis_index("groups"), lax.axis_index("ctx"), lax.axis_index("fsdp")
    count = lax.axis_size("ctx")
    xx, k = f // 2, f % 2
    f1 = f + 1 - 2 * k
    f2 = f + 2 - 4 * xx
    f3 = f2 + 1 - 2 * k
    core, across, corner, other = (g, c, f1), (g, c, f2), (g, c, f3), (1 - g, c, f)
    used = [0]

    def tile(j, chip):
        return pl.ds(pl.multiple_of((2 * j + chip) * LANES, LANES), LANES)

    def remote(src, dst, to):
        n = used[0]
        used[0] += 1
        return pltpu.make_async_remote_copy(
            src_ref=src, dst_ref=dst, send_sem=send_sem.at[n], recv_sem=recv_sem.at[n],
            device_id=to, device_id_type=MESH)

    local_copies = [
        pltpu.make_async_copy(inw_ref.at[:, tile(j, xx)], w.at[f, :, pl.ds(j * LANES, LANES)],
                              loc_sem.at[8 + j]) for j in range(4)]
    local_copies += [
        pltpu.make_async_copy(inw_ref.at[:, pl.ds(D, 512)], w.at[f, :, pl.ds(512, 512)],
                              loc_sem.at[12]),
        pltpu.make_async_copy(dtw_ref, dts.at[f], loc_sem.at[13])]
    load_own = pltpu.make_async_copy(patches_ref, pall.at[f], loc_sem.at[1])
    load_head = pltpu.make_async_copy(head_hbm, head, loc_sem.at[2])
    load_out = pltpu.make_async_copy(outw_ref, ow.at[:, f], loc_sem.at[3])
    barrier = pltpu.get_barrier_semaphore()
    for to in (core, across, corner, other):
        pl.semaphore_signal(barrier, inc=1, device_id=to, device_id_type=MESH)
    for j in range(1, count):
        pl.semaphore_signal(barrier, inc=1, device_id=(g, (c + j) % count, f), device_id_type=MESH)

    tables = [
        pltpu.make_async_copy(src, dst, loc_sem.at[16 + n])
        for n, (src, dst) in enumerate((
            (ops_hbm, ops_ref), (codes_hbm, codes_ref), (bias_hbm, bias_ref), (decay_hbm, decay_ref),
            (skip_hbm, skip_ref), (gains_hbm, gains_ref), (norm_hbm, norm_ref),
            (label_hbm, label_ref)))]
    for copy in tables + local_copies + [load_own, load_head, load_out]:
        copy.start()
    pl.semaphore_wait(barrier, 3 + count)

    chunk = 128 // CHUNKS

    def span(half, q):
        return pl.ds(pl.multiple_of(half * 128 + q * chunk, chunk), chunk)

    first = []
    for q in range(CHUNKS):
        rows = span(g, q)
        group = [remote(inw_ref.at[rows, tile(j, 1 - xx)], w.at[f, rows, pl.ds(j * LANES, LANES)],
                        across) for j in range(4)]
        group.append(remote(inw_ref.at[rows, pl.ds(D, 512)], w.at[f, rows, pl.ds(512, 512)], across))
        for copy in group:
            copy.start()
        first.append(group)
    beside = [remote(inw_ref.at[:, tile(j, xx)], w.at[f, :, pl.ds(j * LANES, LANES)], core)
              for j in range(4)]
    beside.append(remote(inw_ref.at[:, pl.ds(D, 512)], w.at[f, :, pl.ds(512, 512)], core))
    small = [remote(dtw_ref, dts.at[f], to) for to in (across, corner, core)]
    patch_core = remote(patches_ref, pall.at[f], core)
    for copy in small + beside:
        copy.start()
    patch_core.start()
    patch_across = []
    for b in range(4):
        rows = pl.ds(b * 64, 64)
        patch_across.append(remote(patches_ref.at[rows], pall.at[f, rows], across))

    for copy in tables:
        copy.wait()
    pick_row = lax.broadcasted_iota(jnp.int32, (2 * HEADS, LANES), 0)
    pick_col = lax.broadcasted_iota(jnp.int32, (2 * HEADS, LANES), 1)
    head_at = 16 * ((pick_col // 4) % 2) + 4 * (pick_col % 4) + pick_col // 8
    pick = ((pick_row == head_at) & (pick_col < 32)).astype(f32).astype(bf16)
    half_row = lax.broadcasted_iota(jnp.int32, (512, 256), 0)
    half_col = lax.broadcasted_iota(jnp.int32, (512, 256), 1)
    mine = (half_row == 128 * (half_col // 64) + 64 * k + half_col % 64).astype(f32).astype(bf16)
    row32 = lax.broadcasted_iota(jnp.int32, (32, 512), 0)
    col32 = lax.broadcasted_iota(jnp.int32, (32, 512), 1)
    spread_s[...] = ((row32 % 8 == col32 // 64) & (row32 < 24)).astype(f32).astype(bf16)
    row32 = lax.broadcasted_iota(jnp.int32, (32, 1024), 0)
    col32 = lax.broadcasted_iota(jnp.int32, (32, 1024), 1)
    row_l = lax.broadcasted_iota(jnp.int32, (LANES, 512), 0)
    col_l = lax.broadcasted_iota(jnp.int32, (LANES, 512), 1)
    lane_s[...] = (row_l == col_l // 64).astype(f32).astype(bf16)
    wide_s[...] = ((row32 % 8 == col32 // 128) & (row32 < 24)).astype(f32).astype(bf16)
    row = lax.broadcasted_iota(jnp.int32, (BLOCK, BLOCK), 0)
    col = lax.broadcasted_iota(jnp.int32, (BLOCK, BLOCK), 1)
    cum_s[:, :BLOCK] = (row <= col).astype(f32).astype(bf16)
    cum_s[:, BLOCK:] = (row >= col).astype(f32).astype(bf16)
    scales[0:1, :] = jnp.ones((1, D), f32)
    for j in range(2):
        codes = [jnp.full((1, D), codes_ref[j, i].astype(f32), f32) for i in range(WIDTH_AUG + 1)]
        whole = codes[0] + codes[1] + codes[2]
        shares = [codes[i] / whole for i in range(WIDTH_AUG)]
        keep = codes[WIDTH_AUG] / 9.0
        mixed_gain = jnp.zeros((1, D), f32)
        for n in range(NOPS):
            picked = jnp.zeros((1, D), f32)
            for i in range(WIDTH_AUG):
                picked += shares[i] * jnp.where(ops_ref[j, i] == n, 1.0, 0.0)
            mixed_gain += picked * gains_ref[n : n + 1, :]
        scales[j + 1 : j + 2, :] = keep + (1.0 - keep) * mixed_gain
    line = lax.broadcasted_iota(jnp.int32, (8, LANES), 0)
    bias = jnp.zeros((8, LANES), f32)
    rate = jnp.zeros((8, LANES), f32)
    for d in range(2):
        for j in range(4):
            bias = jnp.where(line == 4 * d + j, bias_ref[d, 4 * j + f], bias)
            rate = jnp.where(line == 4 * d + j, decay_ref[d, 4 * j + f], rate)
    rate = -jnp.exp(rate) * LOG2E
    lane_w = lax.broadcasted_iota(jnp.int32, (8, 256), 1)
    skip = jnp.zeros((8, 256), f32)
    for j in range(4):
        skip = jnp.where(lane_w // HEAD_DIM == j, skip_ref[0, 4 * j + f], skip)
    lane_n = lax.broadcasted_iota(jnp.int32, (8, LANES), 1)
    gain_parts = []
    for half in range(2):
        a = jnp.broadcast_to(norm_ref[pl.ds(4 * half + xx, 1), :], (8, LANES))
        b = jnp.broadcast_to(norm_ref[pl.ds(4 * half + 2 + xx, 1), :], (8, LANES))
        even = jnp.where(lane_n < 64, a, pltpu.roll(b, 64, 1))
        odd = jnp.where(lane_n < 64, pltpu.roll(a, 64, 1), b)
        gain_parts.append(jnp.where(k == 0, even, odd))
    gain_s[...] = jnp.concatenate(gain_parts, axis=1)

    relays, onward = [], []

    def to_core(rows):
        copy = remote(w.at[f2, rows], w.at[f2, rows], core)
        copy.start()
        relays.append(copy)

    def select(src):
        wx[src] = dot(w[src, :, :512], mine).astype(bf16)
        wdt[src] = dot(dts[src], pick, TT).astype(bf16)

    for q in range(CHUNKS):
        for copy in first[q]:
            copy.wait_recv()
        rows = span(g, q)
        copy = remote(w.at[f2, rows], w.at[f2, rows], other)
        copy.start()
        onward.append(copy)
        if q == CHUNKS - 2:
            for copy in patch_across:
                copy.start()
        to_core(rows)
    for copy in local_copies:
        copy.wait()
    for copy in small:
        copy.wait_recv()
    select(f)
    for copy in beside:
        copy.wait_recv()
    select(f1)
    for q in range(CHUNKS):
        onward[q].wait_recv()
        to_core(span(1 - g, q))
    select(f2)
    for copy in relays:
        copy.wait_recv()
    select(f3)
    load_own.wait()

    patch_relay = [
        remote(pall.at[f2, pl.ds(b * 64, 64)], pall.at[f2, pl.ds(b * 64, 64)], core)
        for b in range(4)
    ]
    out_across = remote(outw_ref, ow.at[:, f], across)
    out_core = remote(outw_ref, ow.at[:, f], core)
    out_relay = remote(ow.at[:, f2], ow.at[:, f2], core)

    def project(s, _):
        a = s // 4
        pair = (1 - a) * (s // 2) + a * (2 + s % 2)
        b = (1 - a) * (s % 2) + a * ((s - 4 * a) // 2)
        kb, xb = pair % 2, pair // 2
        src = 2 * (xx + xb - 2 * xx * xb) + (k + kb - 2 * k * kb)

        @pl.when(s == 2)
        def _():
            patch_core.wait_recv()

        for b_static in range(2):
            @pl.when(s == 4 + 2 * b_static)
            def _():
                for n in (2 * b_static, 2 * b_static + 1):
                    patch_across[n].wait_recv()
                    patch_relay[n].start()

            @pl.when(s == 5 + 2 * b_static)
            def _():
                for n in (2 * b_static, 2 * b_static + 1):
                    patch_relay[n].wait_recv()

        rows = pall[src, pl.ds(pl.multiple_of(b * 128, 128), 128), :].astype(f32)
        view = jnp.concatenate(
            [(scales[v : v + 1, :] * rows).astype(bf16) for v in range(VIEWS)], axis=0)
        i = 2 * src + b
        out = dot(view, wx[...].reshape(D, 256)).astype(bf16)
        coef = dot(view, w[:, :, 512:].reshape(D, 512)).astype(bf16)
        raw = dot(view, wdt[...].reshape(D, LANES))
        for v in range(VIEWS):
            at = slice(v * 128, (v + 1) * 128)
            x_s[v, i] = out[at]
            coef_s[v, i] = coef[at]
            rawt[8 * v + i] = raw[at].T[:32]
        return 0

    lax.fori_loop(0, 8, project, 0)
    out_across.start()
    out_core.start()

    def triple(values):
        high = values.astype(bf16).astype(f32)
        rest = values - high
        mid = rest.astype(bf16).astype(f32)
        return high, mid, rest - mid

    def stacked(values):
        return jnp.concatenate([*triple(values), jnp.zeros_like(values)], axis=1).astype(bf16)

    blocks = VIEWS * 8
    raw = rawt[:, pl.ds(pl.multiple_of(8 * f, 8), 8), :] + bias[None]
    steps_all = jnp.maximum(raw, 0.0) + jnp.log1p(jnp.exp(-jnp.abs(raw)))
    logs = jnp.concatenate(triple(steps_all * rate[None]), axis=0).reshape(3 * blocks * 8, BLOCK)
    cum = dot(logs.astype(bf16), cum_s[...]).reshape(3, blocks, 8, 2 * BLOCK)
    cum = cum[0] + cum[1] + cum[2]
    way = lax.broadcasted_iota(jnp.int32, (blocks, 8, BLOCK), 1) < 4
    run_all = jnp.where(way, cum[:, :, :BLOCK], cum[:, :, BLOCK:])
    last_all = jnp.where(way, jnp.broadcast_to(cum[:, :, BLOCK - 1 : BLOCK], way.shape),
                         jnp.broadcast_to(cum[:, :, BLOCK : BLOCK + 1], way.shape))
    steps_s[...] = steps_all
    run_s[...] = run_all
    weight_p[...] = stacked(jnp.exp2(last_all - run_all) * steps_all)
    grown_p[...] = stacked(jnp.exp2(run_all))
    run_p[...] = stacked(run_all)
    totals, before = [], [None] * blocks
    for v in range(VIEWS):
        lasts = [last_all[8 * v + i] for i in range(8)]
        ahead_sum, behind_sum = [jnp.zeros((8, LANES), f32)], [jnp.zeros((8, LANES), f32)]
        for i in range(8):
            ahead_sum.append(ahead_sum[-1] + lasts[i])
            behind_sum.append(behind_sum[-1] + lasts[7 - i])
        for i in range(8):
            before[8 * v + i] = jnp.where(line < 4, ahead_sum[i], behind_sum[7 - i])[None]
        totals.append(jnp.where(line < 4, ahead_sum[8], behind_sum[8])[None])
    pad = [jnp.zeros((8 - VIEWS, 8, LANES), f32)]
    decays = jnp.exp2(jnp.concatenate([last_all] + before + totals + pad, axis=0))
    count_rows = 2 * blocks + 8
    on_lane = (lax.broadcasted_iota(jnp.int32, decays.shape, 1)
               == lax.broadcasted_iota(jnp.int32, decays.shape, 2))
    flat = jnp.sum(jnp.where(on_lane, decays, 0.0), axis=1)
    flat = dot(jnp.concatenate(triple(flat), axis=0).astype(bf16), lane_s[...])
    row_s[...] = flat[:count_rows] + flat[count_rows : 2 * count_rows] + flat[2 * count_rows :]

    def states(v):
        fin[v, 0] = jnp.zeros((STATE, 256), f32)
        fin[v, 1] = jnp.zeros((STATE, 256), f32)

        def forward(i, _):
            n = 8 * v + i
            xf = x_s[v, i].astype(f32)
            weight = dot(weight_p[n], spread_s[...], TT)
            for d in range(2):
                high, low = halves(weight[:, 256 * d : 256 * (d + 1)] * xf)
                write = coef_s[v, i, :, 2 * STATE * d : 2 * STATE * d + STATE].T
                fresh = dot(jnp.concatenate([write, write], axis=1),
                            jnp.concatenate([high, low], axis=0))
                if d == 0:
                    state = fin[v, 0]
                    prefix[v, 0, i] = state
                    fin[v, 0] = row_s[pl.ds(n, 1), :256] * state + fresh
                else:
                    fresh_s[i] = fresh
            return 0

        lax.fori_loop(0, 8, forward, 0, unroll=UNROLL_S)

        def backward(m, _):
            i = 7 - m
            state = fin[v, 1]
            prefix[v, 1, i] = state
            fin[v, 1] = row_s[pl.ds(8 * v + i, 1), 256:] * state + fresh_s[i]
            return 0

        lax.fori_loop(0, 8, backward, 0, unroll=8)

    ahead = (g, (c + 1) % count, f)
    behind = (g, (c + count - 1) % count, f)
    depth = STATE // PIECES
    bands = [pl.ds(n * depth, depth) for n in range(PIECES)]
    chain = [[[remote(fin.at[v, d, band], inc.at[v, d, band], (ahead, behind)[d])
               for band in bands] for d in range(2)] for v in range(VIEWS)]

    def hop(v, n):
        for d in range(2):
            place = c if d == 0 else count - 1 - c

            @pl.when(place == n)
            def _():
                if n == 0:
                    inc[v, d] = jnp.zeros((STATE, 256), f32)
                decay = row_s[2 * blocks + v : 2 * blocks + v + 1, 256 * d : 256 * (d + 1)]
                for copy, at in zip(chain[v][d], bands):
                    if n > 0:
                        copy.wait_recv()
                    if 0 < n < count - 1:
                        fin[v, d, at] = fin[v, d, at] + inc[v, d, at] * decay
                    if n < count - 1:
                        copy.start()

    def inside(v, start):
        def body(i, _):
            x = x_s[v, i]
            n = 8 * v + i
            run, steps = run_s[n], steps_s[n]
            coef = coef_s[v, i]
            score_f = dot(coef[:, STATE : 2 * STATE], coef[:, :STATE], NT)
            score_r = dot(coef[:, 3 * STATE :], coef[:, 2 * STATE : 3 * STATE], NT)
            diagonal = jnp.sum(jnp.where(row == col, score_r, 0.0), axis=0, keepdims=True)
            extra = dot(stack3(steps * diagonal), spread_s[:, 256:], TT)
            wide = dot(run_p[n], wide_s[...], TT)
            keep = row >= col
            lane_b = lax.broadcasted_iota(jnp.int32, (BLOCK, LANES), 1)
            none = jnp.zeros((BLOCK, LANES), bf16)
            pieces = []
            for pair in range(2):
                highs, lows = [], []
                for h in (2 * pair, 2 * pair + 1):
                    r = 4 + h
                    gap = jnp.where(keep, wide[:, h * 128 : (h + 1) * 128] - run[h : h + 1],
                                    wide[:, r * 128 : (r + 1) * 128] - run[r : r + 1])
                    weight = jnp.where(keep, score_f * steps[h : h + 1], score_r * steps[r : r + 1])
                    high, low = halves(weight * jnp.exp2(gap))
                    highs.append(high)
                    lows.append(low)
                values = x[:, pair * LANES : (pair + 1) * LANES]
                left, right = jnp.where(lane_b < 64, values, none), jnp.where(lane_b < 64, none, values)
                pieces.append(dot(jnp.concatenate(highs + lows, axis=1),
                                  jnp.concatenate([left, right, left, right], axis=0)))
            local[v, i] = jnp.concatenate(pieces, axis=1) + (skip[0:1] + extra) * x.astype(f32)
            return 0

        lax.fori_loop(start, start + 4, body, 0, unroll=UNROLL_I)

    def carried(v):
        def body(i, _):
            n = 8 * v + i
            grown = dot(grown_p[n], spread_s[...], TT)
            decay = row_s[pl.ds(blocks + n, 1), :]
            mixed = local[v, i]
            for d in range(2):
                at = slice(256 * d, 256 * (d + 1))
                high, low = halves(prefix[v, d, i] + decay[:, at] * inc[v, d])
                read = coef_s[v, i, :, STATE * (1 + 2 * d) : STATE * (2 + 2 * d)]
                mixed += grown[:, at] * dot(jnp.concatenate([read, read], axis=1),
                                            jnp.concatenate([high, low], axis=0))
            local[v, i] = mixed
            square = mixed * mixed
            square = square[:, :LANES] + square[:, LANES:]
            sums = dot(jnp.ones((8, 3 * LANES), bf16), side3(square), NT)
            sq[v, pl.ds(i, 1), :] = sums[0:1]
            return 0

        lax.fori_loop(0, 8, body, 0, unroll=UNROLL_C)

    square_out = [[remote(sq.at[v], sq_in.at[p, v], to)
                   for p, to in enumerate((core, across, corner))] for v in range(VIEWS)]
    normed_out = [[remote(normed.at[v, fp], arrived.at[f, v], to)
                   for fp, to in ((f3, corner), (f2, across), (f1, core))] for v in range(VIEWS)]
    normed_own = [pltpu.make_async_copy(normed.at[v, f], arrived.at[f, v], loc_sem.at[4 + v])
                  for v in range(VIEWS)]

    def finish(v):
        for copy in square_out[v]:
            copy.wait_recv()
        total = (sq[v] + sq_in[0, v]) + (sq_in[1, v] + sq_in[2, v])
        parts = stack3(lax.rsqrt(total / D + 1e-05))
        row_i = lax.broadcasted_iota(jnp.int32, (32, 256), 0)

        def body(i, _):
            pick = ((row_i % 8 == i) & (row_i < 24)).astype(f32).astype(bf16)
            scaling = dot(parts, pick, TT)
            normed[v, i // 2, i % 2] = (local[v, i] * scaling * gain_s[0:1]).astype(bf16)
            return 0

        lax.fori_loop(0, 8, body, 0, unroll=2)
        normed_out[v][0].start()
        normed_out[v][2].start()
        normed_own[v].start()

    def read_out(v):
        carried(v)
        for copy in square_out[v]:
            copy.start()
        if v > 0:
            normed_out[v - 1][1].start()

    states(0)
    hop(0, 0)
    states(1)
    states(2)
    hop(1, 0)
    hop(0, 1)
    inside(0, 0)
    hop(2, 0)
    inside(0, 4)
    hop(0, 2)
    hop(1, 1)
    inside(1, 0)
    inside(1, 4)
    out_across.wait_recv()
    out_relay.start()
    hop(2, 1)
    hop(1, 2)
    hop(0, 3)
    read_out(0)
    inside(2, 0)
    finish(0)
    hop(2, 2)
    hop(1, 3)
    read_out(1)
    inside(2, 4)
    finish(1)
    hop(2, 3)
    read_out(2)
    finish(2)
    normed_out[2][1].start()

    load_head.wait()
    load_out.wait()
    out_core.wait_recv()
    out_relay.wait_recv()

    def hidden(v):
        for copy in normed_out[v]:
            copy.wait_recv()
        normed_own[v].wait()
        for b in range(2):
            full = jnp.concatenate([arrived[s, v, b] for s in range(4)], axis=1)
            total = dot(full, ow[...].reshape(D, D))
            view = (scales[v : v + 1, :] * pall[f, b * 128 : (b + 1) * 128, :].astype(f32)).astype(bf16)
            hid[v, b] = (view.astype(f32) + total).astype(bf16)

    for v in range(VIEWS):
        hidden(v)

    for b in range(2):
        logs = []
        for v in range(VIEWS):
            logits = dot(hid[v, b], head[...])
            shifted = logits - jnp.max(logits, axis=1, keepdims=True)
            logs.append(shifted - jnp.log(jnp.sum(jnp.exp(shifted), axis=1, keepdims=True)))
        top = jnp.maximum(jnp.maximum(logs[0], logs[1]), logs[2])
        mean = top + jnp.log(sum(jnp.exp(log - top) for log in logs)) - jnp.log(f32(VIEWS))
        onehot = (row == label_ref[b : b + 1, :]).astype(f32).T
        spread_sum = jnp.zeros((BLOCK, 1), f32)
        for v in range(VIEWS):
            prob = jnp.exp(logs[v])
            gap = logs[v] - mean
            inner = jnp.sum(prob * gap, axis=1, keepdims=True)
            spread_sum += inner
            grad = (mix_lambda / VIEWS) * prob * (gap - inner)
            if v == 0:
                grad += prob - onehot
            logit[v, b] = (factor * grad).astype(bf16)
        cross = -jnp.sum(onehot * logs[0], axis=1, keepdims=True)
        losses = cross + mix_lambda * (spread_sum / VIEWS)
        loss_ref[b : b + 1, :] = jnp.sum(jnp.where(row == col, losses, 0.0), axis=0, keepdims=True)

    grads = logit[...].reshape(VIEWS * 2 * BLOCK, CLASSES)
    def sum_terms(chip):
        for kk in range(2):
            s = 2 * chip + kk
            for half in range(2):
                lanes = slice(half * LANES, (half + 1) * LANES)
                term = dot(arrived[s, :, :, :, lanes].reshape(VIEWS * 2 * BLOCK, LANES), grads, TT)
                for e in range(2):
                    part[s, 2 * half + e, :, :CLASSES] = term[64 * e : 64 * (e + 1)]
        for m in range(4):
            lanes = pl.ds(pl.multiple_of((2 * m + chip) * LANES, LANES), LANES)
            term = dot(hid[:, :, :, lanes].reshape(VIEWS * 2 * BLOCK, LANES), grads, TT)
            for e in range(2):
                part[2 * chip + e, m, :, CLASSES:] = term[64 * e : 64 * (e + 1)]

    order = [(c + off) % count for off in (2, 3, 1, 0)]
    sum_core = [[remote(part.at[2 * xs + 1 - k, j], got_a.at[n, j], core) for j in order]
                for n, xs in enumerate((1 - xx, xx))]
    sum_terms(1 - xx)
    for copy in sum_core[0]:
        copy.start()
    sum_terms(xx)
    for copy in sum_core[1]:
        copy.start()
    sum_across = []
    for n, j in enumerate(order):
        sum_core[0][n].wait_recv()
        sum_a[0, j] = part[2 * (1 - xx) + k, j] + got_a[0, j]
        copy = remote(sum_a.at[0, j], got_b.at[j], across)
        copy.start()
        sum_across.append(copy)
    sum_ctx = []
    for n, j in enumerate(order):
        sum_core[1][n].wait_recv()
        own = part[2 * xx + k, j] + got_a[1, j]
        sum_across[n].wait_recv()
        sum_a[1, j] = own + got_b[j]
        if n < 3:
            copy = remote(sum_a.at[1, j], got_c.at[n], (g, j, f))
            copy.start()
            sum_ctx.append(copy)
    for copy in sum_ctx:
        copy.wait_recv()
    done = sum_a[1, c]
    for j in range(count - 1):
        done = done + got_c[j]
    sum_ref[...] = done

    sends = [copy for group in first for copy in group] + onward + relays + beside + small
    sends += [patch_core] + patch_across + patch_relay
    sends += [out_across, out_core, out_relay]
    sends += [copy for v in range(VIEWS) for copy in square_out[v] + normed_out[v]]
    sends += sum_core[0] + sum_core[1] + sum_across + sum_ctx
    for copy in sends:
        copy.wait_send()
    for v in range(VIEWS):
        @pl.when(c < count - 1)
        def _():
            for copy in chain[v][0]:
                copy.wait_send()

        @pl.when(c > 0)
        def _():
            for copy in chain[v][1]:
                copy.wait_send()


def close_kernel(sum_ref, head_ref, lost_ref, grad_ref, head_grad_ref, loss_ref):
    head_grad_ref[...] = sum_ref[:, CLASSES:]
    loss_ref[...] = lost_ref[...]
    out = dot(jnp.concatenate(thirds(sum_ref[:, :CLASSES]), axis=0), head_ref[...], NT)
    grad_ref[...] = out[0:64] + out[64:128] + out[128:192]


def fused(patches, labels, op_ids, mix_codes, aug_gains, in_weight, dt_weight, dt_bias,
          decay_log, skip_gain, norm_gain, out_weight, head_weight):
    rows = patches.shape[0]
    ctx_count, shards = lax.axis_size("ctx"), lax.axis_size("fsdp")
    factor = loss_scale / (rows * ctx_count * shards)
    vmem = pl.BlockSpec(memory_space=pltpu.VMEM)
    far = pl.BlockSpec(memory_space=pl.ANY)
    V = pltpu.VMEM
    sums, losses = pl.pallas_call(
        functools.partial(fused_kernel, factor),
        name="fused",
        out_shape=[
            jax.ShapeDtypeStruct((64, 256), f32),
            jax.ShapeDtypeStruct((2, LANES), f32),
        ],
        in_specs=[far] * 13,
        out_specs=[vmem] * 2,
        scratch_shapes=[
            V((4, 256, 1024), bf16), V((4, 256, 256), bf16), V((4, 256, LANES), bf16),
            V((4, 2 * HEADS, 256), bf16), V((4, 256, D), bf16), V((VIEWS, D), f32),
            V((VIEWS, 8, 128, 256), bf16), V((VIEWS, 8, 128, 512), bf16), V((24, 32, 128), f32),
            V((24, 8, 128), f32), V((24, 8, 128), f32), V((24, 32, 128), bf16), V((24, 32, 128), bf16),
            V((24, 32, 128), bf16), V((56, 512), f32), V((8, 128, 256), f32),
            V((VIEWS, 2, 8, 128, 256), f32), V((VIEWS, 2, 128, 256), f32), V((VIEWS, 2, 128, 256), f32),
            V((VIEWS, 8, 128, 256), f32), V((VIEWS, 8, 128), f32), V((PEERS, VIEWS, 8, 128), f32),
            V((VIEWS, 4, 2, 128, 256), bf16), V((4, VIEWS, 2, 128, 256), bf16),
            V((4, 4, 64, D), bf16), V((D, CLASSES), bf16), V((VIEWS, 2, 128, D), bf16),
            V((VIEWS, 2, 128, CLASSES), bf16), V((4, 4, 64, 256), f32), V((2, 4, 64, 256), f32),
            V((2, 4, 64, 256), f32), V((4, 64, 256), f32), V((3, 64, 256), f32),
            V((32, 512), bf16), V((LANES, 512), bf16), V((32, 1024), bf16), V((128, 256), bf16),
            V((8, 256), f32),
            pltpu.SMEM((2, WIDTH_AUG), jnp.int32), pltpu.SMEM((2, WIDTH_AUG + 1), jnp.int32),
            pltpu.SMEM((2, HEADS), f32), pltpu.SMEM((2, HEADS), f32), pltpu.SMEM((1, HEADS), f32),
            V((NOPS, D), f32), V((8, LANES), f32), V((2, LANES), jnp.int32),
            pltpu.SemaphoreType.DMA((24,)),
            pltpu.SemaphoreType.DMA((112,)), pltpu.SemaphoreType.DMA((112,)),
        ],
        compiler_params=pltpu.CompilerParams(
            collective_id=0, has_side_effects=True, vmem_limit_bytes=56 << 20),
        cost_estimate=pl.CostEstimate(flops=20 << 30, bytes_accessed=8 << 20, transcendentals=0),
    )(op_ids, mix_codes, dt_bias, decay_log, skip_gain[None, :],
      aug_gains, norm_gain.reshape(8, LANES), labels.reshape(2, LANES), dt_weight.T,
      patches, in_weight, out_weight.reshape(4, 64, D), head_weight)
    grad_out, grad_head, losses = pl.pallas_call(
        close_kernel,
        name="close",
        out_shape=[
            jax.ShapeDtypeStruct((64, D), f32),
            jax.ShapeDtypeStruct((64, CLASSES), f32),
            jax.ShapeDtypeStruct((2, LANES), f32),
        ],
    )(sums, head_weight, losses)
    return grad_out, grad_head, losses.reshape(rows)


def solution(mesh):
    sizes = dict(mesh.shape)
    small = sizes["groups"] == 2 and sizes["ctx"] == 4 and sizes["fsdp"] == 4
    return jax.shard_map(
        fused if small else on_device,
        mesh=mesh,
        in_specs=(
            P(("groups", "ctx", "fsdp"), None),
            P(("groups", "ctx", "fsdp")),
            P("groups", None),
            P("groups", None),
            P(),
            P("fsdp", None),
            P("fsdp", None),
            P(),
            P(),
            P(),
            P(),
            P("fsdp", None),
            P(),
        ),
        out_specs=(
            P(("groups", "ctx", "fsdp"), None),
            P(("groups", "ctx", "fsdp"), None),
            P(("groups", "ctx", "fsdp")),
        ),
        check_vma=False,
    )
```

```python
import functools
import jax
import jax.numpy as jnp
from jax import lax
from jax.experimental import pallas as pl
from jax.experimental.pallas import tpu as pltpu
from jax.sharding import PartitionSpec as P

D = 1024
HEADS = 16
HEAD_DIM = 64
STATE = 128
CLASSES = 128
VIEWS = 3
NOPS = 9
WIDTH_AUG = 3
BLOCK = 128
LANES = 128
LOG_ROWS = 8


loss_scale = 256.0
mix_lambda = 12.0
highest = lax.Precision.HIGHEST
f32 = jnp.float32
bf16 = jnp.bfloat16


def view_scales(op_ids, mix_codes, aug_gains):
    code_values = mix_codes.astype(jnp.float32)
    weights = code_values[:, :WIDTH_AUG] / jnp.sum(
        code_values[:, :WIDTH_AUG], axis=1, keepdims=True
    )
    keep_share = code_values[:, WIDTH_AUG] / 9.0
    onehot = (op_ids[:, :, None] == jnp.arange(NOPS, dtype=jnp.int32)[None, None, :]).astype(
        jnp.float32
    )
    op_weights = jnp.sum(onehot * weights[:, :, None], axis=1)
    mixed_gain = jnp.dot(op_weights, aug_gains, precision=highest)
    scaled = keep_share[:, None] + (1.0 - keep_share[:, None]) * mixed_gain
    return jnp.concatenate([jnp.ones((1, D), jnp.float32), scaled], axis=0)


def halves(value):
    high = value.astype(bf16)
    return high, (value - high.astype(f32)).astype(bf16)


def thirds(value):
    high = value.astype(bf16)
    rest = value - high.astype(f32)
    mid = rest.astype(bf16)
    return high, mid, (rest - mid.astype(f32)).astype(bf16)


def dot(a, b, dims=((1,), (0,))):
    return lax.dot_general(a, b, (dims, ((), ())), preferred_element_type=f32)


def spread(columns, first, heads):
    rows = columns.shape[0]
    lane = lax.broadcasted_iota(jnp.int32, (rows, LANES), 1)
    pieces = []
    for h in range(first, first + heads, 2):
        left = jnp.broadcast_to(columns[:, h : h + 1], (rows, LANES))
        right = jnp.broadcast_to(columns[:, h + 1 : h + 2], (rows, LANES))
        pieces.append(jnp.where(lane < HEAD_DIM, left, right))
    return jnp.concatenate(pieces, axis=1) if len(pieces) > 1 else pieces[0]


def project_kernel(place_ref, patches_ref, scale_ref, weight_ref, x_ref, coef_ref, raw_ref):
    width = x_ref.shape[2]
    patches = patches_ref[...].astype(f32)
    for v in range(VIEWS):
        view = (scale_ref[v : v + 1, :] * patches).astype(bf16)
        out = dot(view, weight_ref[...])
        x_ref[v] = out[:, :width].astype(bf16)
        coef_ref[v] = out[:, width : width + 4 * STATE].astype(bf16)
        raw_ref[v] = out[:, width + 4 * STATE :]


def states_kernel(heads, raw_ref, x_ref, coef_ref, bias_ref, rate_ref,
                  final_ref, prefix_ref, steps_ref, run_ref, pos_ref):
    rows, width = x_ref.shape[1:]
    pieces = rows // BLOCK
    row = lax.broadcasted_iota(jnp.int32, (BLOCK, BLOCK), 0)
    col = lax.broadcasted_iota(jnp.int32, (BLOCK, BLOCK), 1)
    lower = (row >= col).astype(f32).astype(bf16)
    upper = (row <= col).astype(f32).astype(bf16)
    is_forward = col < heads

    def first_pass(i, carried):
        state, total = carried
        at = pl.ds(pl.multiple_of(i * BLOCK, BLOCK), BLOCK)
        raw = raw_ref[0, at, :] + bias_ref[...]
        steps = jnp.maximum(raw, 0.0) + jnp.log1p(jnp.exp(-jnp.abs(raw)))
        parts = thirds(steps * rate_ref[...])
        down = sum(dot(lower, part) for part in parts)
        up = sum(dot(upper, part) for part in parts)
        run = jnp.where(is_forward, down, up)
        steps_ref[0, at, :] = steps
        run_ref[0, at, :] = run
        pos_ref[0, at, :] = run + total
        last = jnp.where(is_forward[:1], run[BLOCK - 1 :], run[:1])
        x = x_ref[0, at, :].astype(f32)
        weight = spread(jnp.exp(last - run) * steps, 0, heads)
        high, low = halves(weight * x)
        write = coef_ref[0, at, :STATE]
        fresh = dot(write, high, ((0,), (0,))) + dot(write, low, ((0,), (0,)))
        s_high, s_low = halves(state)
        prefix_ref[0, 0, i, :STATE, :] = s_high
        prefix_ref[0, 0, i, STATE:, :] = s_low
        return spread(jnp.exp(last), 0, heads) * state + fresh, total + last

    zero = jnp.zeros((STATE, width), f32)
    no_log = jnp.zeros((1, LANES), f32)
    state, total = lax.fori_loop(0, pieces, first_pass, (zero, no_log), unroll=4)
    final_ref[0, 0, :STATE, :] = state
    final_ref[0, 0, STATE:, :] = jnp.broadcast_to(spread(total, 0, heads), (LOG_ROWS, width))

    def second_pass(k, carried):
        state, total = carried
        i = pieces - 1 - k
        at = pl.ds(pl.multiple_of(i * BLOCK, BLOCK), BLOCK)
        run = run_ref[0, at, :]
        last = run[:1]
        pos_ref[0, at, :] = jnp.where(is_forward, pos_ref[0, at, :], run + total)
        x = x_ref[0, at, :].astype(f32)
        weight = spread(jnp.exp(last - run) * steps_ref[0, at, :], heads, heads)
        high, low = halves(weight * x)
        write = coef_ref[0, at, 2 * STATE : 3 * STATE]
        fresh = dot(write, high, ((0,), (0,))) + dot(write, low, ((0,), (0,)))
        s_high, s_low = halves(state)
        prefix_ref[0, 1, i, :STATE, :] = s_high
        prefix_ref[0, 1, i, STATE:, :] = s_low
        return spread(jnp.exp(last), heads, heads) * state + fresh, total + last

    state, total = lax.fori_loop(0, pieces, second_pass, (zero, no_log), unroll=4)
    final_ref[0, 1, :STATE, :] = state
    final_ref[0, 1, STATE:, :] = jnp.broadcast_to(spread(total, heads, heads), (LOG_ROWS, width))


def inside_kernel(heads, x_ref, coef_ref, prefix_ref, steps_ref, run_ref, skip_ref, *rest):
    out_ref = rest[-1]
    row = lax.broadcasted_iota(jnp.int32, (BLOCK, BLOCK), 0)
    col = lax.broadcasted_iota(jnp.int32, (BLOCK, BLOCK), 1)
    below, above = row > col, row < col
    x = x_ref[0]
    steps_t = steps_ref[0].T
    run = run_ref[0]
    run_t = run.T
    coef = coef_ref[0]
    write_f, read_f = coef[:, :STATE], coef[:, STATE : 2 * STATE]
    write_r, read_r = coef[:, 2 * STATE : 3 * STATE], coef[:, 3 * STATE :]
    score_f = dot(read_f, write_f, ((1,), (1,)))
    score_r = dot(read_r, write_r, ((1,), (1,)))
    lane = lax.broadcasted_iota(jnp.int32, (BLOCK, LANES), 1)
    zero = jnp.zeros((BLOCK, LANES), bf16)
    pieces = []
    for pair in range(heads // 2):
        highs, lows = [], []
        for h in (2 * pair, 2 * pair + 1):
            r = heads + h
            gap = jnp.where(
                below, run[:, h : h + 1] - run_t[h : h + 1], run[:, r : r + 1] - run_t[r : r + 1]
            )
            gap = jnp.where(row == col, 0.0, gap)
            from_f = score_f * steps_t[h : h + 1]
            from_r = score_r * steps_t[r : r + 1]
            weight = jnp.where(below, from_f, jnp.where(above, from_r, from_f + from_r))
            high, low = halves(weight * jnp.exp(gap))
            highs.append(high)
            lows.append(low)
        values = x[:, pair * LANES : (pair + 1) * LANES]
        stacked = jnp.concatenate(
            [jnp.where(lane < HEAD_DIM, values, zero), jnp.where(lane < HEAD_DIM, zero, values)],
            axis=0,
        )
        pieces.append(
            dot(jnp.concatenate(highs, axis=1), stacked)
            + dot(jnp.concatenate(lows, axis=1), stacked)
        )
    inside = jnp.concatenate(pieces, axis=1) if len(pieces) > 1 else pieces[0]
    grown = jnp.exp(run)
    carried_f = dot(jnp.concatenate([read_f, read_f], axis=1), prefix_ref[0, 0, 0])
    carried_r = dot(jnp.concatenate([read_r, read_r], axis=1), prefix_ref[0, 1, 0])
    out_ref[0] = (
        inside
        + spread(grown, 0, heads) * carried_f
        + spread(grown, heads, heads) * carried_r
        + skip_ref[...] * x.astype(f32)
    )


def incoming_kernel(heads, forward_ref, reverse_ref, coef_ref, pos_ref, local_ref,
                    mixed_ref, square_ref, held):
    width = local_ref.shape[2]

    @pl.when(pl.program_id(1) == 0)
    def _():
        for way, before in enumerate((forward_ref, reverse_ref)):
            high, low = halves(before[0])
            held[way, :STATE, :] = high
            held[way, STATE:, :] = low

    grown = jnp.exp(pos_ref[0])
    coef = coef_ref[0]
    read_f = coef[:, STATE : 2 * STATE]
    read_r = coef[:, 3 * STATE :]
    mixed = (
        local_ref[0]
        + spread(grown, 0, heads) * dot(jnp.concatenate([read_f, read_f], axis=1), held[0])
        + spread(grown, heads, heads) * dot(jnp.concatenate([read_r, read_r], axis=1), held[1])
    )
    mixed_ref[0] = mixed
    ones = jnp.ones((8, width), bf16)
    square_ref[0] = sum(dot(ones, part, ((1,), (1,))) for part in thirds(mixed * mixed))


def tail_kernel(shards, factor, normed_ref, out_w_ref, head_ref, patches_ref, scale_ref,
                label_ref, logit_ref, loss_ref, head_grad_ref, hidden_ref=None):
    rows = patches_ref.shape[0]
    head = head_ref[...]
    patches = patches_ref[...].astype(f32)
    hiddens, logs = [], []
    for v in range(VIEWS):
        total = dot(normed_ref[0, v], out_w_ref[0])
        for s in range(1, shards):
            total += dot(normed_ref[s, v], out_w_ref[s])
        view = (scale_ref[v : v + 1, :] * patches).astype(bf16)
        hidden = (view.astype(f32) + total).astype(bf16)
        hiddens.append(hidden)
        logits = dot(hidden, head)
        shifted = logits - jnp.max(logits, axis=1, keepdims=True)
        logs.append(shifted - jnp.log(jnp.sum(jnp.exp(shifted), axis=1, keepdims=True)))
    top = jnp.maximum(jnp.maximum(logs[0], logs[1]), logs[2])
    mean = top + jnp.log(sum(jnp.exp(log - top) for log in logs)) - jnp.log(f32(VIEWS))
    lane = lax.broadcasted_iota(jnp.int32, (rows, CLASSES), 1)
    onehot = (lane == label_ref[...]).astype(f32)
    spread_sum = jnp.zeros((rows, 1), f32)
    grads = []
    for v in range(VIEWS):
        prob = jnp.exp(logs[v])
        gap = logs[v] - mean
        inner = jnp.sum(prob * gap, axis=1, keepdims=True)
        spread_sum += inner
        grad = (mix_lambda / VIEWS) * prob * (gap - inner)
        if v == 0:
            grad += prob - onehot
        grads.append((factor * grad).astype(bf16))
        logit_ref[v] = grads[v]
    cross = -jnp.sum(onehot * logs[0], axis=1, keepdims=True)
    loss_ref[...] = cross + mix_lambda * (spread_sum / VIEWS)
    update = sum(dot(hiddens[v], grads[v], ((0,), (0,))) for v in range(VIEWS))

    @pl.when(pl.program_id(0) == 0)
    def _():
        head_grad_ref[...] = update

    @pl.when(pl.program_id(0) > 0)
    def _():
        head_grad_ref[...] += update


def grad_kernel(shards, normed_ref, logit_ref, head_ref, out_ref):
    grads = logit_ref[0, 0]
    hidden = dot(grads, head_ref[...], ((1,), (1,))).astype(bf16)
    update = dot(normed_ref[0], hidden, ((0,), (0,)))
    first = (pl.program_id(0) == 0) & (pl.program_id(1) == 0)

    @pl.when(first)
    def _():
        out_ref[...] = update

    @pl.when(jnp.logical_not(first))
    def _():
        out_ref[...] += update


def call(kernel, name, flops, moved, limit=48 << 20, **options):
    return pl.pallas_call(
        kernel,
        name=name,
        compiler_params=pltpu.CompilerParams(vmem_limit_bytes=limit),
        cost_estimate=pl.CostEstimate(flops=flops, bytes_accessed=moved, transcendentals=0),
        **options,
    )


def carried_in(state, decay, axis, reverse):
    count = lax.axis_size(axis)
    if reverse:
        hops = [(j, j - 1) for j in range(1, count)]
    else:
        hops = [(j, j + 1) for j in range(count - 1)]
    sent, got = state, jnp.zeros_like(state)
    for hop in range(count - 1):
        got = lax.ppermute(sent, axis, hops)
        sent = decay * got + state
    return got


def scatter_sum(terms, axes, count):
    blocks = terms.reshape(count, -1, terms.shape[1])
    return jnp.sum(lax.all_to_all(blocks, axes, split_axis=0, concat_axis=0), axis=0)


def on_device(
    patches,
    labels,
    op_ids,
    mix_codes,
    aug_gains,
    in_weight,
    dt_weight,
    dt_bias,
    decay_log,
    skip_gain,
    norm_gain,
    out_weight,
    head_weight,
):
    row_count = patches.shape[0]
    ctx_count = lax.axis_size("ctx")
    shards = lax.axis_size("fsdp")
    place = lax.axis_index("fsdp")
    total_patches = row_count * ctx_count * shards
    inner = out_weight.shape[0] * shards
    heads = HEADS // shards
    width = heads * HEAD_DIM
    rows = row_count * shards
    pieces = rows // BLOCK

    if shards == 4:
        across = lax.ppermute(patches, "fsdp", [(f, f ^ 2) for f in range(shards)])
        beside = lax.ppermute(patches, "fsdp", [(f, f ^ 1) for f in range(shards)])
        corner = lax.ppermute(across, "fsdp", [(f, f ^ 1) for f in range(shards)])
        patches_all = jnp.concatenate([patches, beside, across, corner], axis=0)
        flip = place
    else:
        patches_all = lax.all_gather(patches, "fsdp", axis=0, tiled=True)
        flip = jnp.zeros_like(place)
    columns_in = inner + 4 * STATE
    depth = in_weight.shape[0]
    sent_weight = jnp.concatenate(
        [
            in_weight[:, :inner]
            .reshape(depth, heads, shards, HEAD_DIM)
            .transpose(2, 0, 1, 3)
            .reshape(shards, depth, width),
            jnp.broadcast_to(in_weight[None, :, inner:], (shards, depth, 4 * STATE)),
            dt_weight.reshape(depth, 2 * heads, shards).transpose(2, 0, 1),
            jnp.zeros((shards, depth, LANES - 2 * heads), bf16),
        ],
        axis=2,
    )
    mine_weight = lax.all_to_all(sent_weight, "fsdp", split_axis=0, concat_axis=0)
    mine_weight = mine_weight.reshape(D, width + 5 * STATE)
    scales = view_scales(op_ids, mix_codes, aug_gains)
    tile = min(row_count, 128)
    per = row_count // tile
    placed = lambda s, i, flip_ref: ((s ^ flip_ref[0]) * per + i, 0)
    piece = lambda lanes: pl.BlockSpec((VIEWS, tile, lanes), lambda s, i, _: (0, s * per + i, 0))
    constant = lambda *dims: pl.BlockSpec(dims, lambda *_: (0,) * len(dims))
    x, coef, raw = call(
        project_kernel, "project",
        VIEWS * rows * D * (width + 5 * STATE) * 2, rows * D * 8,
        grid_spec=pltpu.PrefetchScalarGridSpec(
            num_scalar_prefetch=1,
            grid=(shards, per),
            in_specs=[pl.BlockSpec((tile, D), placed), constant(VIEWS, D),
                      constant(D, width + 5 * STATE)],
            out_specs=[piece(width), piece(4 * STATE), piece(LANES)],
        ),
        out_shape=[
            jax.ShapeDtypeStruct((VIEWS, rows, width), bf16),
            jax.ShapeDtypeStruct((VIEWS, rows, 4 * STATE), bf16),
            jax.ShapeDtypeStruct((VIEWS, rows, LANES), f32),
        ],
    )(flip.reshape(1).astype(jnp.int32), patches_all, scales, mine_weight)
    raw, out_later = lax.optimization_barrier((raw, out_weight))
    out_all = lax.all_gather(out_later, "fsdp", axis=0, tiled=True)

    def local_lanes(values):
        picked = lax.dynamic_index_in_dim(values.reshape(2 * heads, shards), place, 1, False)
        return jnp.pad(picked, (0, LANES - 2 * heads))[None, :]

    bias = local_lanes(dt_bias)
    rate = local_lanes(-jnp.exp(decay_log))
    skip = lax.dynamic_index_in_dim(skip_gain.reshape(heads, shards), place, 1, False)
    skip = jnp.repeat(skip, HEAD_DIM)[None, :]
    gain = norm_gain.reshape(heads, shards, HEAD_DIM)
    gain = lax.dynamic_index_in_dim(gain, place, 1, False).reshape(1, width)

    whole = lambda *dims: pl.BlockSpec((1, *dims), lambda v: (v,) + (0,) * len(dims))
    fixed = lambda *dims: pl.BlockSpec(dims, lambda *_: (0,) * len(dims))
    final, prefix, steps, run, pos = call(
        functools.partial(states_kernel, heads), "states",
        VIEWS * rows * STATE * width * 8, VIEWS * rows * 8192,
        grid=(VIEWS,),
        in_specs=[whole(rows, LANES), whole(rows, width), whole(rows, 4 * STATE),
                  fixed(1, LANES), fixed(1, LANES)],
        out_specs=[whole(2, STATE + LOG_ROWS, width), whole(2, pieces, 2 * STATE, width),
                   whole(rows, LANES), whole(rows, LANES), whole(rows, LANES)],
        out_shape=[
            jax.ShapeDtypeStruct((VIEWS, 2, STATE + LOG_ROWS, width), f32),
            jax.ShapeDtypeStruct((VIEWS, 2, pieces, 2 * STATE, width), bf16),
            jax.ShapeDtypeStruct((VIEWS, rows, LANES), f32),
            jax.ShapeDtypeStruct((VIEWS, rows, LANES), f32),
            jax.ShapeDtypeStruct((VIEWS, rows, LANES), f32),
        ],
    )(raw, x, coef, bias, rate)
    decay = jnp.exp(final[:, :, STATE : STATE + 1, :])
    forward_in = carried_in(final[:, 0, :STATE], decay[:, 0], "ctx", False)
    reverse_in = carried_in(final[:, 1, :STATE], decay[:, 1], "ctx", True)

    local = ()
    for v in range(VIEWS):
        at = lambda *dims, v=v: pl.BlockSpec(
            (1, *dims), lambda i: (v, i) + (0,) * (len(dims) - 1)
        )
        local = (call(
            functools.partial(inside_kernel, heads), "inside",
            rows * D * 8192, rows * 8192,
            grid=(pieces,),
            in_specs=[at(BLOCK, width), at(BLOCK, 4 * STATE),
                      pl.BlockSpec((1, 2, 1, 2 * STATE, width), lambda i, v=v: (v, 0, i, 0, 0)),
                      at(BLOCK, LANES), at(BLOCK, LANES), fixed(1, width)]
            + [pl.BlockSpec(memory_space=pl.ANY)] * len(local),
            out_specs=at(BLOCK, width),
            out_shape=jax.ShapeDtypeStruct((VIEWS, rows, width), f32),
            input_output_aliases={6: 0} if local else {},
        )(x, coef, prefix, steps, run, skip, *local),)
    (local,) = local
    block = lambda *dims: pl.BlockSpec((1, *dims), lambda v, i: (v, i) + (0,) * (len(dims) - 1))
    entering = pl.BlockSpec((1, STATE, width), lambda v, i: (v, 0, 0))

    span = min(rows, 512)
    mixed, squares = call(
        functools.partial(incoming_kernel, heads), "incoming",
        VIEWS * rows * STATE * width * 8, VIEWS * rows * 8192,
        grid=(VIEWS, rows // span),
        in_specs=[
            entering, entering,
            block(span, 4 * STATE), block(span, LANES), block(span, width)],
        out_specs=[block(span, width), pl.BlockSpec((1, 8, span), lambda v, i: (v, 0, i))],
        out_shape=[
            jax.ShapeDtypeStruct((VIEWS, rows, width), f32),
            jax.ShapeDtypeStruct((VIEWS, 8, rows), f32),
        ],
        scratch_shapes=[pltpu.VMEM((2, 2 * STATE, width), bf16)],
    )(forward_in, reverse_in, coef, pos, local)

    square_total = jnp.sum(lax.all_gather(squares[:, 0, :], "fsdp"), axis=0)
    scaling = lax.rsqrt(square_total / inner + 1e-05)
    normed = (mixed * scaling[:, :, None] * gain[None]).astype(bf16)
    outgoing = normed.reshape(VIEWS, shards, row_count, width).transpose(1, 0, 2, 3)
    arrived = lax.all_to_all(outgoing, "fsdp", split_axis=0, concat_axis=0)

    out_own = out_all.reshape(heads, shards, HEAD_DIM, D).transpose(1, 0, 2, 3)
    out_own = out_own.reshape(shards, width, D)
    tile = min(row_count, 128)
    grads, losses, head_term = call(
        functools.partial(tail_kernel, shards, loss_scale / total_patches), "tail",
        VIEWS * row_count * D * 3000, 6 << 20,
        grid=(row_count // tile,),
        in_specs=[
            pl.BlockSpec((shards, VIEWS, tile, width), lambda i: (0, 0, i, 0)),
            fixed(shards, width, D), fixed(D, CLASSES),
            pl.BlockSpec((tile, D), lambda i: (i, 0)),
            fixed(VIEWS, D),
            pl.BlockSpec((tile, 1), lambda i: (i, 0))],
        out_specs=[
            pl.BlockSpec((VIEWS, tile, CLASSES), lambda i: (0, i, 0)),
            pl.BlockSpec((tile, 1), lambda i: (i, 0)),
            fixed(D, CLASSES)],
        out_shape=[
            jax.ShapeDtypeStruct((VIEWS, row_count, CLASSES), bf16),
            jax.ShapeDtypeStruct((row_count, 1), f32),
            jax.ShapeDtypeStruct((D, CLASSES), f32),
        ],
    )(arrived, out_own, head_weight, patches, scales, labels[:, None])

    if ctx_count * shards == HEADS:
        grads_all = lax.all_gather(grads, "fsdp")
        grad_rows = call(
            functools.partial(grad_kernel, shards), "grads",
            VIEWS * rows * D * (width + CLASSES) * 2, 8 << 20,
            grid=(VIEWS, shards),
            in_specs=[
                pl.BlockSpec((1, row_count, width), lambda v, s: (v, s, 0)),
                pl.BlockSpec((1, 1, row_count, CLASSES), lambda v, s: (s, v, 0, 0)),
                fixed(D, CLASSES)],
            out_specs=fixed(width, D),
            out_shape=jax.ShapeDtypeStruct((width, D), f32),
        )(normed, grads_all, head_weight)
        grad_out = scatter_sum(grad_rows, "ctx", ctx_count)
    else:
        grad_hidden = lax.dot_general(
            grads, head_weight, (((2,), (1,)), ((), ())), preferred_element_type=f32
        ).astype(bf16)
        grad_rows = lax.dot_general(
            arrived, grad_hidden, (((1, 2), (0, 1)), ((), ())), preferred_element_type=f32
        )
        grad_rows = grad_rows.reshape(shards, heads, HEAD_DIM, D).transpose(1, 0, 2, 3)
        grad_out = lax.psum_scatter(
            grad_rows.reshape(inner, D), ("ctx", "fsdp"), scatter_dimension=0, tiled=True
        )
    grad_head = scatter_sum(head_term, ("ctx", "fsdp"), ctx_count * shards)
    return (grad_out, grad_head, losses[:, 0])


LOG2E = 1.4426950408889634
PEERS = 3
CHUNKS = 2
UNROLL_S = 8
PIECES = 4
UNROLL_I = 4
UNROLL_C = 4


def stack3(value):
    high = value.astype(bf16).astype(f32)
    rest = value - high
    mid = rest.astype(bf16).astype(f32)
    low = rest - mid
    return jnp.concatenate([high, mid, low, jnp.zeros_like(value)], axis=0).astype(bf16)


def side3(value):
    return jnp.concatenate(thirds(value), axis=1)


TT = ((0,), (0,))
NT = ((1,), (1,))


def fused_kernel(factor, ops_hbm, codes_hbm, bias_hbm, decay_hbm, skip_hbm,
                 gains_hbm, norm_hbm, label_hbm, dtw_ref,
                 patches_ref, inw_ref, outw_ref, head_hbm,
                 sum_ref, loss_ref,
                 w, wx, wdt, dts, pall, scales,
                 x_s, coef_s, rawt, steps_s, run_s, weight_p, grown_p, run_p, row_s, fresh_s,
                 prefix, fin, inc,
                 local, sq, sq_in, normed, arrived, ow, head, hid, logit, part, sum_a, got_a, got_b,
                 got_c, spread_s, lane_s, wide_s, cum_s, gain_s,
                 ops_ref, codes_ref, bias_ref, decay_ref, skip_ref, gains_ref, norm_ref, label_ref,
                 loc_sem, send_sem, recv_sem):
    MESH = pl.DeviceIdType.MESH
    g, c, f = lax.axis_index("groups"), lax.axis_index("ctx"), lax.axis_index("fsdp")
    count = lax.axis_size("ctx")
    xx, k = f // 2, f % 2
    f1 = f + 1 - 2 * k
    f2 = f + 2 - 4 * xx
    f3 = f2 + 1 - 2 * k
    core, across, corner, other = (g, c, f1), (g, c, f2), (g, c, f3), (1 - g, c, f)
    used = [0]

    def tile(j, chip):
        return pl.ds(pl.multiple_of((2 * j + chip) * LANES, LANES), LANES)

    def remote(src, dst, to):
        n = used[0]
        used[0] += 1
        return pltpu.make_async_remote_copy(
            src_ref=src, dst_ref=dst, send_sem=send_sem.at[n], recv_sem=recv_sem.at[n],
            device_id=to, device_id_type=MESH)

    local_copies = [
        pltpu.make_async_copy(inw_ref.at[:, tile(j, xx)], w.at[f, :, pl.ds(j * LANES, LANES)],
                              loc_sem.at[8 + j]) for j in range(4)]
    local_copies += [
        pltpu.make_async_copy(inw_ref.at[:, pl.ds(D, 512)], w.at[f, :, pl.ds(512, 512)],
                              loc_sem.at[12]),
        pltpu.make_async_copy(dtw_ref, dts.at[f], loc_sem.at[13])]
    load_own = pltpu.make_async_copy(patches_ref, pall.at[f], loc_sem.at[1])
    load_head = pltpu.make_async_copy(head_hbm, head, loc_sem.at[2])
    load_out = pltpu.make_async_copy(outw_ref, ow.at[:, f], loc_sem.at[3])
    barrier = pltpu.get_barrier_semaphore()
    for to in (core, across, corner, other):
        pl.semaphore_signal(barrier, inc=1, device_id=to, device_id_type=MESH)
    for j in range(1, count):
        pl.semaphore_signal(barrier, inc=1, device_id=(g, (c + j) % count, f), device_id_type=MESH)

    tables = [
        pltpu.make_async_copy(src, dst, loc_sem.at[16 + n])
        for n, (src, dst) in enumerate((
            (ops_hbm, ops_ref), (codes_hbm, codes_ref), (bias_hbm, bias_ref), (decay_hbm, decay_ref),
            (skip_hbm, skip_ref), (gains_hbm, gains_ref), (norm_hbm, norm_ref),
            (label_hbm, label_ref)))]
    for copy in tables + local_copies + [load_own, load_head, load_out]:
        copy.start()
    pl.semaphore_wait(barrier, 3 + count)

    zc = c % 2
    along = (g, c + 1 - 2 * zc, f)
    chunk = 64 // CHUNKS

    def span(gg, cc, q):
        return pl.ds(pl.multiple_of((2 * gg + cc) * 64 + q * chunk, chunk), chunk)

    first = []
    for q in range(CHUNKS):
        rows = span(g, zc, q)
        group = [remote(inw_ref.at[rows, tile(j, 1 - xx)], w.at[f, rows, pl.ds(j * LANES, LANES)],
                        across) for j in range(4)]
        group.append(remote(inw_ref.at[rows, pl.ds(D, 512)], w.at[f, rows, pl.ds(512, 512)], across))
        for copy in group:
            copy.start()
        first.append(group)
    beside = [remote(inw_ref.at[:, tile(j, xx)], w.at[f, :, pl.ds(j * LANES, LANES)], core)
              for j in range(4)]
    beside.append(remote(inw_ref.at[:, pl.ds(D, 512)], w.at[f, :, pl.ds(512, 512)], core))
    small = [remote(dtw_ref, dts.at[f], to) for to in (across, corner, core)]
    patch_core = remote(patches_ref, pall.at[f], core)
    for copy in small + beside:
        copy.start()
    patch_core.start()
    patch_across = []
    for b in range(4):
        rows = pl.ds(b * 64, 64)
        patch_across.append(remote(patches_ref.at[rows], pall.at[f, rows], across))

    for copy in tables:
        copy.wait()
    pick_row = lax.broadcasted_iota(jnp.int32, (2 * HEADS, LANES), 0)
    pick_col = lax.broadcasted_iota(jnp.int32, (2 * HEADS, LANES), 1)
    head_at = 16 * ((pick_col // 4) % 2) + 4 * (pick_col % 4) + pick_col // 8
    pick = ((pick_row == head_at) & (pick_col < 32)).astype(f32).astype(bf16)
    half_row = lax.broadcasted_iota(jnp.int32, (512, 256), 0)
    half_col = lax.broadcasted_iota(jnp.int32, (512, 256), 1)
    mine = (half_row == 128 * (half_col // 64) + 64 * k + half_col % 64).astype(f32).astype(bf16)
    row32 = lax.broadcasted_iota(jnp.int32, (32, 512), 0)
    col32 = lax.broadcasted_iota(jnp.int32, (32, 512), 1)
    spread_s[...] = ((row32 % 8 == col32 // 64) & (row32 < 24)).astype(f32).astype(bf16)
    row32 = lax.broadcasted_iota(jnp.int32, (32, 1024), 0)
    col32 = lax.broadcasted_iota(jnp.int32, (32, 1024), 1)
    row_l = lax.broadcasted_iota(jnp.int32, (LANES, 512), 0)
    col_l = lax.broadcasted_iota(jnp.int32, (LANES, 512), 1)
    lane_s[...] = (row_l == col_l // 64).astype(f32).astype(bf16)
    wide_s[...] = ((row32 % 8 == col32 // 128) & (row32 < 24)).astype(f32).astype(bf16)
    row = lax.broadcasted_iota(jnp.int32, (BLOCK, BLOCK), 0)
    col = lax.broadcasted_iota(jnp.int32, (BLOCK, BLOCK), 1)
    cum_s[:, :BLOCK] = (row <= col).astype(f32).astype(bf16)
    cum_s[:, BLOCK:] = (row >= col).astype(f32).astype(bf16)
    scales[0:1, :] = jnp.ones((1, D), f32)
    for j in range(2):
        codes = [jnp.full((1, D), codes_ref[j, i].astype(f32), f32) for i in range(WIDTH_AUG + 1)]
        whole = codes[0] + codes[1] + codes[2]
        shares = [codes[i] / whole for i in range(WIDTH_AUG)]
        keep = codes[WIDTH_AUG] / 9.0
        mixed_gain = jnp.zeros((1, D), f32)
        for n in range(NOPS):
            picked = jnp.zeros((1, D), f32)
            for i in range(WIDTH_AUG):
                picked += shares[i] * jnp.where(ops_ref[j, i] == n, 1.0, 0.0)
            mixed_gain += picked * gains_ref[n : n + 1, :]
        scales[j + 1 : j + 2, :] = keep + (1.0 - keep) * mixed_gain
    line = lax.broadcasted_iota(jnp.int32, (8, LANES), 0)
    bias = jnp.zeros((8, LANES), f32)
    rate = jnp.zeros((8, LANES), f32)
    for d in range(2):
        for j in range(4):
            bias = jnp.where(line == 4 * d + j, bias_ref[d, 4 * j + f], bias)
            rate = jnp.where(line == 4 * d + j, decay_ref[d, 4 * j + f], rate)
    rate = -jnp.exp(rate) * LOG2E
    lane_w = lax.broadcasted_iota(jnp.int32, (8, 256), 1)
    skip = jnp.zeros((8, 256), f32)
    for j in range(4):
        skip = jnp.where(lane_w // HEAD_DIM == j, skip_ref[0, 4 * j + f], skip)
    lane_n = lax.broadcasted_iota(jnp.int32, (8, LANES), 1)
    gain_parts = []
    for half in range(2):
        a = jnp.broadcast_to(norm_ref[pl.ds(4 * half + xx, 1), :], (8, LANES))
        b = jnp.broadcast_to(norm_ref[pl.ds(4 * half + 2 + xx, 1), :], (8, LANES))
        even = jnp.where(lane_n < 64, a, pltpu.roll(b, 64, 1))
        odd = jnp.where(lane_n < 64, pltpu.roll(a, 64, 1), b)
        gain_parts.append(jnp.where(k == 0, even, odd))
    gain_s[...] = jnp.concatenate(gain_parts, axis=1)

    relays, onward = [], []

    def to_core(rows):
        copy = remote(w.at[f2, rows], w.at[f2, rows], core)
        copy.start()
        relays.append(copy)

    def select(src):
        wx[src] = dot(w[src, :, :512], mine).astype(bf16)
        wdt[src] = dot(dts[src], pick, TT).astype(bf16)

    beyond, far = [], []
    for q in range(CHUNKS):
        for copy in first[q]:
            copy.wait_recv()
        rows = span(g, zc, q)
        onward.append(remote(w.at[f2, rows], w.at[f2, rows], other))
        beyond.append(remote(w.at[f2, rows], w.at[f2, rows], along))
        onward[q].start()
        beyond[q].start()
        if q == CHUNKS - 1:
            for copy in patch_across:
                copy.start()
        to_core(rows)
    for q in range(CHUNKS):
        onward[q].wait_recv()
        rows = span(1 - g, zc, q)
        far.append(remote(w.at[f2, rows], w.at[f2, rows], along))
        far[q].start()
        to_core(rows)
        beyond[q].wait_recv()
        to_core(span(g, 1 - zc, q))
    for copy in local_copies:
        copy.wait()
    for copy in small:
        copy.wait_recv()
    select(f)
    for copy in beside:
        copy.wait_recv()
    select(f1)
    for q in range(CHUNKS):
        far[q].wait_recv()
        to_core(span(1 - g, 1 - zc, q))
    select(f2)
    for copy in relays:
        copy.wait_recv()
    select(f3)
    load_own.wait()

    patch_relay = [
        remote(pall.at[f2, pl.ds(b * 64, 64)], pall.at[f2, pl.ds(b * 64, 64)], core)
        for b in range(4)
    ]
    out_across = remote(outw_ref, ow.at[:, f], across)
    out_core = remote(outw_ref, ow.at[:, f], core)
    out_relay = remote(ow.at[:, f2], ow.at[:, f2], core)

    def project(s, _):
        a = s // 4
        pair = (1 - a) * (s // 2) + a * (2 + s % 2)
        b = (1 - a) * (s % 2) + a * ((s - 4 * a) // 2)
        kb, xb = pair % 2, pair // 2
        src = 2 * (xx + xb - 2 * xx * xb) + (k + kb - 2 * k * kb)

        @pl.when(s == 2)
        def _():
            patch_core.wait_recv()

        for b_static in range(2):
            @pl.when(s == 4 + 2 * b_static)
            def _():
                for n in (2 * b_static, 2 * b_static + 1):
                    patch_across[n].wait_recv()
                    patch_relay[n].start()

            @pl.when(s == 5 + 2 * b_static)
            def _():
                for n in (2 * b_static, 2 * b_static + 1):
                    patch_relay[n].wait_recv()

        rows = pall[src, pl.ds(pl.multiple_of(b * 128, 128), 128), :].astype(f32)
        view = jnp.concatenate(
            [(scales[v : v + 1, :] * rows).astype(bf16) for v in range(VIEWS)], axis=0)
        i = 2 * src + b
        out = dot(view, wx[...].reshape(D, 256)).astype(bf16)
        coef = dot(view, w[:, :, 512:].reshape(D, 512)).astype(bf16)
        raw = dot(view, wdt[...].reshape(D, LANES))
        for v in range(VIEWS):
            at = slice(v * 128, (v + 1) * 128)
            x_s[v, i] = out[at]
            coef_s[v, i] = coef[at]
            rawt[8 * v + i] = raw[at].T[:32]
        return 0

    lax.fori_loop(0, 8, project, 0)
    out_across.start()
    out_core.start()

    def triple(values):
        high = values.astype(bf16).astype(f32)
        rest = values - high
        mid = rest.astype(bf16).astype(f32)
        return high, mid, rest - mid

    def stacked(values):
        return jnp.concatenate([*triple(values), jnp.zeros_like(values)], axis=1).astype(bf16)

    blocks = VIEWS * 8
    raw = rawt[:, pl.ds(pl.multiple_of(8 * f, 8), 8), :] + bias[None]
    steps_all = jnp.maximum(raw, 0.0) + jnp.log1p(jnp.exp(-jnp.abs(raw)))
    logs = jnp.concatenate(triple(steps_all * rate[None]), axis=0).reshape(3 * blocks * 8, BLOCK)
    cum = dot(logs.astype(bf16), cum_s[...]).reshape(3, blocks, 8, 2 * BLOCK)
    cum = cum[0] + cum[1] + cum[2]
    way = lax.broadcasted_iota(jnp.int32, (blocks, 8, BLOCK), 1) < 4
    run_all = jnp.where(way, cum[:, :, :BLOCK], cum[:, :, BLOCK:])
    last_all = jnp.where(way, jnp.broadcast_to(cum[:, :, BLOCK - 1 : BLOCK], way.shape),
                         jnp.broadcast_to(cum[:, :, BLOCK : BLOCK + 1], way.shape))
    steps_s[...] = steps_all
    run_s[...] = run_all
    weight_p[...] = stacked(jnp.exp2(last_all - run_all) * steps_all)
    grown_p[...] = stacked(jnp.exp2(run_all))
    run_p[...] = stacked(run_all)
    totals, before = [], [None] * blocks
    for v in range(VIEWS):
        lasts = [last_all[8 * v + i] for i in range(8)]
        ahead_sum, behind_sum = [jnp.zeros((8, LANES), f32)], [jnp.zeros((8, LANES), f32)]
        for i in range(8):
            ahead_sum.append(ahead_sum[-1] + lasts[i])
            behind_sum.append(behind_sum[-1] + lasts[7 - i])
        for i in range(8):
            before[8 * v + i] = jnp.where(line < 4, ahead_sum[i], behind_sum[7 - i])[None]
        totals.append(jnp.where(line < 4, ahead_sum[8], behind_sum[8])[None])
    pad = [jnp.zeros((8 - VIEWS, 8, LANES), f32)]
    decays = jnp.exp2(jnp.concatenate([last_all] + before + totals + pad, axis=0))
    count_rows = 2 * blocks + 8
    on_lane = (lax.broadcasted_iota(jnp.int32, decays.shape, 1)
               == lax.broadcasted_iota(jnp.int32, decays.shape, 2))
    flat = jnp.sum(jnp.where(on_lane, decays, 0.0), axis=1)
    flat = dot(jnp.concatenate(triple(flat), axis=0).astype(bf16), lane_s[...])
    row_s[...] = flat[:count_rows] + flat[count_rows : 2 * count_rows] + flat[2 * count_rows :]

    def states(v):
        fin[v, 0] = jnp.zeros((STATE, 256), f32)
        fin[v, 1] = jnp.zeros((STATE, 256), f32)

        def forward(i, _):
            n = 8 * v + i
            xf = x_s[v, i].astype(f32)
            weight = dot(weight_p[n], spread_s[...], TT)
            for d in range(2):
                high, low = halves(weight[:, 256 * d : 256 * (d + 1)] * xf)
                write = coef_s[v, i, :, 2 * STATE * d : 2 * STATE * d + STATE].T
                fresh = dot(jnp.concatenate([write, write], axis=1),
                            jnp.concatenate([high, low], axis=0))
                if d == 0:
                    state = fin[v, 0]
                    prefix[v, 0, i] = state
                    fin[v, 0] = row_s[pl.ds(n, 1), :256] * state + fresh
                else:
                    fresh_s[i] = fresh
            return 0

        lax.fori_loop(0, 8, forward, 0, unroll=UNROLL_S)

        def backward(m, _):
            i = 7 - m
            state = fin[v, 1]
            prefix[v, 1, i] = state
            fin[v, 1] = row_s[pl.ds(8 * v + i, 1), 256:] * state + fresh_s[i]
            return 0

        lax.fori_loop(0, 8, backward, 0, unroll=8)

    ahead = (g, (c + 1) % count, f)
    behind = (g, (c + count - 1) % count, f)
    depth = STATE // PIECES
    bands = [pl.ds(n * depth, depth) for n in range(PIECES)]
    chain = [[[remote(fin.at[v, d, band], inc.at[v, d, band], (ahead, behind)[d])
               for band in bands] for d in range(2)] for v in range(VIEWS)]

    def hop(v, n):
        for d in range(2):
            place = c if d == 0 else count - 1 - c

            @pl.when(place == n)
            def _():
                if n == 0:
                    inc[v, d] = jnp.zeros((STATE, 256), f32)
                decay = row_s[2 * blocks + v : 2 * blocks + v + 1, 256 * d : 256 * (d + 1)]
                for copy, at in zip(chain[v][d], bands):
                    if n > 0:
                        copy.wait_recv()
                    if 0 < n < count - 1:
                        fin[v, d, at] = fin[v, d, at] + inc[v, d, at] * decay
                    if n < count - 1:
                        copy.start()

    def inside(v, start):
        def body(i, _):
            x = x_s[v, i]
            n = 8 * v + i
            run, steps = run_s[n], steps_s[n]
            coef = coef_s[v, i]
            score_f = dot(coef[:, STATE : 2 * STATE], coef[:, :STATE], NT)
            score_r = dot(coef[:, 3 * STATE :], coef[:, 2 * STATE : 3 * STATE], NT)
            diagonal = jnp.sum(jnp.where(row == col, score_r, 0.0), axis=0, keepdims=True)
            extra = dot(stack3(steps * diagonal), spread_s[:, 256:], TT)
            wide = dot(run_p[n], wide_s[...], TT)
            keep = row >= col
            lane_b = lax.broadcasted_iota(jnp.int32, (BLOCK, LANES), 1)
            none = jnp.zeros((BLOCK, LANES), bf16)
            pieces = []
            for pair in range(2):
                highs, lows = [], []
                for h in (2 * pair, 2 * pair + 1):
                    r = 4 + h
                    gap = jnp.where(keep, wide[:, h * 128 : (h + 1) * 128] - run[h : h + 1],
                                    wide[:, r * 128 : (r + 1) * 128] - run[r : r + 1])
                    weight = jnp.where(keep, score_f * steps[h : h + 1], score_r * steps[r : r + 1])
                    high, low = halves(weight * jnp.exp2(gap))
                    highs.append(high)
                    lows.append(low)
                values = x[:, pair * LANES : (pair + 1) * LANES]
                left, right = jnp.where(lane_b < 64, values, none), jnp.where(lane_b < 64, none, values)
                pieces.append(dot(jnp.concatenate(highs + lows, axis=1),
                                  jnp.concatenate([left, right, left, right], axis=0)))
            local[v, i] = jnp.concatenate(pieces, axis=1) + (skip[0:1] + extra) * x.astype(f32)
            return 0

        lax.fori_loop(start, start + 4, body, 0, unroll=UNROLL_I)

    def carried(v):
        def body(i, _):
            n = 8 * v + i
            grown = dot(grown_p[n], spread_s[...], TT)
            decay = row_s[pl.ds(blocks + n, 1), :]
            mixed = local[v, i]
            for d in range(2):
                at = slice(256 * d, 256 * (d + 1))
                high, low = halves(prefix[v, d, i] + decay[:, at] * inc[v, d])
                read = coef_s[v, i, :, STATE * (1 + 2 * d) : STATE * (2 + 2 * d)]
                mixed += grown[:, at] * dot(jnp.concatenate([read, read], axis=1),
                                            jnp.concatenate([high, low], axis=0))
            local[v, i] = mixed
            square = mixed * mixed
            square = square[:, :LANES] + square[:, LANES:]
            sums = dot(jnp.ones((8, 3 * LANES), bf16), side3(square), NT)
            sq[v, pl.ds(i, 1), :] = sums[0:1]
            return 0

        lax.fori_loop(0, 8, body, 0, unroll=UNROLL_C)

    square_out = [[remote(sq.at[v], sq_in.at[p, v], to)
                   for p, to in enumerate((core, across, corner))] for v in range(VIEWS)]
    normed_out = [[remote(normed.at[v, fp], arrived.at[f, v], to)
                   for fp, to in ((f3, corner), (f2, across), (f1, core))] for v in range(VIEWS)]
    normed_own = [pltpu.make_async_copy(normed.at[v, f], arrived.at[f, v], loc_sem.at[4 + v])
                  for v in range(VIEWS)]

    def finish(v):
        for copy in square_out[v]:
            copy.wait_recv()
        total = (sq[v] + sq_in[0, v]) + (sq_in[1, v] + sq_in[2, v])
        parts = stack3(lax.rsqrt(total / D + 1e-05))
        row_i = lax.broadcasted_iota(jnp.int32, (32, 256), 0)

        def body(i, _):
            pick = ((row_i % 8 == i) & (row_i < 24)).astype(f32).astype(bf16)
            scaling = dot(parts, pick, TT)
            normed[v, i // 2, i % 2] = (local[v, i] * scaling * gain_s[0:1]).astype(bf16)
            return 0

        lax.fori_loop(0, 8, body, 0, unroll=2)
        normed_out[v][0].start()
        normed_out[v][2].start()
        normed_own[v].start()

    def read_out(v):
        carried(v)
        for copy in square_out[v]:
            copy.start()
        if v > 0:
            normed_out[v - 1][1].start()

    states(0)
    hop(0, 0)
    states(1)
    states(2)
    hop(1, 0)
    hop(0, 1)
    inside(0, 0)
    hop(2, 0)
    inside(0, 4)
    hop(0, 2)
    hop(1, 1)
    inside(1, 0)
    inside(1, 4)
    out_across.wait_recv()
    out_relay.start()
    hop(2, 1)
    hop(1, 2)
    hop(0, 3)
    read_out(0)
    inside(2, 0)
    finish(0)
    hop(2, 2)
    hop(1, 3)
    read_out(1)
    inside(2, 4)
    finish(1)
    hop(2, 3)
    read_out(2)
    finish(2)
    normed_out[2][1].start()

    load_head.wait()
    load_out.wait()
    out_core.wait_recv()
    out_relay.wait_recv()

    def hidden(v):
        for copy in normed_out[v]:
            copy.wait_recv()
        normed_own[v].wait()
        for b in range(2):
            full = jnp.concatenate([arrived[s, v, b] for s in range(4)], axis=1)
            total = dot(full, ow[...].reshape(D, D))
            view = (scales[v : v + 1, :] * pall[f, b * 128 : (b + 1) * 128, :].astype(f32)).astype(bf16)
            hid[v, b] = (view.astype(f32) + total).astype(bf16)

    for v in range(VIEWS):
        hidden(v)

    for b in range(2):
        logs = []
        for v in range(VIEWS):
            logits = dot(hid[v, b], head[...])
            shifted = logits - jnp.max(logits, axis=1, keepdims=True)
            logs.append(shifted - jnp.log(jnp.sum(jnp.exp(shifted), axis=1, keepdims=True)))
        top = jnp.maximum(jnp.maximum(logs[0], logs[1]), logs[2])
        mean = top + jnp.log(sum(jnp.exp(log - top) for log in logs)) - jnp.log(f32(VIEWS))
        onehot = (row == label_ref[b : b + 1, :]).astype(f32).T
        spread_sum = jnp.zeros((BLOCK, 1), f32)
        for v in range(VIEWS):
            prob = jnp.exp(logs[v])
            gap = logs[v] - mean
            inner = jnp.sum(prob * gap, axis=1, keepdims=True)
            spread_sum += inner
            grad = (mix_lambda / VIEWS) * prob * (gap - inner)
            if v == 0:
                grad += prob - onehot
            logit[v, b] = (factor * grad).astype(bf16)
        cross = -jnp.sum(onehot * logs[0], axis=1, keepdims=True)
        losses = cross + mix_lambda * (spread_sum / VIEWS)
        loss_ref[b : b + 1, :] = jnp.sum(jnp.where(row == col, losses, 0.0), axis=0, keepdims=True)

    grads = logit[...].reshape(VIEWS * 2 * BLOCK, CLASSES)
    def sum_terms(chip):
        for kk in range(2):
            s = 2 * chip + kk
            for half in range(2):
                lanes = slice(half * LANES, (half + 1) * LANES)
                term = dot(arrived[s, :, :, :, lanes].reshape(VIEWS * 2 * BLOCK, LANES), grads, TT)
                for e in range(2):
                    part[s, 2 * half + e, :, :CLASSES] = term[64 * e : 64 * (e + 1)]
        for m in range(4):
            lanes = pl.ds(pl.multiple_of((2 * m + chip) * LANES, LANES), LANES)
            term = dot(hid[:, :, :, lanes].reshape(VIEWS * 2 * BLOCK, LANES), grads, TT)
            for e in range(2):
                part[2 * chip + e, m, :, CLASSES:] = term[64 * e : 64 * (e + 1)]

    order = [(c + off) % count for off in (2, 3, 1, 0)]
    sum_core = [[remote(part.at[2 * xs + 1 - k, j], got_a.at[n, j], core) for j in order]
                for n, xs in enumerate((1 - xx, xx))]
    sum_terms(1 - xx)
    for copy in sum_core[0]:
        copy.start()
    sum_terms(xx)
    for copy in sum_core[1]:
        copy.start()
    sum_across = []
    for n, j in enumerate(order):
        sum_core[0][n].wait_recv()
        sum_a[0, j] = part[2 * (1 - xx) + k, j] + got_a[0, j]
        copy = remote(sum_a.at[0, j], got_b.at[j], across)
        copy.start()
        sum_across.append(copy)
    sum_ctx = []
    for n, j in enumerate(order):
        sum_core[1][n].wait_recv()
        own = part[2 * xx + k, j] + got_a[1, j]
        sum_across[n].wait_recv()
        sum_a[1, j] = own + got_b[j]
        if n < 3:
            copy = remote(sum_a.at[1, j], got_c.at[n], (g, j, f))
            copy.start()
            sum_ctx.append(copy)
    for copy in sum_ctx:
        copy.wait_recv()
    done = sum_a[1, c]
    for j in range(count - 1):
        done = done + got_c[j]
    sum_ref[...] = done

    sends = [copy for group in first for copy in group] + onward + beyond + far + relays + beside + small
    sends += [patch_core] + patch_across + patch_relay
    sends += [out_across, out_core, out_relay]
    sends += [copy for v in range(VIEWS) for copy in square_out[v] + normed_out[v]]
    sends += sum_core[0] + sum_core[1] + sum_across + sum_ctx
    for copy in sends:
        copy.wait_send()
    for v in range(VIEWS):
        @pl.when(c < count - 1)
        def _():
            for copy in chain[v][0]:
                copy.wait_send()

        @pl.when(c > 0)
        def _():
            for copy in chain[v][1]:
                copy.wait_send()


def close_kernel(sum_ref, head_ref, lost_ref, grad_ref, head_grad_ref, loss_ref):
    head_grad_ref[...] = sum_ref[:, CLASSES:]
    loss_ref[...] = lost_ref[...]
    out = dot(jnp.concatenate(thirds(sum_ref[:, :CLASSES]), axis=0), head_ref[...], NT)
    grad_ref[...] = out[0:64] + out[64:128] + out[128:192]


def fused(patches, labels, op_ids, mix_codes, aug_gains, in_weight, dt_weight, dt_bias,
          decay_log, skip_gain, norm_gain, out_weight, head_weight):
    rows = patches.shape[0]
    ctx_count, shards = lax.axis_size("ctx"), lax.axis_size("fsdp")
    factor = loss_scale / (rows * ctx_count * shards)
    vmem = pl.BlockSpec(memory_space=pltpu.VMEM)
    far = pl.BlockSpec(memory_space=pl.ANY)
    V = pltpu.VMEM
    sums, losses = pl.pallas_call(
        functools.partial(fused_kernel, factor),
        name="fused",
        out_shape=[
            jax.ShapeDtypeStruct((64, 256), f32),
            jax.ShapeDtypeStruct((2, LANES), f32),
        ],
        in_specs=[far] * 13,
        out_specs=[vmem] * 2,
        scratch_shapes=[
            V((4, 256, 1024), bf16), V((4, 256, 256), bf16), V((4, 256, LANES), bf16),
            V((4, 2 * HEADS, 256), bf16), V((4, 256, D), bf16), V((VIEWS, D), f32),
            V((VIEWS, 8, 128, 256), bf16), V((VIEWS, 8, 128, 512), bf16), V((24, 32, 128), f32),
            V((24, 8, 128), f32), V((24, 8, 128), f32), V((24, 32, 128), bf16), V((24, 32, 128), bf16),
            V((24, 32, 128), bf16), V((56, 512), f32), V((8, 128, 256), f32),
            V((VIEWS, 2, 8, 128, 256), f32), V((VIEWS, 2, 128, 256), f32), V((VIEWS, 2, 128, 256), f32),
            V((VIEWS, 8, 128, 256), f32), V((VIEWS, 8, 128), f32), V((PEERS, VIEWS, 8, 128), f32),
            V((VIEWS, 4, 2, 128, 256), bf16), V((4, VIEWS, 2, 128, 256), bf16),
            V((4, 4, 64, D), bf16), V((D, CLASSES), bf16), V((VIEWS, 2, 128, D), bf16),
            V((VIEWS, 2, 128, CLASSES), bf16), V((4, 4, 64, 256), f32), V((2, 4, 64, 256), f32),
            V((2, 4, 64, 256), f32), V((4, 64, 256), f32), V((3, 64, 256), f32),
            V((32, 512), bf16), V((LANES, 512), bf16), V((32, 1024), bf16), V((128, 256), bf16),
            V((8, 256), f32),
            pltpu.SMEM((2, WIDTH_AUG), jnp.int32), pltpu.SMEM((2, WIDTH_AUG + 1), jnp.int32),
            pltpu.SMEM((2, HEADS), f32), pltpu.SMEM((2, HEADS), f32), pltpu.SMEM((1, HEADS), f32),
            V((NOPS, D), f32), V((8, LANES), f32), V((2, LANES), jnp.int32),
            pltpu.SemaphoreType.DMA((24,)),
            pltpu.SemaphoreType.DMA((112,)), pltpu.SemaphoreType.DMA((112,)),
        ],
        compiler_params=pltpu.CompilerParams(
            collective_id=0, has_side_effects=True, vmem_limit_bytes=56 << 20),
        cost_estimate=pl.CostEstimate(flops=20 << 30, bytes_accessed=8 << 20, transcendentals=0),
    )(op_ids, mix_codes, dt_bias, decay_log, skip_gain[None, :],
      aug_gains, norm_gain.reshape(8, LANES), labels.reshape(2, LANES), dt_weight.T,
      patches, in_weight, out_weight.reshape(4, 64, D), head_weight)
    grad_out, grad_head, losses = pl.pallas_call(
        close_kernel,
        name="close",
        out_shape=[
            jax.ShapeDtypeStruct((64, D), f32),
            jax.ShapeDtypeStruct((64, CLASSES), f32),
            jax.ShapeDtypeStruct((2, LANES), f32),
        ],
    )(sums, head_weight, losses)
    return grad_out, grad_head, losses.reshape(rows)


def solution(mesh):
    sizes = dict(mesh.shape)
    small = sizes["groups"] == 2 and sizes["ctx"] == 4 and sizes["fsdp"] == 4
    return jax.shard_map(
        fused if small else on_device,
        mesh=mesh,
        in_specs=(
            P(("groups", "ctx", "fsdp"), None),
            P(("groups", "ctx", "fsdp")),
            P("groups", None),
            P("groups", None),
            P(),
            P("fsdp", None),
            P("fsdp", None),
            P(),
            P(),
            P(),
            P(),
            P("fsdp", None),
            P(),
        ),
        out_specs=(
            P(("groups", "ctx", "fsdp"), None),
            P(("groups", "ctx", "fsdp"), None),
            P(("groups", "ctx", "fsdp")),
        ),
        check_vma=False,
    )
```
